32 devices in a mesh: dp: 8 (over z, y), tensor: 4 (over x, core).
Axes of the slice: x: 2, y: 2, z: 4, core: 2. Of those that a mesh axis runs over, the one named last changes fastest.
Arguments:
- block_in: bfloat16 [16384, 768], P(('dp', 'tensor')), may hold values from -6 to 6
- enc_states: bfloat16 [65536, 768], P(('dp', 'tensor')), may hold values from -6 to 6
- dec_len: int32 [64], P('dp'), may hold values from 32 to 256
- enc_len: int32 [64], P('dp'), may hold values from 128 to 1024
- gain_self: bfloat16 [768], replicated, may hold values from 0.5 to 1.5
- self_query: bfloat16 [768, 768], P(None, 'tensor'), may hold values from -0.02734375 to 0.02734375
- self_key: bfloat16 [768, 768], P(None, 'tensor'), may hold values from -0.21875 to 0.21875
- self_value: bfloat16 [768, 768], P(None, 'tensor'), may hold values from -0.21875 to 0.21875
- self_out: bfloat16 [768, 768], P('tensor'), may hold values from -0.875 to 0.875
- rel_table: bfloat16 [32, 12], P(None, 'tensor'), may hold values from -4 to 4
- gain_cross: bfloat16 [768], replicated, may hold values from 0.5 to 1.5
- cross_query: bfloat16 [768, 768], P(None, 'tensor'), may hold values from -0.02734375 to 0.02734375
- cross_key: bfloat16 [768, 768], P(None, 'tensor'), may hold values from -0.21875 to 0.21875
- cross_value: bfloat16 [768, 768], P(None, 'tensor'), may hold values from -0.21875 to 0.21875
- cross_out: bfloat16 [768, 768], P('tensor'), may hold values from -0.875 to 0.875
- gain_ff: bfloat16 [768], replicated, may hold values from 0.5 to 1.5
- ff_in: bfloat16 [768, 3072], P(None, 'tensor'), may hold values from -0.21875 to 0.21875
- ff_out: bfloat16 [3072, 768], P('tensor'), may hold values from -0.109375 to 0.109375
- out_grad: bfloat16 [16384, 768], P(('dp', 'tensor')), may hold values from -6 to 6
Outputs:
- block_out: bfloat16 [16384, 768], P(('dp', 'tensor'))
- grad_in: float32 [16384, 768], P(('dp', 'tensor'))
- grad_enc: float32 [65536, 768], P(('dp', 'tensor'))
- grad_gain_self: float32 [768], replicated
- grad_self_query: float32 [768, 768], P(None, 'tensor')
- grad_self_key: float32 [768, 768], P(None, 'tensor')
- grad_self_value: float32 [768, 768], P(None, 'tensor')
- grad_self_out: float32 [768, 768], P('tensor')
- grad_rel_table: float32 [32, 12], P(None, 'tensor')
- grad_gain_cross: float32 [768], replicated
- grad_cross_query: float32 [768, 768], P(None, 'tensor')
- grad_cross_key: float32 [768, 768], P(None, 'tensor')
- grad_cross_value: float32 [768, 768], P(None, 'tensor')
- grad_cross_out: float32 [768, 768], P('tensor')
- grad_gain_ff: float32 [768], replicated
- grad_ff_in: float32 [768, 3072], P(None, 'tensor')
- grad_ff_out: float32 [3072, 768], P('tensor')
The draws below stay inside these ranges and needn't reach their ends.
All inputs are finite; a program needn't handle non-finite values.
Results may differ from the reference program's by a relative error of at most 0.025.
Values may be sent and summed in bfloat16 or wider, within the bound.
No kernel may reach another device: no remote copies, remote signals or barrier semaphores. Data moves between devices by JAX's collectives and lax.ppermute only.
A program may use at most 256 MiB of HBM per device.

```python
import math
import jax
import jax.numpy as jnp
import numpy as np
from jax import lax

D = 768
H = 12
DH = 64
FF = 3072
BUCKETS = 32
MAX_DIST = 128
LEN = 256
ENC = 1024
EXAMPLES = 64
TOKENS = 16384
ENC_TOKENS = 65536


def set_ends(result, stream_key, low, top_value):
    dims = result.shape
    spot = [jax.random.randint(jax.random.fold_in(stream_key, axis), (), 0, dims[axis]) for axis in range(len(dims))]
    result = result.at[tuple(spot)].set(low)
    longest = dims.index(max(dims))
    spot[longest] = (spot[longest] + 1) % dims[longest]
    return result.at[tuple(spot)].set(top_value)


def levels(key, extent, shards, least, top_value):
    loudness, own = 1.0, jax.random.fold_in(key, 6)
    for position, parts in shards:
        steps = jnp.exp(jax.random.uniform(jax.random.fold_in(own, position), (parts,), jnp.float32, least / len(shards), top_value / len(shards)))
        loudness = loudness * jnp.repeat(steps, extent[position] // parts).reshape([-1 if axis == position else 1 for axis in range(len(extent))])
    return loudness


def bell_draw(key, extent, scale, limit, split=(), held_as=jnp.bfloat16):
    result = jax.random.normal(key, extent, jnp.float32) * scale
    if len(split) > 0:
        result = levels(key, extent, split, -0.22, 0.18) * result
    return jnp.clip(result, min=-limit, max=limit).astype(held_as)


def setup_inputs(seed: int = 0) -> dict:
    key_of = jax.random.split(jax.random.key(seed), 20)
    return {
        "block_in": bell_draw(key_of[0], (TOKENS, D), 1.0, 6.0, ((0, 32),)),
        "enc_states": bell_draw(key_of[1], (ENC_TOKENS, D), 1.0, 6.0, ((0, 32),)),
        "dec_len": set_ends(jax.random.randint(key_of[2], (EXAMPLES,), LEN // 8, LEN + 1), jax.random.fold_in(key_of[2], 1), LEN // 8, LEN).astype(jnp.int32),
        "enc_len": set_ends(jax.random.randint(key_of[3], (EXAMPLES,), ENC // 8, ENC + 1), jax.random.fold_in(key_of[3], 1), ENC // 8, ENC).astype(jnp.int32),
        "gain_self": jnp.clip(1.0 + 0.1 * jax.random.normal(key_of[4], (D,), jnp.float32), 0.5, 1.5).astype(jnp.bfloat16),
        "self_query": bell_draw(key_of[5], (D, H * DH), (D * DH) ** -0.5, 0.02734375, ((1, 4),)),
        "self_key": bell_draw(key_of[6], (D, H * DH), D ** -0.5, 0.21875, ((1, 4),)),
        "self_value": bell_draw(key_of[7], (D, H * DH), D ** -0.5, 0.21875, ((1, 4),)),
        "self_out": bell_draw(key_of[8], (H * DH, D), (H * DH // 16) ** -0.5, 0.875, ((0, 4),)),
        "rel_table": bell_draw(key_of[9], (BUCKETS, H), 1.0, 4.0, ((1, 4),)),
        "gain_cross": jnp.clip(1.0 + 0.1 * jax.random.normal(key_of[10], (D,), jnp.float32), 0.5, 1.5).astype(jnp.bfloat16),
        "cross_query": bell_draw(key_of[11], (D, H * DH), (D * DH) ** -0.5, 0.02734375, ((1, 4),)),
        "cross_key": bell_draw(key_of[12], (D, H * DH), D ** -0.5, 0.21875, ((1, 4),)),
        "cross_value": bell_draw(key_of[13], (D, H * DH), D ** -0.5, 0.21875, ((1, 4),)),
        "cross_out": bell_draw(key_of[14], (H * DH, D), (H * DH // 16) ** -0.5, 0.875, ((0, 4),)),
        "gain_ff": jnp.clip(1.0 + 0.1 * jax.random.normal(key_of[15], (D,), jnp.float32), 0.5, 1.5).astype(jnp.bfloat16),
        "ff_in": bell_draw(key_of[16], (D, FF), D ** -0.5, 0.21875, ((1, 4),)),
        "ff_out": bell_draw(key_of[17], (FF, D), FF ** -0.5, 0.109375, ((0, 4),)),
        "out_grad": bell_draw(key_of[18], (TOKENS, D), 1.0, 6.0, ((0, 32),)),
    }


@jax.custom_vjp
def low(v):
    return lax.optimization_barrier(v.astype(jnp.bfloat16)).astype(jnp.float32)

@jax.custom_vjp
def low_back(v):
    return v

def low_keep(v):
    return (low(v), None)

def low_pass(kept, grad):
    return (grad,)

def back_keep(v):
    return (v, None)

def back_low(kept, grad):
    return (low(grad),)
low.defvjp(low_keep, low_pass)
low_back.defvjp(back_keep, back_low)
norm_eps = 1e-06
masked_score = -1000000000.0

def bucket_limits():
    half_count = BUCKETS // 2
    growth_ratio = MAX_DIST / half_count
    return np.array([int(math.ceil(half_count * growth_ratio ** (level_index / half_count))) for level_index in range(1, half_count)], dtype=np.int32)

def bucket_index(length):
    places = jnp.arange(length, dtype=jnp.int32)
    distance = jnp.maximum(places[:, None] - places[None, :], 0)
    limits = jnp.asarray(bucket_limits())
    above_count = lax.optimization_barrier(jnp.sum((distance[:, :, None] >= limits[None, None, :]).astype(jnp.int32), axis=2))
    half_count = BUCKETS // 2
    return jnp.where(distance < half_count, distance, half_count + above_count).astype(jnp.int32)

def rounded_both(values):
    return low(low_back(values))

def matmul(former, latter):
    return jnp.dot(former, latter, preferred_element_type=jnp.float32, precision=lax.Precision.HIGHEST)

def rms_norm(values, scales):
    return values * lax.rsqrt(lax.optimization_barrier(jnp.mean(values * values, axis=-1, keepdims=True)) + norm_eps) * scales

def attend(query_rows, key_rows, value_rows, extra_bias, allowed):
    scores = low_back(jnp.einsum('hqd,hkd->hqk', query_rows, key_rows, precision=lax.Precision.HIGHEST) + extra_bias)
    scores = jnp.where(allowed, scores, masked_score)
    top_score = lax.optimization_barrier(jnp.max(scores, axis=-1, keepdims=True))
    weights = jnp.exp(scores - top_score)
    softmax_out = weights / lax.optimization_barrier(jnp.sum(weights, axis=-1, keepdims=True))
    return rounded_both(jnp.einsum('hqk,hkd->hqd', low(softmax_out), value_rows, precision=lax.Precision.HIGHEST))

def split_heads(values, length):
    return values.reshape(EXAMPLES, length, H, DH).transpose(0, 2, 1, 3)

def join_heads(values):
    return values.transpose(0, 2, 1, 3).reshape(EXAMPLES * LEN, H * DH)

def self_example(rel_bias, example_item):
    query_rows, key_rows, value_rows, length = example_item
    places = jnp.arange(LEN, dtype=jnp.int32)
    allowed = (places[None, :] <= places[:, None]) & (places[None, :] < length)
    return attend(query_rows, key_rows, value_rows, rel_bias, allowed[None])

def cross_example(example_item):
    query_rows, key_rows, value_rows, length = example_item
    places = jnp.arange(ENC, dtype=jnp.int32)
    allowed = jnp.broadcast_to(places[None, None, :] < length, (1, LEN, ENC))
    return attend(query_rows, key_rows, value_rows, 0.0, allowed)

def forward(block_rows, enc_rows, params, dec_len, enc_len):
    scale_self, self_query, self_key, self_value, self_out, rel_table, scale_cross, cross_query, cross_key, cross_value, cross_out, scale_ff, ff_in, ff_out = params
    normed = low(rms_norm(block_rows, scale_self))
    query_rows = split_heads(rounded_both(matmul(normed, self_query)), LEN)
    key_rows = split_heads(rounded_both(matmul(normed, self_key)), LEN)
    value_rows = split_heads(rounded_both(matmul(normed, self_value)), LEN)
    rel_bias = jnp.transpose(rel_table[bucket_index(LEN)], (2, 0, 1))
    self_step = jax.checkpoint(self_example)

    def self_mapped(example_item):
        return self_step(rel_bias, example_item)
    mixed_rows = join_heads(lax.map(self_mapped, (query_rows, key_rows, value_rows, dec_len)))
    after_self = block_rows + low_back(matmul(mixed_rows, self_out))
    normed = low(rms_norm(after_self, scale_cross))
    query_rows = split_heads(rounded_both(matmul(normed, cross_query)), LEN)
    key_rows = split_heads(rounded_both(matmul(enc_rows, cross_key)), ENC)
    value_rows = split_heads(rounded_both(matmul(enc_rows, cross_value)), ENC)
    mixed_rows = join_heads(lax.map(jax.checkpoint(cross_example), (query_rows, key_rows, value_rows, enc_len)))
    after_cross = after_self + low_back(matmul(mixed_rows, cross_out))
    normed = low(rms_norm(after_cross, scale_ff))
    pre_act = low_back(matmul(normed, ff_in))
    hidden = low(jax.nn.gelu(pre_act, approximate=True))
    return after_cross + low_back(matmul(hidden, ff_out))

def reference(block_in, enc_states, dec_len, enc_len, gain_self, self_query, self_key, self_value, self_out, rel_table, gain_cross, cross_query, cross_key, cross_value, cross_out, gain_ff, ff_in, ff_out, out_grad):
    params = tuple((weight.astype(jnp.float32) for weight in (gain_self, self_query, self_key, self_value, self_out, rel_table, gain_cross, cross_query, cross_key, cross_value, cross_out, gain_ff, ff_in, ff_out)))

    def wrapped(block_rows, enc_rows, param_list):
        return forward(block_rows, enc_rows, param_list, dec_len, enc_len)
    block_out, pullback = jax.vjp(wrapped, block_in.astype(jnp.float32), enc_states.astype(jnp.float32), params)
    grad_in, grad_enc, gradients = pullback(out_grad.astype(jnp.float32))
    return (block_out.astype(jnp.bfloat16), grad_in, grad_enc, gradients[0], gradients[1], gradients[2], gradients[3], gradients[4], gradients[5], gradients[6], gradients[7], gradients[8], gradients[9], gradients[10], gradients[11], gradients[12], gradients[13])
```

```python
import math

import jax
import jax.numpy as jnp
import numpy as np
from jax import lax
from jax.experimental import pallas as pl
from jax.experimental.pallas import tpu as pltpu
from jax.sharding import PartitionSpec as P

BUCKETS = 32
MAX_DIST = 128
LEN = 256
ENC = 1024
DH = 64

norm_eps = 1e-06
masked_score = -1000000000.0
bf16 = jnp.bfloat16
f32 = jnp.float32
VMEM_CAP = 60 * 1024 * 1024


def bucket_of_distance():
    half_count = BUCKETS // 2
    growth_ratio = MAX_DIST / half_count
    limits = np.array(
        [int(math.ceil(half_count * growth_ratio ** (m / half_count))) for m in range(1, half_count)],
        dtype=np.int32,
    )
    distance = np.arange(LEN, dtype=np.int32)
    above = np.sum(distance[:, None] >= limits[None, :], axis=1)
    return np.where(distance < half_count, distance, half_count + above).astype(np.int32)


def nn(a, b):
    return lax.dot_general(a, b, (((1,), (0,)), ((), ())), preferred_element_type=f32)


def nt(a, b):
    return lax.dot_general(a, b, (((1,), (1,)), ((), ())), preferred_element_type=f32)


def tn(a, b):
    return lax.dot_general(a, b, (((0,), (0,)), ((), ())), preferred_element_type=f32)


def inv_rms(v):
    return lax.rsqrt(jnp.mean(v * v, axis=-1, keepdims=True) + norm_eps)


def normed(v, gain):
    return (v * inv_rms(v) * gain).astype(bf16)


def norm_back(v, gain, e):
    s = inv_rms(v)
    ge = gain * e
    dot = jnp.mean(ge * v, axis=-1, keepdims=True)
    grad_v = s * ge - v * (s * s * s * dot)
    grad_gain = jnp.sum(e * v * s, axis=0, keepdims=True)
    return grad_v, grad_gain


def lane_half(shape, h):
    lane = lax.broadcasted_iota(jnp.int32, shape, 1)
    return (lane < DH) if h == 0 else (lane >= DH)


def call(kernel, out_shape, args, *, grid=(), in_specs=None, out_specs=None, scratch=(), flops=0, nbytes=0, trans=0, name=None):
    kw = {}
    if in_specs is not None:
        kw["in_specs"] = in_specs
    if out_specs is not None:
        kw["out_specs"] = out_specs
    return pl.pallas_call(
        kernel,
        out_shape=out_shape,
        grid=grid,
        scratch_shapes=scratch,
        compiler_params=pltpu.CompilerParams(vmem_limit_bytes=VMEM_CAP),
        cost_estimate=pl.CostEstimate(flops=int(flops), bytes_accessed=int(nbytes), transcendentals=int(trans)),
        name=name,
        **kw,
    )(*args)


def whole(shape):
    return pl.BlockSpec(shape, lambda *_: (0,) * len(shape))


SMEM = pl.BlockSpec(memory_space=pltpu.SMEM)


def pack_kernel(y_ref, q_ref, k_ref, v_ref, o_ref, own_ref, half_ref):
    w = o_ref.shape[0]
    own_ref[0:w] = q_ref[...].T
    own_ref[w : 2 * w] = k_ref[...].T
    own_ref[2 * w : 3 * w] = v_ref[...].T
    own_ref[3 * w : 4 * w] = o_ref[...]
    y = y_ref[0]

    @pl.when(y == 0)
    def _():
        half_ref[...] = own_ref[0 : 2 * w]

    @pl.when(y != 0)
    def _():
        half_ref[...] = own_ref[2 * w : 4 * w]


def pack(y, q, k, v, o):
    w, d = o.shape
    return call(
        pack_kernel,
        (jax.ShapeDtypeStruct((4 * w, d), bf16), jax.ShapeDtypeStruct((2 * w, d), bf16)),
        (y, q, k, v, o),
        in_specs=[SMEM] + [whole(t.shape) for t in (q, k, v, o)],
        out_specs=(whole((4 * w, d)), whole((2 * w, d))),
        nbytes=4 * 4 * w * d,
        name="pack",
    )


def self_fwd_kernel(last, len_ref, x_ref, g_ref, g2_ref, wa_ref, wb_ref, bias_ref, *rest):
    if last:
        xin_ref, q_ref, k_ref, vt_ref, e_ref, r_ref, at_ref, x1_ref, n1_ref, n2_ref, bs_ref = rest
    else:
        q_ref, k_ref, vt_ref, e_ref, r_ref, at_ref, x1_ref, bs_ref = rest
    w = wa_ref.shape[0] // 4
    nh = 2 * w // DH
    nb = x_ref.shape[0] // LEN
    x = x_ref[...].astype(f32)
    n1 = normed(x, g_ref[...].astype(f32))
    if last:
        n1_ref[...] = n1

    def rows(i):
        return jnp.concatenate([wa_ref[i * w : (i + 1) * w], wb_ref[i * w : (i + 1) * w]], axis=0)

    q_ref[...] = nt(n1, rows(0)).astype(bf16)
    k_ref[...] = nt(n1, rows(1)).astype(bf16)
    vt_ref[...] = nt(rows(2), n1).astype(bf16)
    key = lax.broadcasted_iota(jnp.int32, (LEN, LEN), 0)
    query = lax.broadcasted_iota(jnp.int32, (LEN, LEN), 1)
    for p in range(nh // 2):
        lanes = slice(p * 2 * DH, (p + 1) * 2 * DH)
        for h in range(2):
            row = jnp.broadcast_to(bias_ref[2 * p + h : 2 * p + h + 1, :], (LEN, LEN))
            bs_ref[h] = pltpu.roll(row, 0, 1, stride=1, stride_axis=0)
        for b in range(nb):
            tok = slice(b * LEN, (b + 1) * LEN)
            allowed = (key <= query) & (key < len_ref[b])
            kp = k_ref[tok, lanes]
            qp = q_ref[tok, lanes]
            outs = []
            for h in range(2):
                head = 2 * p + h
                qh = jnp.where(lane_half(qp.shape, h), qp, jnp.zeros_like(qp))
                s = nt(kp, qh) + bs_ref[h]
                s = jnp.where(allowed, s, masked_score)
                top = jnp.max(s, axis=0, keepdims=True)
                e = jnp.exp(s - top)
                r = 1.0 / jnp.sum(e, axis=0, keepdims=True)
                eb = e.astype(bf16)
                e_ref[b, head] = eb
                r_ref[b, head : head + 1, :] = r
                outs.append(nn(vt_ref[head * DH : (head + 1) * DH, tok], eb) * r)
            at_ref[lanes, tok] = jnp.concatenate(outs, axis=0).astype(bf16)
    mixed = tn(at_ref[...], rows(3))
    if last:
        x1 = xin_ref[...] + mixed
        n2_ref[...] = normed(x1, g2_ref[...].astype(f32))
    else:
        x1 = x + mixed
    x1_ref[...] = x1


def self_fwd(last, lens, x, g, g2, wa, wb, bias, xin=None):
    t, d = x.shape
    w = wa.shape[0] // 4
    c = 2 * w
    nh = c // DH
    nb = t // LEN
    outs = [
        jax.ShapeDtypeStruct((t, c), bf16),
        jax.ShapeDtypeStruct((t, c), bf16),
        jax.ShapeDtypeStruct((c, t), bf16),
        jax.ShapeDtypeStruct((nb, nh, LEN, LEN), bf16),
        jax.ShapeDtypeStruct((nb, nh, LEN), f32),
        jax.ShapeDtypeStruct((c, t), bf16),
        jax.ShapeDtypeStruct((t, d), f32),
    ]
    args = [lens, x, g, g2, wa, wb, bias]
    if last:
        args.append(xin)
        outs += [jax.ShapeDtypeStruct((t, d), bf16)] * 2
    flops = 2 * t * d * c * 4 + 2 * t * LEN * nh * 128 * 2
    return call(
        lambda *r: self_fwd_kernel(last, *r),
        tuple(outs),
        args,
        in_specs=[SMEM] + [whole(a.shape) for a in args[1:]],
        out_specs=tuple(whole(o.shape) for o in outs),
        scratch=[pltpu.VMEM((2, LEN, LEN), f32)],
        flops=flops * 3,
        nbytes=12 * 1024 * 1024,
        trans=t * LEN * nh,
        name="self_fwd",
    )


def enc_kv_kernel(enc_ref, wa_ref, wb_ref, k_ref, kt_ref, v_ref, vt_ref):
    w = wa_ref.shape[0] // 4
    enc = enc_ref[...]

    def rows(i):
        return jnp.concatenate([wa_ref[i * w : (i + 1) * w], wb_ref[i * w : (i + 1) * w]], axis=0)

    wk = rows(1)
    wv = rows(2)
    k = nt(enc, wk).astype(bf16)
    k_ref[...] = k
    kt_ref[...] = k.T
    vt = nt(wv, enc).astype(bf16)
    vt_ref[...] = vt
    v_ref[...] = vt.T


def enc_kv(enc, wa, wb):
    t, d = enc.shape
    c = wa.shape[0] // 2
    rows = 512
    return call(
        enc_kv_kernel,
        (
            jax.ShapeDtypeStruct((t, c), bf16),
            jax.ShapeDtypeStruct((c, t), bf16),
            jax.ShapeDtypeStruct((t, c), bf16),
            jax.ShapeDtypeStruct((c, t), bf16),
        ),
        (enc, wa, wb),
        grid=(t // rows,),
        in_specs=[pl.BlockSpec((rows, d), lambda i: (i, 0)), whole(wa.shape), whole(wb.shape)],
        out_specs=(
            pl.BlockSpec((rows, c), lambda i: (i, 0)),
            pl.BlockSpec((c, rows), lambda i: (0, i)),
            pl.BlockSpec((rows, c), lambda i: (i, 0)),
            pl.BlockSpec((c, rows), lambda i: (0, i)),
        ),
        flops=2 * t * d * c * 2 * 2,
        nbytes=t * d * 2 + 4 * t * c * 2,
        name="enc_kv",
    )


def cross_fwd_kernel(last, pairs, len_ref, n2_ref, g_ref, wa_ref, wb_ref, k_ref, vt_ref, xin_ref, *rest):
    if last:
        q_ref, e_ref, r_ref, at_ref, x2_ref, n3_ref = rest
    else:
        q_ref, e_ref, r_ref, at_ref, x2_ref = rest
    w = wa_ref.shape[0] // 4
    step = pl.program_id(0)
    b = step // pairs
    p = lax.rem(step, pairs)

    def rows(i):
        return jnp.concatenate([wa_ref[i * w : (i + 1) * w], wb_ref[i * w : (i + 1) * w]], axis=0)

    @pl.when(step == 0)
    def _():
        q_ref[...] = nt(n2_ref[...], rows(0)).astype(bf16)

    tok = pl.ds(pl.multiple_of(b * LEN, LEN), LEN)
    lanes = pl.ds(pl.multiple_of(p * 2 * DH, 2 * DH), 2 * DH)
    qp = q_ref[tok, lanes]
    key = lax.broadcasted_iota(jnp.int32, (ENC, LEN), 0)
    allowed = key < len_ref[b]
    outs = []
    for h in range(2):
        qh = jnp.where(lane_half(qp.shape, h), qp, jnp.zeros_like(qp))
        s = nt(k_ref[...], qh)
        s = jnp.where(allowed, s, masked_score)
        top = jnp.max(s, axis=0, keepdims=True)
        e = jnp.exp(s - top)
        r = 1.0 / jnp.sum(e, axis=0, keepdims=True)
        eb = e.astype(bf16)
        e_ref[0, h] = eb
        r_ref[0, h : h + 1, :] = r
        outs.append(nn(vt_ref[h * DH : (h + 1) * DH, :], eb) * r)
    at_ref[lanes, tok] = jnp.concatenate(outs, axis=0).astype(bf16)

    @pl.when(step == pl.num_programs(0) - 1)
    def _():
        x2 = xin_ref[...] + tn(at_ref[...], rows(3))
        x2_ref[...] = x2
        if last:
            n3_ref[...] = normed(x2, g_ref[...].astype(f32))


def cross_fwd(last, lens, n2, g, wa, wb, k, vt, xin):
    t, d = n2.shape
    w = wa.shape[0] // 4
    c = 2 * w
    nb = t // LEN
    pairs = c // (2 * DH)
    outs = [
        jax.ShapeDtypeStruct((t, c), bf16),
        jax.ShapeDtypeStruct((nb * pairs, 2, ENC, LEN), bf16),
        jax.ShapeDtypeStruct((nb * pairs, 2, LEN), f32),
        jax.ShapeDtypeStruct((c, t), bf16),
        jax.ShapeDtypeStruct((t, d), f32),
    ]
    specs = [
        whole((t, c)),
        pl.BlockSpec((1, 2, ENC, LEN), lambda i: (i, 0, 0, 0)),
        pl.BlockSpec((1, 2, LEN), lambda i: (i, 0, 0)),
        whole((c, t)),
        whole((t, d)),
    ]
    if last:
        outs.append(jax.ShapeDtypeStruct((t, d), bf16))
        specs.append(whole((t, d)))
    return call(
        lambda *r: cross_fwd_kernel(last, pairs, *r),
        tuple(outs),
        (lens, n2, g, wa, wb, k, vt, xin),
        grid=(nb * pairs,),
        in_specs=[
            SMEM,
            whole(n2.shape),
            whole(g.shape),
            whole(wa.shape),
            whole(wb.shape),
            pl.BlockSpec((ENC, 2 * DH), lambda i: (i // pairs, i % pairs)),
            pl.BlockSpec((2 * DH, ENC), lambda i: (i % pairs, i // pairs)),
            whole(xin.shape),
        ],
        out_specs=tuple(specs),
        flops=3 * (2 * t * d * c * 2 + 2 * t * ENC * c * 2 * 2),
        nbytes=14 * 1024 * 1024,
        trans=t * ENC * (c // DH),
        name="cross_fwd",
    )


ROOT = math.sqrt(2.0 / math.pi)
CUBE = 0.044715


def ff_kernel(last, n3_ref, gf_ref, wia_ref, woa_ref, wib_ref, wob_ref, *rest):
    if last:
        yin_ref, gin_ref, x2_ref, g_ref = rest[:4]
        gwia, gwoa, gwib, gwob, out_ref, gx2_ref, go2_ref, gg_ref, y_ref, gn_ref, n3t_ref = rest[4:]
    else:
        gwia, gwoa, gwib, gwob, y_ref, gn_ref, n3t_ref = rest
    step = pl.program_id(0)

    @pl.when(step == 0)
    def _():
        n3t_ref[...] = n3_ref[...].T
        if last:
            y_ref[...] = yin_ref[...]
            gn_ref[...] = gin_ref[...]
        else:
            y_ref[...] = jnp.zeros_like(y_ref)
            gn_ref[...] = jnp.zeros_like(gn_ref)

    n3 = n3_ref[...]
    gf = gf_ref[...]
    for wi_ref, wo_ref, gwi, gwo in ((wia_ref, woa_ref, gwia, gwoa), (wib_ref, wob_ref, gwib, gwob)):
        u = nn(n3, wi_ref[...])
        dh = nt(gf, wo_ref[...])
        u2 = u * u
        th = jnp.tanh(ROOT * u * (1.0 + CUBE * u2))
        half = 0.5 * (1.0 + th)
        r = (u * half).astype(bf16)
        slope = half + 0.5 * u * (1.0 - th * th) * (ROOT * (1.0 + (3.0 * CUBE) * u2))
        gu = (dh * slope).astype(bf16)
        y_ref[...] += nn(r, wo_ref[...])
        gn_ref[...] += nt(gu, wi_ref[...])
        gwo[...] = tn(r, gf).astype(bf16)
        gwi[...] = nn(n3t_ref[...], gu).astype(bf16)

    if last:

        @pl.when(step == pl.num_programs(0) - 1)
        def _():
            x2 = x2_ref[...]
            out_ref[...] = (x2 + y_ref[...]).astype(bf16)
            gx, gg = norm_back(x2, g_ref[...].astype(f32), gn_ref[...])
            gx2 = gf.astype(f32) + gx
            gx2_ref[...] = gx2
            go2_ref[...] = gx2.astype(bf16)
            gg_ref[...] = gg


def ff(last, n3, gf, wia, woa, wib, wob, yin=None, gin=None, x2=None, g=None):
    t, d = n3.shape
    hid = wia.shape[1]
    blk = 256
    args = [n3, gf, wia, woa, wib, wob]
    col = pl.BlockSpec((d, blk), lambda i: (0, i))
    row = pl.BlockSpec((blk, d), lambda i: (i, 0))
    in_specs = [whole((t, d)), whole((t, d)), col, row, col, row]
    outs = [jax.ShapeDtypeStruct((d, hid), bf16), jax.ShapeDtypeStruct((hid, d), bf16)] * 2
    specs = [col, row, col, row]
    acc = jax.ShapeDtypeStruct((t, d), f32)
    scratch = [pltpu.VMEM((d, t), bf16)]
    if last:
        args += [yin, gin, x2, g]
        in_specs += [whole((t, d))] * 3 + [whole(g.shape)]
        outs += [jax.ShapeDtypeStruct((t, d), bf16), acc, jax.ShapeDtypeStruct((t, d), bf16), jax.ShapeDtypeStruct((1, d), f32)]
        specs += [whole((t, d))] * 3 + [whole((1, d))]
        scratch = [pltpu.VMEM((t, d), f32)] * 2 + scratch
    else:
        outs += [acc, acc]
        specs += [whole((t, d))] * 2
    return call(
        lambda *r: ff_kernel(last, *r),
        tuple(outs),
        args,
        grid=(hid // blk,),
        in_specs=in_specs,
        out_specs=tuple(specs),
        scratch=scratch,
        flops=2 * 6 * 2 * t * d * hid * 2,
        nbytes=12 * 1024 * 1024,
        trans=2 * t * hid,
        name="ff",
    )


def head_pair_back(k_t, v, q, ga, ga_t, a_t, es, rs, extra=None):
    gv = None
    gk = None
    gq_t = []
    for h in range(2):
        part = slice(h * DH, (h + 1) * DH)
        r = rs[h]
        gah = ga_t[part].astype(f32) * r
        delta = jnp.sum(gah * a_t[part].astype(f32), axis=0, keepdims=True)
        gah = gah.astype(bf16)
        zero = jnp.zeros_like(gah)
        rhs = jnp.concatenate([gah, zero] if h == 0 else [zero, gah], axis=0)
        gp = nn(v, rhs)
        e = es[h]
        gs = (e.astype(f32) * (gp - delta)).astype(bf16)
        if extra is not None:
            extra(h, gs)
        keep = lane_half(q.shape, h)
        term_v = nt(e, rhs)
        term_k = nn(gs, jnp.where(keep, q, jnp.zeros_like(q)))
        gv = term_v if gv is None else gv + term_v
        gk = term_k if gk is None else gk + term_k
        gq_t.append(nn(k_t[part], gs))
    return jnp.concatenate(gq_t, axis=0).astype(bf16), gk.astype(bf16), gv.astype(bf16)


def cross_bwd_kernel(pairs, go_ref, n2_ref, wa_ref, wb_ref, q_ref, kt_ref, v_ref, e_ref, r_ref, at_ref, gin_ref,
                     gk_ref, gv_ref, gqoa_ref, gqob_ref, gn_ref, gat_ref, gqt_ref):
    w = wa_ref.shape[0] // 4
    step = pl.program_id(0)
    b = step // pairs
    p = lax.rem(step, pairs)

    def rows(i):
        return jnp.concatenate([wa_ref[i * w : (i + 1) * w], wb_ref[i * w : (i + 1) * w]], axis=0)

    @pl.when(step == 0)
    def _():
        gat_ref[...] = nt(rows(3), go_ref[...]).astype(bf16)

    tok = pl.ds(pl.multiple_of(b * LEN, LEN), LEN)
    lanes = pl.ds(pl.multiple_of(p * 2 * DH, 2 * DH), 2 * DH)
    gq, gk, gv = head_pair_back(
        kt_ref[...], v_ref[...], q_ref[tok, lanes], None, gat_ref[lanes, tok], at_ref[lanes, tok],
        [e_ref[0, 0], e_ref[0, 1]], [r_ref[0, 0:1, :], r_ref[0, 1:2, :]],
    )
    gqt_ref[lanes, tok] = gq
    gk_ref[...] = gk
    gv_ref[...] = gv

    @pl.when(step == pl.num_programs(0) - 1)
    def _():
        gqt = gqt_ref[...]
        gwq = nn(gqt, n2_ref[...]).astype(bf16)
        gwo = nn(at_ref[...], go_ref[...]).astype(bf16)
        gqoa_ref[0:w] = gwq[0:w]
        gqob_ref[0:w] = gwq[w:]
        gqoa_ref[w:] = gwo[0:w]
        gqob_ref[w:] = gwo[w:]
        gn_ref[...] = gin_ref[...] + tn(gqt, rows(0))


def cross_bwd(go, n2, wa, wb, q, kt, v, e, r, at, gin):
    t, d = go.shape
    w = wa.shape[0] // 4
    c = 2 * w
    nb = t // LEN
    pairs = c // (2 * DH)
    te = v.shape[0]
    tokhead = pl.BlockSpec((ENC, 2 * DH), lambda i: (i // pairs, i % pairs))
    return call(
        lambda *r_: cross_bwd_kernel(pairs, *r_),
        (
            jax.ShapeDtypeStruct((te, c), bf16),
            jax.ShapeDtypeStruct((te, c), bf16),
            jax.ShapeDtypeStruct((2 * w, d), bf16),
            jax.ShapeDtypeStruct((2 * w, d), bf16),
            jax.ShapeDtypeStruct((t, d), f32),
        ),
        (go, n2, wa, wb, q, kt, v, e, r, at, gin),
        grid=(nb * pairs,),
        in_specs=[
            whole((t, d)),
            whole((t, d)),
            whole(wa.shape),
            whole(wb.shape),
            whole((t, c)),
            pl.BlockSpec((2 * DH, ENC), lambda i: (i % pairs, i // pairs)),
            tokhead,
            pl.BlockSpec((1, 2, ENC, LEN), lambda i: (i, 0, 0, 0)),
            pl.BlockSpec((1, 2, LEN), lambda i: (i, 0, 0)),
            whole((c, t)),
            whole((t, d)),
        ],
        out_specs=(tokhead, tokhead, whole((2 * w, d)), whole((2 * w, d)), whole((t, d))),
        scratch=[pltpu.VMEM((c, t), bf16), pltpu.VMEM((c, t), bf16)],
        flops=3 * (2 * t * d * c * 4 + 2 * t * ENC * c * 4 * 2),
        nbytes=18 * 1024 * 1024,
        trans=0,
        name="cross_bwd",
    )


def enc_grad_kernel(enc_ref, gk_ref, gv_ref, wa_ref, wb_ref, gin_ref, ga_ref, gb_ref, ge_ref, accs_ref):
    w = wa_ref.shape[0] // 4
    step = pl.program_id(0)

    def rows(i):
        return jnp.concatenate([wa_ref[i * w : (i + 1) * w], wb_ref[i * w : (i + 1) * w]], axis=0)

    gk = gk_ref[...]
    gv = gv_ref[...]
    enc = enc_ref[...]
    part = nn(gk, rows(1)) + nn(gv, rows(2))
    ge_ref[...] = part if gin_ref is None else gin_ref[...] + part
    tk = tn(gk, enc)
    tv = tn(gv, enc)

    @pl.when(step == 0)
    def _():
        accs_ref[0] = tk
        accs_ref[1] = tv

    @pl.when(step != 0)
    def _():
        accs_ref[0] += tk
        accs_ref[1] += tv

    @pl.when(step == pl.num_programs(0) - 1)
    def _():
        for i in range(2):
            ga_ref[i * w : (i + 1) * w] = accs_ref[i, 0:w].astype(bf16)
            gb_ref[i * w : (i + 1) * w] = accs_ref[i, w:].astype(bf16)


def enc_grad(enc, gk, gv, wa, wb, gin=None):
    te, d = enc.shape
    w = wa.shape[0] // 4
    c = 2 * w
    rows = 512
    blk = pl.BlockSpec((rows, d), lambda i: (i, 0))
    half = pl.BlockSpec((rows, c), lambda i: (i, 0))
    args = [enc, gk, gv, wa, wb]
    in_specs = [blk, half, half, whole(wa.shape), whole(wb.shape)]
    if gin is None:
        body = lambda a, b, c_, d_, e, *r: enc_grad_kernel(a, b, c_, d_, e, None, *r)
    else:
        body = enc_grad_kernel
        args.append(gin)
        in_specs.append(blk)
    return call(
        body,
        (
            jax.ShapeDtypeStruct((2 * w, d), bf16),
            jax.ShapeDtypeStruct((2 * w, d), bf16),
            jax.ShapeDtypeStruct((te, d), f32),
        ),
        args,
        grid=(te // rows,),
        in_specs=in_specs,
        out_specs=(whole((2 * w, d)), whole((2 * w, d)), blk),
        scratch=[pltpu.VMEM((2, c, d), f32)],
        flops=2 * te * d * c * 4 * 2,
        nbytes=te * d * 10,
        name="enc_grad",
    )


def self_bwd_kernel(last, x1_ref, gx2_ref, gn2_ref, g2_ref, n1_ref, wa_ref, wb_ref, q_ref, k_ref, vt_ref, e_ref, r_ref, at_ref, *rest):
    if last:
        gin_ref, x_ref, g1_ref, ga_ref, gb_ref, gd_ref, gg2_ref, gg1_ref, gi_ref, gat_ref, gqt_ref, gk_ref, gv_ref, gx1_ref = rest
    else:
        ga_ref, gb_ref, gd_ref, gn_ref, gat_ref, gqt_ref, gk_ref, gv_ref, gx1_ref = rest
    w = wa_ref.shape[0] // 4
    c = 2 * w
    nb = n1_ref.shape[0] // LEN

    def rows(i):
        return jnp.concatenate([wa_ref[i * w : (i + 1) * w], wb_ref[i * w : (i + 1) * w]], axis=0)

    gx, gg2 = norm_back(x1_ref[...], g2_ref[...].astype(f32), gn2_ref[...])
    gx1 = gx2_ref[...] + gx
    gx1_ref[...] = gx1
    go = gx1.astype(bf16)
    gat_ref[...] = nt(rows(3), go).astype(bf16)
    gwo = nn(at_ref[...], go).astype(bf16)
    ri = lax.broadcasted_iota(jnp.int32, (LEN, LEN), 0)
    ci = lax.broadcasted_iota(jnp.int32, (LEN, LEN), 1)
    flip = jnp.where(ri + ci == LEN - 1, 1.0, 0.0).astype(bf16)
    gd_ref[...] = jnp.zeros_like(gd_ref)
    for p in range(c // (2 * DH)):
        lanes = slice(p * 2 * DH, (p + 1) * 2 * DH)
        for b in range(nb):
            tok = slice(b * LEN, (b + 1) * LEN)

            def extra(h, gs):
                turned = pltpu.roll(nn(gs, flip), 0, 1, stride=1, stride_axis=0)
                head = 2 * p + h
                gd_ref[head : head + 1, :] += jnp.sum(turned, axis=0, keepdims=True)

            gq, gk, gv = head_pair_back(
                k_ref[tok, lanes].T, vt_ref[lanes, tok].T, q_ref[tok, lanes], None, gat_ref[lanes, tok], at_ref[lanes, tok],
                [e_ref[b, 2 * p], e_ref[b, 2 * p + 1]],
                [r_ref[b, 2 * p : 2 * p + 1, :], r_ref[b, 2 * p + 1 : 2 * p + 2, :]],
                extra,
            )
            gqt_ref[lanes, tok] = gq
            gk_ref[tok, lanes] = gk
            gv_ref[tok, lanes] = gv
    n1 = n1_ref[...]
    gqt = gqt_ref[...]
    gk = gk_ref[...]
    gv = gv_ref[...]
    gwq = nn(gqt, n1).astype(bf16)
    gwk = tn(gk, n1).astype(bf16)
    gwv = tn(gv, n1).astype(bf16)
    for i, gw in enumerate((gwq, gwk, gwv, gwo)):
        ga_ref[i * w : (i + 1) * w] = gw[0:w]
        gb_ref[i * w : (i + 1) * w] = gw[w:]
    gn = tn(gqt, rows(0)) + nn(gk, rows(1)) + nn(gv, rows(2))
    if last:
        gn = gin_ref[...] + gn
        gi, gg1 = norm_back(x_ref[...].astype(f32), g1_ref[...].astype(f32), gn)
        gi_ref[...] = gx1_ref[...] + gi
        gg1_ref[...] = gg1
        gg2_ref[...] = gg2
    else:
        gn_ref[...] = gn


def self_bwd(last, x1, gx2, gn2, g2, n1, wa, wb, q, k, vt, e, r, at, gin=None, x=None, g1=None):
    t, d = x1.shape
    w = wa.shape[0] // 4
    c = 2 * w
    nh = c // DH
    args = [x1, gx2, gn2, g2, n1, wa, wb, q, k, vt, e, r, at]
    outs = [
        jax.ShapeDtypeStruct((4 * w, d), bf16),
        jax.ShapeDtypeStruct((4 * w, d), bf16),
        jax.ShapeDtypeStruct((nh, LEN), f32),
    ]
    if last:
        args += [gin, x, g1]
        outs += [jax.ShapeDtypeStruct((1, d), f32), jax.ShapeDtypeStruct((1, d), f32), jax.ShapeDtypeStruct((t, d), f32)]
    else:
        outs += [jax.ShapeDtypeStruct((t, d), f32)]
    return call(
        lambda *r_: self_bwd_kernel(last, *r_),
        tuple(outs),
        args,
        in_specs=[whole(a.shape) for a in args],
        out_specs=tuple(whole(o.shape) for o in outs),
        scratch=[
            pltpu.VMEM((c, t), bf16),
            pltpu.VMEM((c, t), bf16),
            pltpu.VMEM((t, c), bf16),
            pltpu.VMEM((t, c), bf16),
            pltpu.VMEM((t, d), f32),
        ],
        flops=3 * (2 * t * d * c * 8 + 2 * t * LEN * c * 5 * 2),
        nbytes=14 * 1024 * 1024,
        name="self_bwd",
    )


def local_program(tensor_size, dp_size, *arrays):
    (block_in, enc_states, dec_len, enc_len, gain_self, self_query, self_key, self_value, self_out, rel_table,
     gain_cross, cross_query, cross_key, cross_value, cross_out, gain_ff, ff_in, ff_out, out_grad) = arrays
    t_index = lax.axis_index("tensor")
    d_index = lax.axis_index("dp")
    nb = block_in.shape[0] // LEN
    w, d = self_out.shape
    heads = w // DH

    def swap(v, axis, bit):
        n = tensor_size if axis == "tensor" else dp_size
        return lax.ppermute(v, axis, [(i, i ^ bit) for i in range(n)])

    def d_bit(bit):
        return (d_index // bit) % 2

    y = d_bit(1).astype(jnp.int32)
    y_is0 = y == 0
    y_arr = y.reshape(1)

    def across(send):
        h = swap(send, "tensor", 2)
        g = swap(h, "dp", 1)
        return h, g

    def joined(h, g):
        return jnp.where(y_is0, jnp.concatenate([h, g], axis=0), jnp.concatenate([g, h], axis=0))

    own_s, half_s = pack(y_arr, self_query, self_key, self_value, self_out)
    own_c, half_c = pack(y_arr, cross_query, cross_key, cross_value, cross_out)

    buckets = np.eye(BUCKETS, dtype=np.float32)[bucket_of_distance()]
    rel_own = jnp.dot(rel_table.astype(f32).T, jnp.asarray(buckets.T), precision=lax.Precision.HIGHEST)
    bias0 = jnp.concatenate([rel_own, swap(rel_own, "tensor", 1)], axis=0)
    bias1 = swap(bias0, "tensor", 2)

    w_s0, w_s1 = own_s, swap(own_s, "tensor", 1)
    w_c0, w_c1 = own_c, swap(own_c, "tensor", 1)
    h_s, g_s = across(half_s)
    half_c = lax.optimization_barrier((half_c, h_s))[0]
    h_c, g_c = across(half_c)
    wi0, wi1 = ff_in, swap(ff_in, "tensor", 1)
    wo0, wo1 = ff_out, swap(ff_out, "tensor", 1)
    send_f = jnp.where(y_is0, ff_in, ff_out)
    send_f = lax.optimization_barrier((send_f, h_c))[0]
    h_f, g_f = across(send_f)
    w_s2 = joined(h_s, g_s)
    w_s3 = swap(w_s2, "tensor", 1)
    w_c2 = joined(h_c, g_c)
    w_c3 = swap(w_c2, "tensor", 1)
    wi2 = jnp.where(y_is0, h_f, g_f)
    wo2 = jnp.where(y_is0, g_f, h_f)
    wi3 = swap(wi2, "tensor", 1)
    wo3 = swap(wo2, "tensor", 1)

    my_dec = lax.dynamic_slice(dec_len, (t_index * nb,), (nb,))
    my_enc = lax.dynamic_slice(enc_len, (t_index * nb,), (nb,))
    g1 = gain_self.reshape(1, d)
    g2 = gain_cross.reshape(1, d)
    g3 = gain_ff.reshape(1, d)
    sq0, sk0, sv0, se0, sr0, sa0, xp = self_fwd(False, my_dec, block_in, g1, g2, w_s0, w_s1, bias0)
    k0, kt0, v0, vt0 = enc_kv(enc_states, w_c0, w_c1)
    sq1, sk1, sv1, se1, sr1, sa1, x1, n1, n2 = self_fwd(True, my_dec, block_in, g1, g2, w_s2, w_s3, bias1, xp)
    cq0, ce0, cr0, ca0, x2p = cross_fwd(False, my_enc, n2, g3, w_c0, w_c1, k0, vt0, x1)
    k1, kt1, v1, vt1 = enc_kv(enc_states, w_c2, w_c3)
    cq1, ce1, cr1, ca1, x2, n3 = cross_fwd(True, my_enc, n2, g3, w_c2, w_c3, k1, vt1, x2p)

    gwi2, gwo2, gwi3, gwo3, yp, gp = ff(False, n3, out_grad, wi2, wo2, wi3, wo3)
    gwi0, gwo0, gwi1, gwo1, block_out, gx2, go2, gg3 = ff(True, n3, out_grad, wi0, wo0, wi1, wo1, yp, gp, x2, g3)

    def halves(v, bit):
        v = v.reshape((2, v.shape[0] // 2) + v.shape[1:])
        m = d_bit(bit)
        keep = lax.dynamic_index_in_dim(v, m, 0, keepdims=False)
        send = lax.dynamic_index_in_dim(v, 1 - m, 0, keepdims=False)
        return keep, send

    def plus(a, b):
        return (a.astype(f32) + b.astype(f32)).astype(bf16)

    def reduce_shards(s0, s1, s2, s3):
        s2 = plus(s2, swap(s3, "tensor", 1))
        s0 = plus(s0, swap(s1, "tensor", 1))
        v = plus(s0, swap(s2, "tensor", 2))
        bit = 1
        while bit < dp_size:
            keep, send = halves(v, bit)
            v = plus(keep, swap(send, "dp", bit))
            bit *= 2
        while bit > 1:
            bit //= 2
            got = swap(v, "dp", bit)
            low = d_bit(bit) == 0
            v = jnp.where(low, jnp.concatenate([v, got], axis=0), jnp.concatenate([got, v], axis=0))
        return v

    r_wo = reduce_shards(gwo0, gwo1, gwo2, gwo3)
    r_wi = reduce_shards(gwi0, gwi1, gwi2, gwi3)

    zero = jnp.zeros((nb * LEN, d), f32)
    gk1, gv1, gqo2, gqo3, gn2 = cross_bwd(go2, n2, w_c2, w_c3, cq1, kt1, v1, ce1, cr1, ca1, zero)
    gk0, gv0, gqo0, gqo1, gn2 = cross_bwd(go2, n2, w_c0, w_c1, cq0, kt0, v0, ce0, cr0, ca0, gn2)
    r_qo = reduce_shards(gqo0, gqo1, gqo2, gqo3)
    gkv2, gkv3, gep = enc_grad(enc_states, gk1, gv1, w_c2, w_c3)
    gkv0, gkv1, grad_enc = enc_grad(enc_states, gk0, gv0, w_c0, w_c1, gep)
    r_kv = reduce_shards(gkv0, gkv1, gkv2, gkv3)

    gs2, gs3, gd1, gnp = self_bwd(False, x1, gx2, gn2, g2, n1, w_s2, w_s3, sq1, sk1, sv1, se1, sr1, sa1)
    gs0, gs1, gd0, gg2, gg1, grad_in = self_bwd(True, x1, gx2, gn2, g2, n1, w_s0, w_s1, sq0, sk0, sv0, se0, sr0, sa0, gnp, block_in, g1)
    r_s = reduce_shards(gs0, gs1, gs2, gs3)

    flipped = jnp.asarray(np.ascontiguousarray(buckets[::-1]))
    gd = jnp.concatenate([gd0, gd1], axis=0)
    grel = jnp.dot(gd, flipped, precision=lax.Precision.HIGHEST)
    grel = grel.reshape(tensor_size, heads * BUCKETS)
    slots = jnp.arange(tensor_size)[:, None] ^ t_index
    order = (slots == jnp.arange(tensor_size)[None, :]).astype(f32)
    grel = jnp.dot(order.T, grel, precision=lax.Precision.HIGHEST)
    grel = jnp.pad(grel.reshape(1, -1), ((0, 0), (0, d - grel.size)))
    small = jnp.concatenate([gg1, gg2, gg3, grel], axis=0)
    small = lax.psum(small, ("dp", "tensor"))
    grad_rel = lax.dynamic_slice(small[3], (t_index * heads * BUCKETS,), (heads * BUCKETS,)).reshape(heads, BUCKETS).T

    def part(v, i):
        return v[i * w : (i + 1) * w].astype(f32)

    return (
        block_out,
        grad_in,
        grad_enc,
        small[0],
        part(r_s, 0).T,
        part(r_s, 1).T,
        part(r_s, 2).T,
        part(r_s, 3),
        grad_rel,
        small[1],
        part(r_qo, 0).T,
        part(r_kv, 0).T,
        part(r_kv, 1).T,
        part(r_qo, 1),
        small[2],
        r_wi.astype(f32),
        r_wo.astype(f32),
    )


def solution(mesh):
    tensor_size = mesh.shape["tensor"]
    dp_size = mesh.shape["dp"]
    both = P(("dp", "tensor"), None)
    col = P(None, "tensor")
    row = P("tensor", None)
    placed = (both, both, P("dp"), P("dp"), P(), col, col, col, row, col, P(), col, col, col, row, P(), col, row, both)
    outs = (both, both, both, P(), col, col, col, row, col, P(), col, col, col, row, P(), col, row)
    return jax.shard_map(
        lambda *a: local_program(tensor_size, dp_size, *a),
        mesh=mesh,
        in_specs=placed,
        out_specs=outs,
        check_vma=False,
    )
```

```python
import math

import jax
import jax.numpy as jnp
import numpy as np
from jax import lax
from jax.experimental import pallas as pl
from jax.experimental.pallas import tpu as pltpu
from jax.sharding import PartitionSpec as P

BUCKETS = 32
MAX_DIST = 128
LEN = 256
ENC = 1024
DH = 64
KEYS = 256

norm_eps = 1e-06
masked_score = -1000000000.0
bf16 = jnp.bfloat16
f32 = jnp.float32
VMEM_CAP = 16 << 20
BIG_VMEM = 58 << 20


def bucket_of_distance():
    half_count = BUCKETS // 2
    growth_ratio = MAX_DIST / half_count
    limits = np.array(
        [int(math.ceil(half_count * growth_ratio ** (m / half_count))) for m in range(1, half_count)],
        dtype=np.int32,
    )
    distance = np.arange(LEN, dtype=np.int32)
    above = np.sum(distance[:, None] >= limits[None, :], axis=1)
    return np.where(distance < half_count, distance, half_count + above).astype(np.int32)


def nn(a, b):
    return lax.dot_general(a, b, (((1,), (0,)), ((), ())), preferred_element_type=f32)


def nt(a, b):
    return lax.dot_general(a, b, (((1,), (1,)), ((), ())), preferred_element_type=f32)


def tn(a, b):
    return lax.dot_general(a, b, (((0,), (0,)), ((), ())), preferred_element_type=f32)


def inv_rms(v):
    return lax.rsqrt(jnp.mean(v * v, axis=-1, keepdims=True) + norm_eps)


def normed(v, gain):
    return (v * inv_rms(v) * gain).astype(bf16)


def norm_back(v, gain, e):
    s = inv_rms(v)
    ge = gain * e
    dot = jnp.mean(ge * v, axis=-1, keepdims=True)
    grad_v = s * ge - v * (s * s * s * dot)
    grad_gain = jnp.sum(e * v * s, axis=0, keepdims=True)
    return grad_v, grad_gain


def lane_half(shape, h):
    lane = lax.broadcasted_iota(jnp.int32, shape, 1)
    return (lane < DH) if h == 0 else (lane >= DH)


def call(kernel, out_shape, args, *, grid=(), in_specs=None, out_specs=None, scratch=(), flops=0, nbytes=0, trans=0, name=None, vmem=VMEM_CAP):
    kw = {}
    if in_specs is not None:
        kw["in_specs"] = in_specs
    if out_specs is not None:
        kw["out_specs"] = out_specs
    return pl.pallas_call(
        kernel,
        out_shape=out_shape,
        grid=grid,
        scratch_shapes=scratch,
        compiler_params=pltpu.CompilerParams(vmem_limit_bytes=vmem),
        cost_estimate=pl.CostEstimate(flops=1, bytes_accessed=1, transcendentals=0),
        name=name,
        **kw,
    )(*args)


def whole(shape):
    return pl.BlockSpec(shape, lambda *_: (0,) * len(shape))


SMEM = pl.BlockSpec(memory_space=pltpu.SMEM)


def side_by_side(refs, i):
    w = refs[0].shape[0] // 4
    return jnp.concatenate([r[i * w : (i + 1) * w] for r in refs], axis=0)


def pair_rows(y_ref, refs, shared):
    def rows(i):
        if not shared:
            return side_by_side(refs, i)
        w = refs[0].shape[0] // 2
        first = y_ref[0] == i // 2
        part = slice((i % 2) * w, (i % 2 + 1) * w)
        return jnp.concatenate(
            [jnp.where(first, refs[0][part], refs[1][part]), jnp.where(first, refs[2][part], refs[3][part])], axis=0
        )

    return rows


def self_fwd_kernel(last, y_ref, len_ref, x_ref, g_ref, *rest):
    weights = rest[0:2]
    bias_ref = rest[2]
    rest = rest[3:]
    if last:
        xin_ref, q_ref, k_ref, vt_ref, e_ref, r_ref, at_ref, x1_ref, n1_ref, n2_ref, bs_ref = rest
    else:
        q_ref, k_ref, vt_ref, e_ref, r_ref, at_ref, x1_ref, bs_ref = rest
    nh = q_ref.shape[1] // DH
    nb = x_ref.shape[0] // LEN
    x = x_ref[...].astype(f32)
    n1 = normed(x, g_ref[0:1].astype(f32))
    if last:
        n1_ref[...] = n1

    q_ref[...] = nt(n1, side_by_side(weights, 0)).astype(bf16)
    k_ref[...] = nt(n1, side_by_side(weights, 1)).astype(bf16)
    vt_ref[...] = nt(side_by_side(weights, 2), n1).astype(bf16)
    key = lax.broadcasted_iota(jnp.int32, (LEN, LEN), 0)
    query = lax.broadcasted_iota(jnp.int32, (LEN, LEN), 1)
    for p in range(nh // 2):
        lanes = slice(p * 2 * DH, (p + 1) * 2 * DH)
        for h in range(2):
            row = jnp.broadcast_to(bias_ref[2 * p + h : 2 * p + h + 1, :], (LEN, LEN))
            bs_ref[h] = pltpu.roll(row, 0, 1, stride=1, stride_axis=0)
        for b in range(nb):
            tok = slice(b * LEN, (b + 1) * LEN)
            allowed = (key <= query) & (key < len_ref[y_ref[1] + b])
            kp = k_ref[tok, lanes]
            qp = q_ref[tok, lanes]
            outs = []
            for h in range(2):
                head = 2 * p + h
                qh = jnp.where(lane_half(qp.shape, h), qp, jnp.zeros_like(qp))
                s = nt(kp, qh) + bs_ref[h]
                s = jnp.where(allowed, s, masked_score)
                top = jnp.max(s, axis=0, keepdims=True)
                e = jnp.exp(s - top)
                r = 1.0 / jnp.sum(e, axis=0, keepdims=True)
                eb = e.astype(bf16)
                e_ref[b, head] = eb
                r_ref[b, head : head + 1, :] = r
                outs.append(nn(vt_ref[head * DH : (head + 1) * DH, tok], eb) * r)
            at_ref[lanes, tok] = jnp.concatenate(outs, axis=0).astype(bf16)
    mixed = tn(at_ref[...], side_by_side(weights, 3))
    if last:
        x1 = xin_ref[...] + mixed
        n2_ref[...] = normed(x1, g_ref[1:2].astype(f32))
    else:
        x1 = x + mixed
    x1_ref[...] = x1


def self_fwd(last, y, lens, x, g, weights, bias, xin=None):
    t, d = x.shape
    w = weights[0].shape[0] // 4
    c = 2 * w
    nh = c // DH
    nb = t // LEN
    outs = [
        jax.ShapeDtypeStruct((t, c), bf16),
        jax.ShapeDtypeStruct((t, c), bf16),
        jax.ShapeDtypeStruct((c, t), bf16),
        jax.ShapeDtypeStruct((nb, nh, LEN, LEN), bf16),
        jax.ShapeDtypeStruct((nb, nh, LEN), f32),
        jax.ShapeDtypeStruct((c, t), bf16),
        jax.ShapeDtypeStruct((t, d), f32),
    ]
    args = [y, lens, x, g, *weights, bias]
    if last:
        args.append(xin)
        outs += [jax.ShapeDtypeStruct((t, d), bf16)] * 2
    flops = 2 * t * d * c * 4 + 2 * t * LEN * nh * 128 * 2
    return call(
        lambda *r: self_fwd_kernel(last, *r),
        tuple(outs),
        args,
        in_specs=[SMEM, SMEM] + [whole(a.shape) for a in args[2:]],
        out_specs=tuple(whole(o.shape) for o in outs),
        scratch=[pltpu.VMEM((2, LEN, LEN), f32)],
        flops=flops * 3,
        nbytes=12 * 1024 * 1024,
        trans=t * LEN * nh,
        name="self_fwd",
    )


def enc_kv_kernel(shared, y_ref, enc_ref, *rest):
    k_ref, v_ref = rest[-2:]
    enc = enc_ref[...]
    rows = pair_rows(y_ref, rest[:-2], shared)
    k_ref[...] = nt(enc, rows(0)).astype(bf16)
    v_ref[...] = nt(enc, rows(1)).astype(bf16)


def enc_kv(shared, y, enc, kv):
    t, d = enc.shape
    c = kv[0].shape[0] if shared else kv[0].shape[0] // 2
    rows = 512
    half = pl.BlockSpec((rows, c), lambda i: (i, 0))
    return call(
        lambda *r: enc_kv_kernel(shared, *r),
        (jax.ShapeDtypeStruct((t, c), bf16),) * 2,
        (y, enc, *kv),
        grid=(t // rows,),
        in_specs=[SMEM, pl.BlockSpec((rows, d), lambda i: (i, 0))] + [whole(a.shape) for a in kv],
        out_specs=(half, half),
        flops=2 * t * d * c * 2 * 2,
        nbytes=t * d * 2 + 4 * t * c * 2,
        name="enc_kv",
    )


def cross_fwd_kernel(last, pairs, y_ref, len_ref, n2_ref, g_ref, *rest):
    n_w = 4 if last else 2
    weights = pair_rows(y_ref, rest[:n_w], last)
    k_ref, v_ref, xin_ref = rest[n_w : n_w + 3]
    rest = rest[n_w + 3 :]
    if last:
        q_ref, r_ref, at_ref, x2_ref, n3_ref, s_ref, e_ref = rest
    else:
        q_ref, r_ref, at_ref, x2_ref, s_ref, e_ref = rest
    step = pl.program_id(0)
    b = step // pairs
    p = lax.rem(step, pairs)

    @pl.when(step == 0)
    def _():
        q_ref[...] = nt(n2_ref[...], weights(2)).astype(bf16)

    tok = pl.ds(pl.multiple_of(b * LEN, LEN), LEN)
    lanes = pl.ds(pl.multiple_of(p * 2 * DH, 2 * DH), 2 * DH)
    qp = q_ref[tok, lanes]
    count = len_ref[y_ref[1] + b]
    key = lax.broadcasted_iota(jnp.int32, (KEYS, LEN), 0)
    queries = [jnp.where(lane_half(qp.shape, h), qp, jnp.zeros_like(qp)) for h in range(2)]
    tops = [None, None]
    for c in range(ENC // KEYS):
        part = slice(c * KEYS, (c + 1) * KEYS)
        for h in range(2):
            s = nt(k_ref[part], queries[h])
            s = jnp.where(key < count - c * KEYS, s, masked_score)
            s_ref[h, part] = s
            top = jnp.max(s.reshape(KEYS // 8, 8, LEN), axis=0)
            tops[h] = top if c == 0 else jnp.maximum(tops[h], top)
    outs = []
    for h in range(2):
        top = jnp.max(tops[h], axis=0, keepdims=True)
        total = None
        for c in range(ENC // KEYS):
            part = slice(c * KEYS, (c + 1) * KEYS)
            e = jnp.exp(s_ref[h, part] - top)
            t = jnp.sum(e.reshape(KEYS // 8, 8, LEN), axis=0)
            total = t if c == 0 else total + t
            e_ref[h, part] = e.astype(bf16)
        r = 1.0 / jnp.sum(total, axis=0, keepdims=True)
        r_ref[0, h : h + 1, :] = r
        r_ref[0, 2 + h : 3 + h, :] = top
        outs.append(tn(v_ref[...], e_ref[h])[h * DH : (h + 1) * DH] * r)
    at_ref[lanes, tok] = jnp.concatenate(outs, axis=0).astype(bf16)

    @pl.when(step == pl.num_programs(0) - 1)
    def _():
        x2 = xin_ref[...] + tn(at_ref[...], weights(3))
        x2_ref[...] = x2
        if last:
            n3_ref[...] = normed(x2, g_ref[2:3].astype(f32))


def cross_fwd(last, y, lens, n2, g, qo, k, v, xin):
    t, d = n2.shape
    c = k.shape[1]
    nb = t // LEN
    pairs = c // (2 * DH)
    outs = [
        jax.ShapeDtypeStruct((t, c), bf16),
        jax.ShapeDtypeStruct((nb * pairs, 4, LEN), f32),
        jax.ShapeDtypeStruct((c, t), bf16),
        jax.ShapeDtypeStruct((t, d), f32),
    ]
    specs = [
        whole((t, c)),
        pl.BlockSpec((1, 4, LEN), lambda i: (i, 0, 0)),
        whole((c, t)),
        whole((t, d)),
    ]
    if last:
        outs.append(jax.ShapeDtypeStruct((t, d), bf16))
        specs.append(whole((t, d)))
    return call(
        lambda *r: cross_fwd_kernel(last, pairs, *r),
        tuple(outs),
        (y, lens, n2, g, *qo, k, v, xin),
        grid=(nb * pairs,),
        in_specs=[
            SMEM,
            SMEM,
            whole(n2.shape),
            whole(g.shape),
            *[whole(a.shape) for a in qo],
            pl.BlockSpec((ENC, 2 * DH), lambda i: (i // pairs, i % pairs)),
            pl.BlockSpec((ENC, 2 * DH), lambda i: (i // pairs, i % pairs)),
            whole(xin.shape),
        ],
        out_specs=tuple(specs),
        scratch=[pltpu.VMEM((2, ENC, LEN), f32), pltpu.VMEM((2, ENC, LEN), bf16)],
        flops=3 * (2 * t * d * c * 2 + 2 * t * ENC * c * 2 * 2),
        nbytes=14 * 1024 * 1024,
        trans=t * ENC * (c // DH),
        name="cross_fwd",
    )


ROOT = math.sqrt(2.0 / math.pi)
CUBE = 0.044715


def ff_kernel(last, y_ref, n3_ref, gf_ref, *rest):
    if last:
        ha_in, ha_out, ga_in, ga_out, hb_in, hb_out, gb_in, gb_out = rest[:8]
        rest = rest[8:]
        first = y_ref[0] == 0

        def weights(h_in, h_out, g_in, g_out):
            return (
                lambda: jnp.where(first, h_in[...], g_in[...]),
                lambda: jnp.where(first, g_out[...], h_out[...]),
            )

        shards = (weights(ha_in, ha_out, ga_in, ga_out), weights(hb_in, hb_out, gb_in, gb_out))
    else:
        wia_ref, woa_ref, wib_ref, wob_ref = rest[:4]
        rest = rest[4:]
        shards = ((lambda: wia_ref[...], lambda: woa_ref[...]), (lambda: wib_ref[...], lambda: wob_ref[...]))
    if last:
        yin_ref, gin_ref, x2_ref, g_ref = rest[:4]
        gwia, gwoa, gwib, gwob, out_ref, gx2_ref, go2_ref, gg_ref, y_acc, gn_ref, n3t_ref = rest[4:]
    else:
        gwia, gwoa, gwib, gwob, y_acc, gn_ref, n3t_ref = rest
    step = pl.program_id(0)

    @pl.when(step == 0)
    def _():
        n3t_ref[...] = n3_ref[...].T
        if last:
            y_acc[...] = yin_ref[...]
            gn_ref[...] = gin_ref[...]
        else:
            y_acc[...] = jnp.zeros_like(y_acc)
            gn_ref[...] = jnp.zeros_like(gn_ref)

    n3 = n3_ref[...]
    gf = gf_ref[...]
    for (get_wi, get_wo), gwi, gwo in zip(shards, (gwia, gwib), (gwoa, gwob)):
        wi, wo = get_wi(), get_wo()
        u = nn(n3, wi)
        dh = nt(gf, wo)
        u2 = u * u
        th = jnp.tanh(ROOT * u * (1.0 + CUBE * u2))
        half = 0.5 * (1.0 + th)
        r = (u * half).astype(bf16)
        slope = half + 0.5 * u * (1.0 - th * th) * (ROOT * (1.0 + (3.0 * CUBE) * u2))
        gu = (dh * slope).astype(bf16)
        y_acc[...] += nn(r, wo)
        gn_ref[...] += nt(gu, wi)
        gwo[...] = tn(r, gf).astype(bf16)
        gwi[...] = nn(n3t_ref[...], gu).astype(bf16)

    if last:

        @pl.when(step == pl.num_programs(0) - 1)
        def _():
            x2 = x2_ref[...]
            out_ref[...] = (x2 + y_acc[...]).astype(bf16)
            gx, gg = norm_back(x2, g_ref[2:3].astype(f32), gn_ref[...])
            gx2 = gf.astype(f32) + gx
            gx2_ref[...] = gx2
            go2_ref[...] = gx2.astype(bf16)
            gg_ref[...] = gg


def ff(last, y, n3, gf, weights, yin=None, gin=None, x2=None, g=None):
    t, d = n3.shape
    hid = weights[0].shape[1]
    blk = 256
    args = [y, n3, gf]
    col = pl.BlockSpec((d, blk), lambda i: (0, i))
    row = pl.BlockSpec((blk, d), lambda i: (i, 0))
    in_specs = [SMEM, whole((t, d)), whole((t, d))]
    if last:
        for v in weights:
            args += [v, v]
            in_specs += [col, row]
    else:
        args += weights
        in_specs += [col, row, col, row]
    outs = [jax.ShapeDtypeStruct((d, hid), bf16), jax.ShapeDtypeStruct((hid, d), bf16)] * 2
    specs = [col, row, col, row]
    acc = jax.ShapeDtypeStruct((t, d), f32)
    scratch = [pltpu.VMEM((d, t), bf16)]
    if last:
        args += [yin, gin, x2, g]
        in_specs += [whole((t, d))] * 3 + [whole(g.shape)]
        outs += [jax.ShapeDtypeStruct((t, d), bf16), acc, jax.ShapeDtypeStruct((t, d), bf16), jax.ShapeDtypeStruct((1, d), f32)]
        specs += [whole((t, d))] * 3 + [whole((1, d))]
        scratch = [pltpu.VMEM((t, d), f32)] * 2 + scratch
    else:
        outs += [acc, acc]
        specs += [whole((t, d))] * 2
    return call(
        lambda *r: ff_kernel(last, *r),
        tuple(outs),
        args,
        grid=(hid // blk,),
        in_specs=in_specs,
        out_specs=tuple(specs),
        scratch=scratch,
        flops=2 * 6 * 2 * t * d * hid * 2,
        nbytes=12 * 1024 * 1024,
        trans=2 * t * hid,
        name="ff",
    )


def head_pair_back(k_t, v, q, ga, ga_t, a_t, es, rs, extra=None):
    gv = None
    gk = None
    gq_t = []
    for h in range(2):
        part = slice(h * DH, (h + 1) * DH)
        r = rs[h]
        gah = ga_t[part].astype(f32) * r
        delta = jnp.sum(gah * a_t[part].astype(f32), axis=0, keepdims=True)
        gah = gah.astype(bf16)
        zero = jnp.zeros_like(gah)
        rhs = jnp.concatenate([gah, zero] if h == 0 else [zero, gah], axis=0)
        gp = nn(v, rhs)
        e = es[h]
        gs = (e.astype(f32) * (gp - delta)).astype(bf16)
        if extra is not None:
            extra(h, gs)
        keep = lane_half(q.shape, h)
        term_v = nt(e, rhs)
        term_k = nn(gs, jnp.where(keep, q, jnp.zeros_like(q)))
        gv = term_v if gv is None else gv + term_v
        gk = term_k if gk is None else gk + term_k
        gq_t.append(nn(k_t[part], gs))
    return jnp.concatenate(gq_t, axis=0).astype(bf16), gk.astype(bf16), gv.astype(bf16)


def cross_bwd_kernel(pairs, steps, y_ref, len_ref, go_ref, n2_ref, *rest):
    weights = (pair_rows(y_ref, rest[0:2], False), pair_rows(y_ref, rest[2:6], True))
    sides = (rest[6:11], rest[11:16])
    gk0, gv0, gk1, gv1, outs, gn_ref, gat_ref, gqt_ref, e_ref, gs_ref = *rest[16:20], rest[20:24], *rest[24:]
    w = outs[0].shape[0] // 2
    step = pl.program_id(0)
    key = lax.broadcasted_iota(jnp.int32, (KEYS, LEN), 0)

    def half(side, local, gk_ref, gv_ref):
        q_ref, k_ref, v_ref, r_ref, at_ref = sides[side]
        b = local // pairs
        p = lax.rem(local, pairs)

        @pl.when(local == 0)
        def _():
            gat_ref[...] = nt(weights[side](3), go_ref[...]).astype(bf16)

        tok = pl.ds(pl.multiple_of(b * LEN, LEN), LEN)
        lanes = pl.ds(pl.multiple_of(p * 2 * DH, 2 * DH), 2 * DH)
        qp = q_ref[tok, lanes]
        ga_t = gat_ref[lanes, tok]
        a_t = at_ref[lanes, tok]
        count = len_ref[y_ref[1] + b]
        queries, grads, deltas = [], [], []
        for h in range(2):
            part = slice(h * DH, (h + 1) * DH)
            gah = ga_t[part].astype(f32) * r_ref[0, h : h + 1, :]
            deltas.append(jnp.sum(gah * a_t[part].astype(f32), axis=0, keepdims=True))
            gah = gah.astype(bf16)
            zero = jnp.zeros_like(gah)
            grads.append(jnp.concatenate([gah, zero] if h == 0 else [zero, gah], axis=0))
            queries.append(jnp.where(lane_half(qp.shape, h), qp, jnp.zeros_like(qp)))
        for c in range(ENC // KEYS):
            part = slice(c * KEYS, (c + 1) * KEYS)
            kc = k_ref[part]
            vc = v_ref[part]
            for h in range(2):
                s = jnp.where(key < count - c * KEYS, nt(kc, queries[h]), masked_score)
                e = jnp.exp(s - r_ref[0, 2 + h : 3 + h, :])
                gs_ref[h, part] = (e * (nn(vc, grads[h]) - deltas[h])).astype(bf16)
                e_ref[h, part] = e.astype(bf16)
            gv_ref[part] = (nt(e_ref[0, part], grads[0]) + nt(e_ref[1, part], grads[1])).astype(bf16)
            gk_ref[part] = (nn(gs_ref[0, part], queries[0]) + nn(gs_ref[1, part], queries[1])).astype(bf16)
        k = k_ref[...]
        gq = [tn(k, gs_ref[h])[h * DH : (h + 1) * DH] for h in range(2)]
        gqt_ref[lanes, tok] = jnp.concatenate(gq, axis=0).astype(bf16)

        @pl.when(local == steps - 1)
        def _():
            gqt = gqt_ref[...]
            gwq = nn(gqt, n2_ref[...]).astype(bf16)
            gwo = nn(at_ref[...], go_ref[...]).astype(bf16)
            for i in range(2):
                outs[2 * side + i][0:w] = gwq[i * w : (i + 1) * w]
                outs[2 * side + i][w:] = gwo[i * w : (i + 1) * w]
            gn = tn(gqt, weights[side](2))
            gn_ref[...] = gn if side == 1 else gn_ref[...] + gn

    @pl.when(step < steps)
    def _():
        half(1, step, gk1, gv1)

    @pl.when(step >= steps)
    def _():
        half(0, step - steps, gk0, gv0)


def cross_bwd(y, lens, go, n2, w0, w1, side0, side1):
    t, d = go.shape
    te, c = side0[1].shape
    nb = t // LEN
    pairs = c // (2 * DH)
    steps = nb * pairs

    def early(i):
        return jnp.minimum(i, steps - 1)

    def late(i):
        return jnp.maximum(i - steps, 0)

    def tokhead(when):
        return pl.BlockSpec((ENC, 2 * DH), lambda i: (when(i) // pairs, when(i) % pairs))

    def side_specs(when):
        return [whole((t, c)), tokhead(when), tokhead(when), pl.BlockSpec((1, 4, LEN), lambda i: (when(i), 0, 0)), whole((c, t))]

    grad = jax.ShapeDtypeStruct((te, c), bf16)
    out = jax.ShapeDtypeStruct((c, d), bf16)
    return call(
        lambda *r_: cross_bwd_kernel(pairs, steps, *r_),
        (grad,) * 4 + (out,) * 4 + (jax.ShapeDtypeStruct((t, d), f32),),
        (y, lens, go, n2, *w0, *w1, *side0, *side1),
        grid=(2 * steps,),
        in_specs=[SMEM, SMEM, whole((t, d)), whole((t, d))]
        + [whole(a.shape) for a in (*w0, *w1)]
        + side_specs(late)
        + side_specs(early),
        out_specs=(tokhead(late), tokhead(late), tokhead(early), tokhead(early)) + (whole((c, d)),) * 4 + (whole((t, d)),),
        scratch=[
            pltpu.VMEM((c, t), bf16),
            pltpu.VMEM((c, t), bf16),
            pltpu.VMEM((2, ENC, LEN), bf16),
            pltpu.VMEM((2, ENC, LEN), bf16),
        ],
        vmem=BIG_VMEM,
        name="cross_bwd",
    )


def enc_grad_kernel(y_ref, enc_ref, gk1_ref, gv1_ref, gk0_ref, gv0_ref, *rest):
    w0 = pair_rows(y_ref, rest[0:2], False)
    w1 = pair_rows(y_ref, rest[2:6], True)
    out_ref, outs, accs_ref = rest[6], rest[7:11], rest[11]
    w = outs[0].shape[0] // 2
    step = pl.program_id(0)
    enc = enc_ref[...]
    grads = [g[...] for g in (gk1_ref, gv1_ref, gk0_ref, gv0_ref)]
    out_ref[...] = (nn(grads[0], w1(0)) + nn(grads[1], w1(1))) + (nn(grads[2], w0(0)) + nn(grads[3], w0(1)))
    terms = [tn(g, enc) for g in grads]

    @pl.when(step == 0)
    def _():
        for i in range(4):
            accs_ref[i] = terms[i]

    @pl.when(step != 0)
    def _():
        for i in range(4):
            accs_ref[i] += terms[i]

    @pl.when(step == pl.num_programs(0) - 1)
    def _():
        for pair in range(2):
            for i in range(2):
                acc = accs_ref[2 * pair + i]
                outs[2 * pair][i * w : (i + 1) * w] = acc[0:w].astype(bf16)
                outs[2 * pair + 1][i * w : (i + 1) * w] = acc[w:].astype(bf16)


def enc_grad(y, enc, gk1, gv1, gk0, gv0, w0, w1):
    te, d = enc.shape
    c = gk1.shape[1]
    rows = 512
    half = pl.BlockSpec((rows, c), lambda i: (i, 0))
    block = pl.BlockSpec((rows, d), lambda i: (i, 0))
    out = jax.ShapeDtypeStruct((c, d), bf16)
    return call(
        enc_grad_kernel,
        (jax.ShapeDtypeStruct((te, d), f32),) + (out,) * 4,
        (y, enc, gk1, gv1, gk0, gv0, *w0, *w1),
        grid=(te // rows,),
        in_specs=[SMEM, block] + [half] * 4 + [whole(a.shape) for a in (*w0, *w1)],
        out_specs=(block,) + (whole((c, d)),) * 4,
        scratch=[pltpu.VMEM((4, c, d), f32)],
        vmem=BIG_VMEM,
        name="enc_grad",
    )


def self_bwd_kernel(x_ref, x1_ref, gx2_ref, gn2_ref, g_ref, n1_ref, *rest):
    weights = rest[0:4]
    sides = (rest[4:10], rest[10:16])
    outs = rest[16:20]
    gd_ref, gg2_ref, gg1_ref, gi_ref, gat_ref, gqt_ref, gk_ref, gv_ref, gx1_ref = rest[20:]
    w = outs[0].shape[0] // 4
    c = 2 * w
    nb = n1_ref.shape[0] // LEN
    gx, gg2 = norm_back(x1_ref[...], g_ref[1:2].astype(f32), gn2_ref[...])
    gx1 = gx2_ref[...] + gx
    gx1_ref[...] = gx1
    gg2_ref[...] = gg2
    go = gx1.astype(bf16)
    ri = lax.broadcasted_iota(jnp.int32, (LEN, LEN), 0)
    ci = lax.broadcasted_iota(jnp.int32, (LEN, LEN), 1)
    flip = jnp.where(ri + ci == LEN - 1, 1.0, 0.0).astype(bf16)
    n1 = n1_ref[...]
    gn = None
    for side in (1, 0):
        shards = weights[2 * side : 2 * side + 2]
        q_ref, k_ref, vt_ref, e_ref, r_ref, at_ref = sides[side]
        gat_ref[...] = nt(side_by_side(shards, 3), go).astype(bf16)
        gwo = nn(at_ref[...], go).astype(bf16)
        for p in range(c // (2 * DH)):
            lanes = slice(p * 2 * DH, (p + 1) * 2 * DH)
            for h in range(2):
                head = side * (c // DH) + 2 * p + h
                gd_ref[head : head + 1, :] = jnp.zeros((1, LEN), f32)
            for b in range(nb):
                tok = slice(b * LEN, (b + 1) * LEN)

                def extra(h, gs):
                    turned = pltpu.roll(nn(gs, flip), 0, 1, stride=1, stride_axis=0)
                    head = side * (c // DH) + 2 * p + h
                    gd_ref[head : head + 1, :] += jnp.sum(turned, axis=0, keepdims=True)

                gq, gk, gv = head_pair_back(
                    k_ref[tok, lanes].T, vt_ref[lanes, tok].T, q_ref[tok, lanes], None, gat_ref[lanes, tok], at_ref[lanes, tok],
                    [e_ref[b, 2 * p], e_ref[b, 2 * p + 1]],
                    [r_ref[b, 2 * p : 2 * p + 1, :], r_ref[b, 2 * p + 1 : 2 * p + 2, :]],
                    extra,
                )
                gqt_ref[lanes, tok] = gq
                gk_ref[tok, lanes] = gk
                gv_ref[tok, lanes] = gv
        gqt = gqt_ref[...]
        gk = gk_ref[...]
        gv = gv_ref[...]
        gwq = nn(gqt, n1).astype(bf16)
        gwk = tn(gk, n1).astype(bf16)
        gwv = tn(gv, n1).astype(bf16)
        for i, gw in enumerate((gwq, gwk, gwv, gwo)):
            for j in range(2):
                outs[2 * side + j][i * w : (i + 1) * w] = gw[j * w : (j + 1) * w]
        part = tn(gqt, side_by_side(shards, 0)) + nn(gk, side_by_side(shards, 1)) + nn(gv, side_by_side(shards, 2))
        gn = part if gn is None else gn + part
    gi, gg1 = norm_back(x_ref[...].astype(f32), g_ref[0:1].astype(f32), gn)
    gi_ref[...] = gx1_ref[...] + gi
    gg1_ref[...] = gg1


def self_bwd(x, x1, gx2, gn2, g, n1, weights, side0, side1):
    t, d = x1.shape
    c = weights[0].shape[0] // 2
    args = [x, x1, gx2, gn2, g, n1, *weights, *side0, *side1]
    outs = [jax.ShapeDtypeStruct((2 * c, d), bf16)] * 4 + [
        jax.ShapeDtypeStruct((2 * c // DH, LEN), f32),
        jax.ShapeDtypeStruct((1, d), f32),
        jax.ShapeDtypeStruct((1, d), f32),
        jax.ShapeDtypeStruct((t, d), f32),
    ]
    return call(
        self_bwd_kernel,
        tuple(outs),
        args,
        in_specs=[whole(a.shape) for a in args],
        out_specs=tuple(whole(o.shape) for o in outs),
        scratch=[
            pltpu.VMEM((c, t), bf16),
            pltpu.VMEM((c, t), bf16),
            pltpu.VMEM((t, c), bf16),
            pltpu.VMEM((t, c), bf16),
            pltpu.VMEM((t, d), f32),
        ],
        vmem=BIG_VMEM,
        name="self_bwd",
    )


def local_program(tensor_size, dp_size, *arrays):
    (block_in, enc_states, dec_len, enc_len, gain_self, self_query, self_key, self_value, self_out, rel_table,
     gain_cross, cross_query, cross_key, cross_value, cross_out, gain_ff, ff_in, ff_out, out_grad) = arrays
    t_index = lax.axis_index("tensor")
    d_index = lax.axis_index("dp")
    nb = block_in.shape[0] // LEN
    w, d = self_out.shape
    heads = w // DH

    def swap(v, axis, bit):
        n = tensor_size if axis == "tensor" else dp_size
        return lax.ppermute(v, axis, [(i, i ^ bit) for i in range(n)])

    def d_bit(bit):
        return (d_index // bit) % 2

    y = d_bit(1).astype(jnp.int32)
    y_is0 = y == 0
    place = jnp.stack([y, (t_index * nb).astype(jnp.int32)])

    def core(v):
        return swap(v, "tensor", 1)

    def over_x(v):
        return swap(v, "tensor", 2)

    def over_y(v):
        return swap(v, "dp", 1)

    def fence(*vals):
        return lax.optimization_barrier(vals)

    gains = jnp.stack([gain_self, gain_cross, gain_ff])

    buckets = np.eye(BUCKETS, dtype=np.float32)[bucket_of_distance()]
    rel_own = jnp.dot(rel_table.astype(f32).T, jnp.asarray(buckets.T), precision=lax.Precision.HIGHEST)
    rel_x = over_x(rel_own)
    own_s = jnp.concatenate([self_query.T, self_key.T, self_value.T, self_out], axis=0)
    own_s, rel_own = fence(own_s, rel_own)
    x_s = over_x(own_s)
    s_0 = [own_s, core(own_s)]
    bias0 = jnp.concatenate([rel_own, core(rel_own)], axis=0)
    own_c = jnp.concatenate([cross_key.T, cross_value.T, cross_query.T, cross_out], axis=0)
    c_0 = [own_c, core(own_c)]
    out = self_fwd(False, place, dec_len, block_in, gains, s_0, bias0)
    *out, c_0[1] = fence(*out, c_0[1])
    fq0, fk0, fv0, fe0, fr0, fa0, xp = out
    k0, v0 = enc_kv(False, place, enc_states, c_0)
    k0, v0, xp, x_s, rel_x = fence(k0, v0, xp, x_s, rel_x)
    s_1 = [x_s, core(x_s)]
    bias1 = jnp.concatenate([rel_x, core(rel_x)], axis=0)
    half = own_c.shape[0] // 2
    send_c, x_s = fence(jnp.where(y_is0, own_c[:half], own_c[half:]), x_s)
    x_c = over_x(send_c)
    out = self_fwd(True, place, dec_len, block_in, gains, s_1, bias1, xp)
    *out, x_c = fence(*out, x_c)
    fq1, fk1, fv1, fe1, fr1, fa1, x1, n1, n2 = out
    send_f, x_c = fence(jnp.where(y_is0, ff_in, ff_out), x_c)
    x_f = over_x(send_f)
    y_c, c_c = over_y(x_c), core(x_c)
    cq0, cr0, ca0, x2p = cross_fwd(False, place, enc_len, n2, gains, c_0, k0, v0, x1)
    x2p, y_c, c_c = fence(x2p, y_c, c_c)
    c_1 = [x_c, y_c, c_c, core(y_c)]
    wi1, wo1 = core(ff_in), core(ff_out)
    k1, v1 = enc_kv(True, place, enc_states, c_1)
    k1, v1, x_f = fence(k1, v1, x_f)
    y_f, c_f = over_y(x_f), core(x_f)
    cq1, cr1, ca1, x2, n3 = cross_fwd(True, place, enc_len, n2, gains, c_1, k1, v1, x2p)
    n3, x2, wi1, wo1, c_f = fence(n3, x2, wi1, wo1, c_f)

    rest_size = dp_size // 2
    m = d_index // 2
    rest_groups = [[2 * i + j for i in range(rest_size)] for j in range(2)]

    def plus(*vals):
        total = vals[0].astype(f32)
        for v in vals[1:]:
            total = total + v.astype(f32)
        return total.astype(bf16)

    def pick(v, n, i):
        v = v.reshape((n, v.shape[0] // n) + v.shape[1:])
        return lax.dynamic_index_in_dim(v, i, 0, keepdims=False)

    def ordered(a, b):
        return jnp.where(y_is0, jnp.concatenate([a, b], axis=0), jnp.concatenate([b, a], axis=0))

    def sent_y(*vals):
        return over_y(plus(*[pick(v, 2, 1 - y) for v in vals]))

    def kept_y(*vals):
        return [pick(v, 2, y) for v in vals]

    def sum_ordered(parts):
        while len(parts) > 1:
            parts = [a + b for a, b in zip(parts[0::2], parts[1::2])]
        return parts[0]

    def stage_z(v):
        return [pick(v, rest_size, m)] + [swap(pick(v, rest_size, m ^ j), "dp", 2 * j) for j in range(1, rest_size)]

    def stage_z_back(v):
        return [v] + [swap(v, "dp", 2 * j) for j in range(1, rest_size)]

    def ordered_z(parts):
        bit = 1
        while len(parts) > 1:
            low = (m // bit) % 2 == 0
            parts = [
                jnp.where(low, jnp.concatenate([a, b], axis=0), jnp.concatenate([b, a], axis=0))
                for a, b in zip(parts[0::2], parts[1::2])
            ]
            bit *= 2
        return parts[0]

    gwi0, gwo0, gwi1, gwo1, yp, gp = ff(False, place, n3, out_grad, [ff_in, ff_out, wi1, wo1])
    yp, y_f = fence(yp, y_f)
    a1, b1 = core(gwo1), core(gwi1)
    f_1 = [x_f, y_f, c_f, core(y_f)]
    out = ff(True, place, n3, out_grad, f_1, yp, gp, x2, gains)
    *out, a1, b1 = fence(*out, a1, b1)
    gwi2, gwo2, gwi3, gwo3, block_out, gx2, go2, gg3 = out
    a3, b3 = core(gwo3), core(gwi3)
    a3, b3, go2 = fence(a3, b3, go2)
    wo_s = plus(gwo2, a3)
    wi_send = jnp.concatenate(
        [plus(pick(gwi0, 2, 1 - y), pick(b1, 2, 1 - y)), plus(pick(gwi2, 2, 1 - y), pick(b3, 2, 1 - y))], axis=0
    )
    wo_s, wi_send, go2 = fence(wo_s, wi_send, go2)
    xo = over_x(wo_s)
    ywi = over_y(wi_send)
    out = cross_bwd(place, enc_len, go2, n2, c_0, c_1, (cq0, k0, v0, cr0, ca0), (cq1, k1, v1, cr1, ca1))
    *out, xo, ywi = fence(*out, xo, ywi)
    gk0, gv0, gk1, gv1, gqo0, gqo1, gqo2, gqo3, gn2 = out
    c3 = core(gqo3)
    hid = gwi0.shape[0] // 2
    wi_x = plus(pick(gwi2, 2, y), pick(b3, 2, y), ywi[hid:])
    wo_y = plus(*[pick(v, 2, 1 - y) for v in (gwo0, a1, xo)])
    wi_x, wo_y, c3, gn2 = fence(wi_x, wo_y, c3, gn2)
    wq_x = jnp.concatenate([wi_x, plus(gqo2, c3)], axis=0)
    wq_x, gn2 = fence(wq_x, gn2)
    xwq, ywo = over_x(wq_x), over_y(wo_y)
    out = self_bwd(
        block_in, x1, gx2, gn2, gains, n1, [*s_0, *s_1], (fq0, fk0, fv0, fe0, fr0, fa0), (fq1, fk1, fv1, fe1, fr1, fa1)
    )
    *out, xwq, ywo = fence(*out, xwq, ywo)
    gs0, gs1, gs2, gs3, gd, gg2, gg1, grad_in = out
    s3, c1 = core(gs3), core(gqo1)
    flipped = jnp.asarray(np.ascontiguousarray(buckets[::-1]))
    grel = jnp.dot(gd, flipped, precision=lax.Precision.HIGHEST)
    grel = grel.reshape(tensor_size, heads * BUCKETS)
    slots = jnp.arange(tensor_size)[:, None] ^ t_index
    order = (slots == jnp.arange(tensor_size)[None, :]).astype(f32)
    grel = jnp.dot(order.T, grel, precision=lax.Precision.HIGHEST)
    grel = jnp.pad(grel.reshape(1, -1), ((0, 0), (0, d - grel.size)))
    small = jnp.concatenate([gg1, gg2, gg3, grel], axis=0)
    small_got = core(small)
    xwi, xqo = xwq[:hid], xwq[hid:]
    f_u = jnp.concatenate(
        [plus(*kept_y(gwo0, a1, xo), ywo), plus(*kept_y(gwi0, b1), ywi[:hid], xwi)], axis=0
    )
    s3, c1, f_u, gk0 = fence(s3, c1, f_u, gk0)
    s_x = plus(gs2, s3)
    s_x, gk0 = fence(s_x, gk0)
    xs = over_x(s_x)
    s1 = core(gs1)
    zf = stage_z(f_u)
    grad_enc, gkv2, gkv3, gkv0, gkv1 = enc_grad(place, enc_states, gk1, gv1, gk0, gv0, c_0, c_1)
    gkv3, s1, small_got, *zf = fence(gkv3, s1, small_got, *zf)
    f_w = plus(*zf)
    bf = stage_z_back(f_w)
    k3, k1 = core(gkv3), core(gkv1)
    xs, f_w = fence(xs, f_w)
    small = small + small_got
    small_got = over_y(small)
    ys = sent_y(gs0, s1, xs)
    k3, small = fence(k3, small)
    xkv = over_x(plus(gkv2, k3))
    ys, xkv, k1, small_got = fence(ys, xkv, k1, small_got)
    zs = stage_z(plus(*kept_y(gs0, s1, xs), ys))
    qo_t, kv_t = (gqo0, c1, xqo), (gkv0, k1, xkv)
    yc = over_y(plus(*[jnp.where(y_is0, b_, a_) for a_, b_ in zip(qo_t, kv_t)]))
    small = small + small_got
    small_got = over_x(small)
    yc, small_got, *both = fence(yc, small_got, *zs, *bf)
    zs, bf = both[:rest_size], both[rest_size:]
    bs = stage_z_back(plus(*zs))
    zc = stage_z(plus(*[jnp.where(y_is0, a_, b_) for a_, b_ in zip(qo_t, kv_t)], yc))
    f_v = ordered_z(bf)
    f_f = over_y(f_v)
    small = small + small_got
    small_z = [small, *[swap(small, "dp", 2 * j) for j in range(1, rest_size)]]
    both = fence(*zc, *bs, *small_z)
    zc, bs, small_z = both[:rest_size], both[rest_size : 2 * rest_size], both[2 * rest_size :]
    bc = stage_z_back(plus(*zc))
    s_v = ordered_z(bs)
    s_f = over_y(s_v)
    small = sum_ordered(small_z)
    n_f = f_v.shape[0] // 2
    r_wo = ordered(f_v[:n_f], f_f[:n_f]).astype(f32)
    r_wi = ordered(f_v[n_f:], f_f[n_f:]).astype(f32)
    s_f, r_wo, r_wi, *bc = fence(s_f, r_wo, r_wi, *bc)
    c_v = ordered_z(bc)
    c_f = over_y(c_v)
    r_s = ordered(s_v, s_f)
    g_s = [r_s[i * w : (i + 1) * w].astype(f32) for i in range(4)]
    c_f, *g_s = fence(c_f, *g_s)
    c_w = [jnp.where(y_is0, a_, b_) for a_, b_ in ((c_v, c_f), (c_f, c_v))]
    g_c = [v[i * w : (i + 1) * w].astype(f32) for v in c_w for i in range(2)]
    grad_rel = lax.dynamic_slice(small[3], (t_index * heads * BUCKETS,), (heads * BUCKETS,)).reshape(heads, BUCKETS).T

    return (
        block_out,
        grad_in,
        grad_enc,
        small[0],
        g_s[0].T,
        g_s[1].T,
        g_s[2].T,
        g_s[3],
        grad_rel,
        small[1],
        g_c[0].T,
        g_c[2].T,
        g_c[3].T,
        g_c[1],
        small[2],
        r_wi,
        r_wo,
    )


def solution(mesh):
    tensor_size = mesh.shape["tensor"]
    dp_size = mesh.shape["dp"]
    both = P(("dp", "tensor"), None)
    col = P(None, "tensor")
    row = P("tensor", None)
    placed = (both, both, P("dp"), P("dp"), P(), col, col, col, row, col, P(), col, col, col, row, P(), col, row, both)
    outs = (both, both, both, P(), col, col, col, row, col, P(), col, col, col, row, P(), col, row)
    return jax.shard_map(
        lambda *a: local_program(tensor_size, dp_size, *a),
        mesh=mesh,
        in_specs=placed,
        out_specs=outs,
        check_vma=False,
    )
```

```python
import math

import jax
import jax.numpy as jnp
import numpy as np
from jax import lax
from jax.experimental import pallas as pl
from jax.experimental.pallas import tpu as pltpu
from jax.sharding import PartitionSpec as P

BUCKETS = 32
MAX_DIST = 128
LEN = 256
ENC = 1024
DH = 64
KEYS = 256

norm_eps = 1e-06
masked_score = -1000000000.0
bf16 = jnp.bfloat16
f32 = jnp.float32
VMEM_CAP = 16 << 20
BIG_VMEM = 58 << 20


def bucket_of_distance():
    half_count = BUCKETS // 2
    growth_ratio = MAX_DIST / half_count
    limits = np.array(
        [int(math.ceil(half_count * growth_ratio ** (m / half_count))) for m in range(1, half_count)],
        dtype=np.int32,
    )
    distance = np.arange(LEN, dtype=np.int32)
    above = np.sum(distance[:, None] >= limits[None, :], axis=1)
    return np.where(distance < half_count, distance, half_count + above).astype(np.int32)


def nn(a, b):
    return lax.dot_general(a, b, (((1,), (0,)), ((), ())), preferred_element_type=f32)


def nt(a, b):
    return lax.dot_general(a, b, (((1,), (1,)), ((), ())), preferred_element_type=f32)


def tn(a, b):
    return lax.dot_general(a, b, (((0,), (0,)), ((), ())), preferred_element_type=f32)


def inv_rms(v):
    return lax.rsqrt(jnp.mean(v * v, axis=-1, keepdims=True) + norm_eps)


def normed(v, gain):
    return (v * inv_rms(v) * gain).astype(bf16)


def norm_back(v, gain, e):
    s = inv_rms(v)
    ge = gain * e
    dot = jnp.mean(ge * v, axis=-1, keepdims=True)
    grad_v = s * ge - v * (s * s * s * dot)
    grad_gain = jnp.sum(e * v * s, axis=0, keepdims=True)
    return grad_v, grad_gain


def lane_half(shape, h):
    lane = lax.broadcasted_iota(jnp.int32, shape, 1)
    return (lane < DH) if h == 0 else (lane >= DH)


def both_heads(rows):
    zero = jnp.zeros_like(rows)
    return jnp.concatenate([jnp.where(lane_half(rows.shape, h), rows, zero) for h in range(2)], axis=0)


def call(kernel, out_shape, args, *, grid=(), in_specs=None, out_specs=None, scratch=(), flops=0, nbytes=0, trans=0, name=None, vmem=VMEM_CAP):
    kw = {}
    if in_specs is not None:
        kw["in_specs"] = in_specs
    if out_specs is not None:
        kw["out_specs"] = out_specs
    return pl.pallas_call(
        kernel,
        out_shape=out_shape,
        grid=grid,
        scratch_shapes=scratch,
        compiler_params=pltpu.CompilerParams(vmem_limit_bytes=vmem),
        cost_estimate=pl.CostEstimate(flops=1, bytes_accessed=1, transcendentals=0),
        name=name,
        **kw,
    )(*args)


def whole(shape):
    return pl.BlockSpec(shape, lambda *_: (0,) * len(shape))


SMEM = pl.BlockSpec(memory_space=pltpu.SMEM)


def side_by_side(refs, i):
    w = refs[0].shape[0] // 4
    return jnp.concatenate([r[i * w : (i + 1) * w] for r in refs], axis=0)


def pair_rows(y_ref, refs, shared):
    def rows(i):
        if not shared:
            return side_by_side(refs, i)
        w = refs[0].shape[0] // 2
        first = y_ref[0] == i // 2
        part = slice((i % 2) * w, (i % 2 + 1) * w)
        return jnp.concatenate(
            [jnp.where(first, refs[0][part], refs[1][part]), jnp.where(first, refs[2][part], refs[3][part])], axis=0
        )

    return rows


def self_fwd_kernel(last, y_ref, len_ref, x_ref, g_ref, *rest):
    weights = rest[0:2]
    bias_ref = rest[2]
    rest = rest[3:]
    if last:
        xin_ref, q_ref, k_ref, vt_ref, e_ref, r_ref, at_ref, x1_ref, n1_ref, n2_ref, bs_ref = rest
    else:
        q_ref, k_ref, vt_ref, e_ref, r_ref, at_ref, x1_ref, bs_ref = rest
    nh = q_ref.shape[1] // DH
    nb = x_ref.shape[0] // LEN
    x = x_ref[...].astype(f32)
    n1 = normed(x, g_ref[0:1].astype(f32))
    if last:
        n1_ref[...] = n1

    q_ref[...] = nt(n1, side_by_side(weights, 0)).astype(bf16)
    k_ref[...] = nt(n1, side_by_side(weights, 1)).astype(bf16)
    vt_ref[...] = nt(side_by_side(weights, 2), n1).astype(bf16)
    key = lax.broadcasted_iota(jnp.int32, (LEN, LEN), 0)
    query = lax.broadcasted_iota(jnp.int32, (LEN, LEN), 1)
    for p in range(nh // 2):
        lanes = slice(p * 2 * DH, (p + 1) * 2 * DH)
        for h in range(2):
            row = jnp.broadcast_to(bias_ref[2 * p + h : 2 * p + h + 1, :], (LEN, LEN))
            bs_ref[h] = pltpu.roll(row, 0, 1, stride=1, stride_axis=0)
        for b in range(nb):
            tok = slice(b * LEN, (b + 1) * LEN)
            allowed = (key <= query) & (key < len_ref[y_ref[1] + b])
            kp = k_ref[tok, lanes]
            qp = q_ref[tok, lanes]
            outs = []
            for h in range(2):
                head = 2 * p + h
                qh = jnp.where(lane_half(qp.shape, h), qp, jnp.zeros_like(qp))
                s = nt(kp, qh) + bs_ref[h]
                s = jnp.where(allowed, s, masked_score)
                top = jnp.max(s, axis=0, keepdims=True)
                e = jnp.exp(s - top)
                r = 1.0 / jnp.sum(e, axis=0, keepdims=True)
                eb = e.astype(bf16)
                e_ref[b, head] = eb
                r_ref[b, head : head + 1, :] = r
                outs.append(nn(vt_ref[head * DH : (head + 1) * DH, tok], eb) * r)
            at_ref[lanes, tok] = jnp.concatenate(outs, axis=0).astype(bf16)
    mixed = tn(at_ref[...], side_by_side(weights, 3))
    if last:
        x1 = xin_ref[...] + mixed
        n2_ref[...] = normed(x1, g_ref[1:2].astype(f32))
    else:
        x1 = x + mixed
    x1_ref[...] = x1


def self_fwd(last, y, lens, x, g, weights, bias, xin=None):
    t, d = x.shape
    w = weights[0].shape[0] // 4
    c = 2 * w
    nh = c // DH
    nb = t // LEN
    outs = [
        jax.ShapeDtypeStruct((t, c), bf16),
        jax.ShapeDtypeStruct((t, c), bf16),
        jax.ShapeDtypeStruct((c, t), bf16),
        jax.ShapeDtypeStruct((nb, nh, LEN, LEN), bf16),
        jax.ShapeDtypeStruct((nb, nh, LEN), f32),
        jax.ShapeDtypeStruct((c, t), bf16),
        jax.ShapeDtypeStruct((t, d), f32),
    ]
    args = [y, lens, x, g, *weights, bias]
    if last:
        args.append(xin)
        outs += [jax.ShapeDtypeStruct((t, d), bf16)] * 2
    flops = 2 * t * d * c * 4 + 2 * t * LEN * nh * 128 * 2
    return call(
        lambda *r: self_fwd_kernel(last, *r),
        tuple(outs),
        args,
        in_specs=[SMEM, SMEM] + [whole(a.shape) for a in args[2:]],
        out_specs=tuple(whole(o.shape) for o in outs),
        scratch=[pltpu.VMEM((2, LEN, LEN), f32)],
        flops=flops * 3,
        nbytes=12 * 1024 * 1024,
        trans=t * LEN * nh,
        name="self_fwd",
    )


def enc_kv_kernel(shared, y_ref, enc_ref, *rest):
    k_ref, v_ref = rest[-2:]
    enc = enc_ref[...]
    rows = pair_rows(y_ref, rest[:-2], shared)
    k_ref[...] = nt(enc, rows(0)).astype(bf16)
    v_ref[...] = nt(enc, rows(1)).astype(bf16)


def enc_kv(shared, y, enc, kv):
    t, d = enc.shape
    c = kv[0].shape[0] if shared else kv[0].shape[0] // 2
    rows = 512
    half = pl.BlockSpec((rows, c), lambda i: (i, 0))
    return call(
        lambda *r: enc_kv_kernel(shared, *r),
        (jax.ShapeDtypeStruct((t, c), bf16),) * 2,
        (y, enc, *kv),
        grid=(t // rows,),
        in_specs=[SMEM, pl.BlockSpec((rows, d), lambda i: (i, 0))] + [whole(a.shape) for a in kv],
        out_specs=(half, half),
        flops=2 * t * d * c * 2 * 2,
        nbytes=t * d * 2 + 4 * t * c * 2,
        name="enc_kv",
    )


def cross_fwd_kernel(last, pairs, y_ref, len_ref, n2_ref, g_ref, *rest):
    n_w = 4 if last else 2
    weights = pair_rows(y_ref, rest[:n_w], last)
    k_ref, v_ref, xin_ref = rest[n_w : n_w + 3]
    rest = rest[n_w + 3 :]
    if last:
        q_ref, r_ref, at_ref, x2_ref, n3_ref, s_ref, e_ref = rest
    else:
        q_ref, r_ref, at_ref, x2_ref, s_ref, e_ref = rest
    step = pl.program_id(0)
    b = step // pairs
    p = lax.rem(step, pairs)

    @pl.when(step == 0)
    def _():
        q_ref[...] = nt(n2_ref[...], weights(2)).astype(bf16)

    tok = pl.ds(pl.multiple_of(b * LEN, LEN), LEN)
    lanes = pl.ds(pl.multiple_of(p * 2 * DH, 2 * DH), 2 * DH)
    qp = q_ref[tok, lanes]
    count = len_ref[y_ref[1] + b]
    key = lax.broadcasted_iota(jnp.int32, (KEYS, 2 * LEN), 0)
    queries = both_heads(qp)
    top = None
    for c in range(ENC // KEYS):
        part = slice(c * KEYS, (c + 1) * KEYS)
        s = jnp.where(key < count - c * KEYS, nt(k_ref[part], queries), masked_score)
        s_ref[part] = s
        t = jnp.max(s.reshape(KEYS // 8, 8, 2 * LEN), axis=0)
        top = t if c == 0 else jnp.maximum(top, t)
    top = jnp.max(top, axis=0, keepdims=True)
    total = None
    for c in range(ENC // KEYS):
        part = slice(c * KEYS, (c + 1) * KEYS)
        e = jnp.exp(s_ref[part] - top)
        t = jnp.sum(e.reshape(KEYS // 8, 8, 2 * LEN), axis=0)
        total = t if c == 0 else total + t
        e_ref[part] = e.astype(bf16)
    r = 1.0 / jnp.sum(total, axis=0, keepdims=True)
    mixed = tn(v_ref[...], e_ref[...]) * r
    outs = []
    for h in range(2):
        half = slice(h * LEN, (h + 1) * LEN)
        r_ref[0, h : h + 1, :] = r[:, half]
        r_ref[0, 2 + h : 3 + h, :] = top[:, half]
        outs.append(mixed[h * DH : (h + 1) * DH, half])
    at_ref[lanes, tok] = jnp.concatenate(outs, axis=0).astype(bf16)

    @pl.when(step == pl.num_programs(0) - 1)
    def _():
        x2 = xin_ref[...] + tn(at_ref[...], weights(3))
        x2_ref[...] = x2
        if last:
            n3_ref[...] = normed(x2, g_ref[2:3].astype(f32))


def cross_fwd(last, y, lens, n2, g, qo, k, v, xin):
    t, d = n2.shape
    c = k.shape[1]
    nb = t // LEN
    pairs = c // (2 * DH)
    outs = [
        jax.ShapeDtypeStruct((t, c), bf16),
        jax.ShapeDtypeStruct((nb * pairs, 4, LEN), f32),
        jax.ShapeDtypeStruct((c, t), bf16),
        jax.ShapeDtypeStruct((t, d), f32),
    ]
    specs = [
        whole((t, c)),
        pl.BlockSpec((1, 4, LEN), lambda i: (i, 0, 0)),
        whole((c, t)),
        whole((t, d)),
    ]
    if last:
        outs.append(jax.ShapeDtypeStruct((t, d), bf16))
        specs.append(whole((t, d)))
    return call(
        lambda *r: cross_fwd_kernel(last, pairs, *r),
        tuple(outs),
        (y, lens, n2, g, *qo, k, v, xin),
        grid=(nb * pairs,),
        in_specs=[
            SMEM,
            SMEM,
            whole(n2.shape),
            whole(g.shape),
            *[whole(a.shape) for a in qo],
            pl.BlockSpec((ENC, 2 * DH), lambda i: (i // pairs, i % pairs)),
            pl.BlockSpec((ENC, 2 * DH), lambda i: (i // pairs, i % pairs)),
            whole(xin.shape),
        ],
        out_specs=tuple(specs),
        scratch=[pltpu.VMEM((ENC, 2 * LEN), f32), pltpu.VMEM((ENC, 2 * LEN), bf16)],
        flops=3 * (2 * t * d * c * 2 + 2 * t * ENC * c * 2 * 2),
        nbytes=14 * 1024 * 1024,
        trans=t * ENC * (c // DH),
        name="cross_fwd",
    )


ROOT = math.sqrt(2.0 / math.pi)
CUBE = 0.044715


def ff_kernel(last, y_ref, n3_ref, gf_ref, *rest):
    if last:
        ha_in, ha_out, ga_in, ga_out, hb_in, hb_out, gb_in, gb_out = rest[:8]
        rest = rest[8:]
        first = y_ref[0] == 0

        def weights(h_in, h_out, g_in, g_out):
            return (
                lambda: jnp.where(first, h_in[...], g_in[...]),
                lambda: jnp.where(first, g_out[...], h_out[...]),
            )

        shards = (weights(ha_in, ha_out, ga_in, ga_out), weights(hb_in, hb_out, gb_in, gb_out))
    else:
        wia_ref, woa_ref, wib_ref, wob_ref = rest[:4]
        rest = rest[4:]
        shards = ((lambda: wia_ref[...], lambda: woa_ref[...]), (lambda: wib_ref[...], lambda: wob_ref[...]))
    if last:
        yin_ref, gin_ref, x2_ref, g_ref = rest[:4]
        gwia, gwoa, gwib, gwob, out_ref, gx2_ref, go2_ref, gg_ref, y_acc, gn_ref, n3t_ref = rest[4:]
    else:
        gwia, gwoa, gwib, gwob, y_acc, gn_ref, n3t_ref = rest
    step = pl.program_id(0)

    @pl.when(step == 0)
    def _():
        n3t_ref[...] = n3_ref[...].T
        if last:
            y_acc[...] = yin_ref[...]
            gn_ref[...] = gin_ref[...]
        else:
            y_acc[...] = jnp.zeros_like(y_acc)
            gn_ref[...] = jnp.zeros_like(gn_ref)

    n3 = n3_ref[...]
    gf = gf_ref[...]
    kept = []
    for (get_wi, get_wo), gwi, gwo in zip(shards, (gwia, gwib), (gwoa, gwob)):
        wi, wo = get_wi(), get_wo()
        u = nn(n3, wi)
        dh = nt(gf, wo)
        u2 = u * u
        th = jnp.tanh(ROOT * u * (1.0 + CUBE * u2))
        half = 0.5 * (1.0 + th)
        r = (u * half).astype(bf16)
        slope = half + 0.5 * u * (1.0 - th * th) * (ROOT * (1.0 + (3.0 * CUBE) * u2))
        gu = (dh * slope).astype(bf16)
        kept.append((r, wo, gu, wi))
        gwo[...] = tn(r, gf).astype(bf16)
        gwi[...] = nn(n3t_ref[...], gu).astype(bf16)
    r, wo, gu, wi = [jnp.concatenate(v, axis=a) for v, a in zip(zip(*kept), (1, 0, 1, 1))]
    y_acc[...] += nn(r, wo)
    gn_ref[...] += nt(gu, wi)

    if last:

        @pl.when(step == pl.num_programs(0) - 1)
        def _():
            x2 = x2_ref[...]
            out_ref[...] = (x2 + y_acc[...]).astype(bf16)
            gx, gg = norm_back(x2, g_ref[2:3].astype(f32), gn_ref[...])
            gx2 = gf.astype(f32) + gx
            gx2_ref[...] = gx2
            go2_ref[...] = gx2.astype(bf16)
            gg_ref[...] = gg


def ff(last, y, n3, gf, weights, yin=None, gin=None, x2=None, g=None):
    t, d = n3.shape
    hid = weights[0].shape[1]
    blk = 256
    args = [y, n3, gf]
    col = pl.BlockSpec((d, blk), lambda i: (0, i))
    row = pl.BlockSpec((blk, d), lambda i: (i, 0))
    in_specs = [SMEM, whole((t, d)), whole((t, d))]
    if last:
        for v in weights:
            args += [v, v]
            in_specs += [col, row]
    else:
        args += weights
        in_specs += [col, row, col, row]
    outs = [jax.ShapeDtypeStruct((d, hid), bf16), jax.ShapeDtypeStruct((hid, d), bf16)] * 2
    specs = [col, row, col, row]
    acc = jax.ShapeDtypeStruct((t, d), f32)
    scratch = [pltpu.VMEM((d, t), bf16)]
    if last:
        args += [yin, gin, x2, g]
        in_specs += [whole((t, d))] * 3 + [whole(g.shape)]
        outs += [jax.ShapeDtypeStruct((t, d), bf16), acc, jax.ShapeDtypeStruct((t, d), bf16), jax.ShapeDtypeStruct((1, d), f32)]
        specs += [whole((t, d))] * 3 + [whole((1, d))]
        scratch = [pltpu.VMEM((t, d), f32)] * 2 + scratch
    else:
        outs += [acc, acc]
        specs += [whole((t, d))] * 2
    return call(
        lambda *r: ff_kernel(last, *r),
        tuple(outs),
        args,
        grid=(hid // blk,),
        in_specs=in_specs,
        out_specs=tuple(specs),
        scratch=scratch,
        flops=2 * 6 * 2 * t * d * hid * 2,
        nbytes=12 * 1024 * 1024,
        trans=2 * t * hid,
        vmem=20 << 20,
        name="ff",
    )


def head_pair_back(k_t, v, q, ga, ga_t, a_t, es, rs, extra=None):
    gv = None
    gk = None
    gq_t = []
    for h in range(2):
        part = slice(h * DH, (h + 1) * DH)
        r = rs[h]
        gah = ga_t[part].astype(f32) * r
        delta = jnp.sum(gah * a_t[part].astype(f32), axis=0, keepdims=True)
        gah = gah.astype(bf16)
        zero = jnp.zeros_like(gah)
        rhs = jnp.concatenate([gah, zero] if h == 0 else [zero, gah], axis=0)
        gp = nn(v, rhs)
        e = es[h]
        gs = (e.astype(f32) * (gp - delta)).astype(bf16)
        if extra is not None:
            extra(h, gs)
        keep = lane_half(q.shape, h)
        term_v = nt(e, rhs)
        term_k = nn(gs, jnp.where(keep, q, jnp.zeros_like(q)))
        gv = term_v if gv is None else gv + term_v
        gk = term_k if gk is None else gk + term_k
        gq_t.append(nn(k_t[part], gs))
    return jnp.concatenate(gq_t, axis=0).astype(bf16), gk.astype(bf16), gv.astype(bf16)


def cross_bwd_kernel(pairs, steps, y_ref, len_ref, go_ref, n2_ref, *rest):
    weights = (pair_rows(y_ref, rest[0:2], False), pair_rows(y_ref, rest[2:6], True))
    sides = (rest[6:11], rest[11:16])
    gk0, gv0, gk1, gv1, outs, gn_ref, gat_ref, gqt_ref, e_ref, gs_ref = *rest[16:20], rest[20:24], *rest[24:]
    w = outs[0].shape[0] // 2
    step = pl.program_id(0)
    key = lax.broadcasted_iota(jnp.int32, (KEYS, 2 * LEN), 0)

    def half(side, local, gk_ref, gv_ref):
        q_ref, k_ref, v_ref, r_ref, at_ref = sides[side]
        b = local // pairs
        p = lax.rem(local, pairs)

        @pl.when(local == 0)
        def _():
            gat_ref[...] = nt(weights[side](3), go_ref[...]).astype(bf16)

        tok = pl.ds(pl.multiple_of(b * LEN, LEN), LEN)
        lanes = pl.ds(pl.multiple_of(p * 2 * DH, 2 * DH), 2 * DH)
        qp = q_ref[tok, lanes]
        ga_t = gat_ref[lanes, tok]
        a_t = at_ref[lanes, tok]
        count = len_ref[y_ref[1] + b]
        grads, deltas = [], []
        for h in range(2):
            part = slice(h * DH, (h + 1) * DH)
            gah = ga_t[part].astype(f32) * r_ref[0, h : h + 1, :]
            deltas.append(jnp.sum(gah * a_t[part].astype(f32), axis=0, keepdims=True))
            gah = gah.astype(bf16)
            zero = jnp.zeros_like(gah)
            grads.append(jnp.concatenate([gah, zero] if h == 0 else [zero, gah], axis=0))
        grads = jnp.concatenate(grads, axis=1)
        delta = jnp.concatenate(deltas, axis=1)
        top = jnp.concatenate([r_ref[0, 2:3, :], r_ref[0, 3:4, :]], axis=1)
        queries = both_heads(qp)
        for c in range(ENC // KEYS):
            part = slice(c * KEYS, (c + 1) * KEYS)
            s = jnp.where(key < count - c * KEYS, nt(k_ref[part], queries), masked_score)
            e = jnp.exp(s - top)
            gs_ref[part] = (e * (nn(v_ref[part], grads) - delta)).astype(bf16)
            e_ref[part] = e.astype(bf16)
        gv_ref[...] = nt(e_ref[...], grads).astype(bf16)
        gk_ref[...] = nn(gs_ref[...], queries).astype(bf16)
        gq = tn(k_ref[...], gs_ref[...])
        gqt_ref[lanes, tok] = jnp.concatenate([gq[0:DH, 0:LEN], gq[DH:, LEN:]], axis=0).astype(bf16)

        @pl.when(local == steps - 1)
        def _():
            gqt = gqt_ref[...]
            gwq = nn(gqt, n2_ref[...]).astype(bf16)
            gwo = nn(at_ref[...], go_ref[...]).astype(bf16)
            for i in range(2):
                outs[2 * side + i][0:w] = gwq[i * w : (i + 1) * w]
                outs[2 * side + i][w:] = gwo[i * w : (i + 1) * w]
            gn = tn(gqt, weights[side](2))
            gn_ref[...] = gn if side == 1 else gn_ref[...] + gn

    @pl.when(step < steps)
    def _():
        half(1, step, gk1, gv1)

    @pl.when(step >= steps)
    def _():
        half(0, step - steps, gk0, gv0)


def cross_bwd(y, lens, go, n2, w0, w1, side0, side1):
    t, d = go.shape
    te, c = side0[1].shape
    nb = t // LEN
    pairs = c // (2 * DH)
    steps = nb * pairs

    def early(i):
        return jnp.minimum(i, steps - 1)

    def late(i):
        return jnp.maximum(i - steps, 0)

    def tokhead(when):
        return pl.BlockSpec((ENC, 2 * DH), lambda i: (when(i) // pairs, when(i) % pairs))

    def side_specs(when):
        return [whole((t, c)), tokhead(when), tokhead(when), pl.BlockSpec((1, 4, LEN), lambda i: (when(i), 0, 0)), whole((c, t))]

    grad = jax.ShapeDtypeStruct((te, c), bf16)
    out = jax.ShapeDtypeStruct((c, d), bf16)
    return call(
        lambda *r_: cross_bwd_kernel(pairs, steps, *r_),
        (grad,) * 4 + (out,) * 4 + (jax.ShapeDtypeStruct((t, d), f32),),
        (y, lens, go, n2, *w0, *w1, *side0, *side1),
        grid=(2 * steps,),
        in_specs=[SMEM, SMEM, whole((t, d)), whole((t, d))]
        + [whole(a.shape) for a in (*w0, *w1)]
        + side_specs(late)
        + side_specs(early),
        out_specs=(tokhead(late), tokhead(late), tokhead(early), tokhead(early)) + (whole((c, d)),) * 4 + (whole((t, d)),),
        scratch=[
            pltpu.VMEM((c, t), bf16),
            pltpu.VMEM((c, t), bf16),
            pltpu.VMEM((ENC, 2 * LEN), bf16),
            pltpu.VMEM((ENC, 2 * LEN), bf16),
        ],
        vmem=BIG_VMEM,
        name="cross_bwd",
    )


def enc_grad_kernel(y_ref, enc_ref, gk1_ref, gv1_ref, gk0_ref, gv0_ref, *rest):
    w0 = pair_rows(y_ref, rest[0:2], False)
    w1 = pair_rows(y_ref, rest[2:6], True)
    out_ref, outs, accs_ref = rest[6], rest[7:11], rest[11]
    w = outs[0].shape[0] // 2
    step = pl.program_id(0)
    enc = enc_ref[...]
    grads = [g[...] for g in (gk1_ref, gv1_ref, gk0_ref, gv0_ref)]
    rhs = jnp.concatenate([w1(0), w1(1), w0(0), w0(1)], axis=0)
    out_ref[...] = nn(jnp.concatenate(grads, axis=1), rhs)
    terms = [tn(g, enc) for g in grads]

    @pl.when(step == 0)
    def _():
        for i in range(4):
            accs_ref[i] = terms[i]

    @pl.when(step != 0)
    def _():
        for i in range(4):
            accs_ref[i] += terms[i]

    @pl.when(step == pl.num_programs(0) - 1)
    def _():
        for pair in range(2):
            for i in range(2):
                acc = accs_ref[2 * pair + i]
                outs[2 * pair][i * w : (i + 1) * w] = acc[0:w].astype(bf16)
                outs[2 * pair + 1][i * w : (i + 1) * w] = acc[w:].astype(bf16)


def enc_grad(y, enc, gk1, gv1, gk0, gv0, w0, w1):
    te, d = enc.shape
    c = gk1.shape[1]
    rows = 512
    half = pl.BlockSpec((rows, c), lambda i: (i, 0))
    block = pl.BlockSpec((rows, d), lambda i: (i, 0))
    out = jax.ShapeDtypeStruct((c, d), bf16)
    return call(
        enc_grad_kernel,
        (jax.ShapeDtypeStruct((te, d), f32),) + (out,) * 4,
        (y, enc, gk1, gv1, gk0, gv0, *w0, *w1),
        grid=(te // rows,),
        in_specs=[SMEM, block] + [half] * 4 + [whole(a.shape) for a in (*w0, *w1)],
        out_specs=(block,) + (whole((c, d)),) * 4,
        scratch=[pltpu.VMEM((4, c, d), f32)],
        vmem=BIG_VMEM,
        name="enc_grad",
    )


def self_bwd_kernel(x_ref, x1_ref, gx2_ref, gn2_ref, g_ref, n1_ref, *rest):
    weights = rest[0:4]
    sides = (rest[4:10], rest[10:16])
    outs = rest[16:20]
    gd_ref, gg2_ref, gg1_ref, gi_ref, gat_ref, gqt_ref, gk_ref, gv_ref, gx1_ref = rest[20:]
    w = outs[0].shape[0] // 4
    c = 2 * w
    nb = n1_ref.shape[0] // LEN
    gx, gg2 = norm_back(x1_ref[...], g_ref[1:2].astype(f32), gn2_ref[...])
    gx1 = gx2_ref[...] + gx
    gx1_ref[...] = gx1
    gg2_ref[...] = gg2
    go = gx1.astype(bf16)
    ri = lax.broadcasted_iota(jnp.int32, (LEN, LEN), 0)
    ci = lax.broadcasted_iota(jnp.int32, (LEN, LEN), 1)
    flip = jnp.where(ri + ci == LEN - 1, 1.0, 0.0).astype(bf16)
    n1 = n1_ref[...]
    gn = None
    for side in (1, 0):
        shards = weights[2 * side : 2 * side + 2]
        q_ref, k_ref, vt_ref, e_ref, r_ref, at_ref = sides[side]
        gat_ref[...] = nt(side_by_side(shards, 3), go).astype(bf16)
        gwo = nn(at_ref[...], go).astype(bf16)
        for p in range(c // (2 * DH)):
            lanes = slice(p * 2 * DH, (p + 1) * 2 * DH)
            for h in range(2):
                head = side * (c // DH) + 2 * p + h
                gd_ref[head : head + 1, :] = jnp.zeros((1, LEN), f32)
            for b in range(nb):
                tok = slice(b * LEN, (b + 1) * LEN)

                def extra(h, gs):
                    turned = pltpu.roll(nn(gs, flip), 0, 1, stride=1, stride_axis=0)
                    head = side * (c // DH) + 2 * p + h
                    gd_ref[head : head + 1, :] += jnp.sum(turned, axis=0, keepdims=True)

                gq, gk, gv = head_pair_back(
                    k_ref[tok, lanes].T, vt_ref[lanes, tok].T, q_ref[tok, lanes], None, gat_ref[lanes, tok], at_ref[lanes, tok],
                    [e_ref[b, 2 * p], e_ref[b, 2 * p + 1]],
                    [r_ref[b, 2 * p : 2 * p + 1, :], r_ref[b, 2 * p + 1 : 2 * p + 2, :]],
                    extra,
                )
                gqt_ref[lanes, tok] = gq
                gk_ref[tok, lanes] = gk
                gv_ref[tok, lanes] = gv
        gqt = gqt_ref[...]
        gk = gk_ref[...]
        gv = gv_ref[...]
        gwq = nn(gqt, n1).astype(bf16)
        gwk = tn(gk, n1).astype(bf16)
        gwv = tn(gv, n1).astype(bf16)
        for i, gw in enumerate((gwq, gwk, gwv, gwo)):
            for j in range(2):
                outs[2 * side + j][i * w : (i + 1) * w] = gw[j * w : (j + 1) * w]
        part = tn(gqt, side_by_side(shards, 0)) + nn(gk, side_by_side(shards, 1)) + nn(gv, side_by_side(shards, 2))
        gn = part if gn is None else gn + part
    gi, gg1 = norm_back(x_ref[...].astype(f32), g_ref[0:1].astype(f32), gn)
    gi_ref[...] = gx1_ref[...] + gi
    gg1_ref[...] = gg1


def self_bwd(x, x1, gx2, gn2, g, n1, weights, side0, side1):
    t, d = x1.shape
    c = weights[0].shape[0] // 2
    args = [x, x1, gx2, gn2, g, n1, *weights, *side0, *side1]
    outs = [jax.ShapeDtypeStruct((2 * c, d), bf16)] * 4 + [
        jax.ShapeDtypeStruct((2 * c // DH, LEN), f32),
        jax.ShapeDtypeStruct((1, d), f32),
        jax.ShapeDtypeStruct((1, d), f32),
        jax.ShapeDtypeStruct((t, d), f32),
    ]
    return call(
        self_bwd_kernel,
        tuple(outs),
        args,
        in_specs=[whole(a.shape) for a in args],
        out_specs=tuple(whole(o.shape) for o in outs),
        scratch=[
            pltpu.VMEM((c, t), bf16),
            pltpu.VMEM((c, t), bf16),
            pltpu.VMEM((t, c), bf16),
            pltpu.VMEM((t, c), bf16),
            pltpu.VMEM((t, d), f32),
        ],
        vmem=BIG_VMEM,
        name="self_bwd",
    )


def local_program(tensor_size, dp_size, *arrays):
    (block_in, enc_states, dec_len, enc_len, gain_self, self_query, self_key, self_value, self_out, rel_table,
     gain_cross, cross_query, cross_key, cross_value, cross_out, gain_ff, ff_in, ff_out, out_grad) = arrays
    t_index = lax.axis_index("tensor")
    d_index = lax.axis_index("dp")
    nb = block_in.shape[0] // LEN
    w, d = self_out.shape
    heads = w // DH

    def swap(v, axis, bit):
        n = tensor_size if axis == "tensor" else dp_size
        return lax.ppermute(v, axis, [(i, i ^ bit) for i in range(n)])

    def d_bit(bit):
        return (d_index // bit) % 2

    y = d_bit(1).astype(jnp.int32)
    y_is0 = y == 0
    place = jnp.stack([y, (t_index * nb).astype(jnp.int32)])

    def core(v):
        return swap(v, "tensor", 1)

    def over_x(v):
        return swap(v, "tensor", 2)

    def over_y(v):
        return swap(v, "dp", 1)

    def fence(*vals):
        return lax.optimization_barrier(vals)

    gains = jnp.stack([gain_self, gain_cross, gain_ff])

    buckets = np.eye(BUCKETS, dtype=np.float32)[bucket_of_distance()]
    rel_own = jnp.dot(rel_table.astype(f32).T, jnp.asarray(buckets.T), precision=lax.Precision.HIGHEST)
    rel_x = over_x(rel_own)
    own_s = jnp.concatenate([self_query.T, self_key.T, self_value.T, self_out], axis=0)
    own_s, rel_own = fence(own_s, rel_own)
    x_s = over_x(own_s)
    s_0 = [own_s, core(own_s)]
    bias0 = jnp.concatenate([rel_own, core(rel_own)], axis=0)
    own_c = jnp.concatenate([cross_key.T, cross_value.T, cross_query.T, cross_out], axis=0)
    c_0 = [own_c, core(own_c)]
    out = self_fwd(False, place, dec_len, block_in, gains, s_0, bias0)
    *out, c_0[1] = fence(*out, c_0[1])
    fq0, fk0, fv0, fe0, fr0, fa0, xp = out
    k0, v0 = enc_kv(False, place, enc_states, c_0)
    k0, v0, xp, x_s, rel_x = fence(k0, v0, xp, x_s, rel_x)
    s_1 = [x_s, core(x_s)]
    bias1 = jnp.concatenate([rel_x, core(rel_x)], axis=0)
    half = own_c.shape[0] // 2
    send_c, x_s = fence(jnp.where(y_is0, own_c[:half], own_c[half:]), x_s)
    x_c = over_x(send_c)
    send_f, s_1[1], xp = fence(jnp.where(y_is0, ff_in, ff_out), s_1[1], xp)
    x_f = over_x(send_f)
    out = self_fwd(True, place, dec_len, block_in, gains, s_1, bias1, xp)
    *out, x_c = fence(*out, x_c)
    fq1, fk1, fv1, fe1, fr1, fa1, x1, n1, n2 = out
    y_c, c_c = over_y(x_c), core(x_c)
    cq0, cr0, ca0, x2p = cross_fwd(False, place, enc_len, n2, gains, c_0, k0, v0, x1)
    x2p, y_c, c_c = fence(x2p, y_c, c_c)
    c_1 = [x_c, y_c, c_c, core(y_c)]
    wi1, wo1 = core(ff_in), core(ff_out)
    k1, v1 = enc_kv(True, place, enc_states, c_1)
    k1, v1, x_f = fence(k1, v1, x_f)
    y_f, c_f = over_y(x_f), core(x_f)
    cq1, cr1, ca1, x2, n3 = cross_fwd(True, place, enc_len, n2, gains, c_1, k1, v1, x2p)
    n3, x2, wi1, wo1, c_f = fence(n3, x2, wi1, wo1, c_f)

    rest_size = dp_size // 2
    m = d_index // 2
    rest_groups = [[2 * i + j for i in range(rest_size)] for j in range(2)]

    def plus(*vals):
        total = vals[0].astype(f32)
        for v in vals[1:]:
            total = total + v.astype(f32)
        return total.astype(bf16)

    def pick(v, n, i):
        v = v.reshape((n, v.shape[0] // n) + v.shape[1:])
        return lax.dynamic_index_in_dim(v, i, 0, keepdims=False)

    def ordered(a, b):
        return jnp.where(y_is0, jnp.concatenate([a, b], axis=0), jnp.concatenate([b, a], axis=0))

    def sent_y(*vals):
        return over_y(plus(*[pick(v, 2, 1 - y) for v in vals]))

    def kept_y(*vals):
        return [pick(v, 2, y) for v in vals]

    def sum_ordered(parts):
        while len(parts) > 1:
            parts = [a + b for a, b in zip(parts[0::2], parts[1::2])]
        return parts[0]

    def stage_z(v):
        return [pick(v, rest_size, m)] + [swap(pick(v, rest_size, m ^ j), "dp", 2 * j) for j in range(1, rest_size)]

    def stage_z_back(v):
        return [v] + [swap(v, "dp", 2 * j) for j in range(1, rest_size)]

    def ordered_z(parts):
        bit = 1
        while len(parts) > 1:
            low = (m // bit) % 2 == 0
            parts = [
                jnp.where(low, jnp.concatenate([a, b], axis=0), jnp.concatenate([b, a], axis=0))
                for a, b in zip(parts[0::2], parts[1::2])
            ]
            bit *= 2
        return parts[0]

    gwi0, gwo0, gwi1, gwo1, yp, gp = ff(False, place, n3, out_grad, [ff_in, ff_out, wi1, wo1])
    yp, y_f = fence(yp, y_f)
    a1, b1 = core(gwo1), core(gwi1)
    f_1 = [x_f, y_f, c_f, core(y_f)]
    out = ff(True, place, n3, out_grad, f_1, yp, gp, x2, gains)
    *out, a1, b1 = fence(*out, a1, b1)
    gwi2, gwo2, gwi3, gwo3, block_out, gx2, go2, gg3 = out
    a3, b3 = core(gwo3), core(gwi3)
    a3, b3, go2 = fence(a3, b3, go2)
    wo_s = plus(gwo2, a3)
    wi_send = jnp.concatenate(
        [plus(pick(gwi0, 2, 1 - y), pick(b1, 2, 1 - y)), plus(pick(gwi2, 2, 1 - y), pick(b3, 2, 1 - y))], axis=0
    )
    wo_s, wi_send, go2 = fence(wo_s, wi_send, go2)
    xo = over_x(wo_s)
    ywi = over_y(wi_send)
    out = cross_bwd(place, enc_len, go2, n2, c_0, c_1, (cq0, k0, v0, cr0, ca0), (cq1, k1, v1, cr1, ca1))
    *out, xo, ywi = fence(*out, xo, ywi)
    gk0, gv0, gk1, gv1, gqo0, gqo1, gqo2, gqo3, gn2 = out
    c3 = core(gqo3)
    hid = gwi0.shape[0] // 2
    wi_x = plus(pick(gwi2, 2, y), pick(b3, 2, y), ywi[hid:])
    wo_y = plus(*[pick(v, 2, 1 - y) for v in (gwo0, a1, xo)])
    wi_x, wo_y, c3, gk0 = fence(wi_x, wo_y, c3, gk0)
    xwi, ywo = over_x(wi_x), over_y(wo_y)
    qo_x, gk0 = fence(plus(gqo2, c3), gk0)
    xqo = over_x(qo_x)
    grad_enc, gkv2, gkv3, gkv0, gkv1 = enc_grad(place, enc_states, gk1, gv1, gk0, gv0, c_0, c_1)
    gkv3, gn2, xwi, ywo = fence(gkv3, gn2, xwi, ywo)
    k3, k1, c1 = core(gkv3), core(gkv1), core(gqo1)
    f_u = jnp.concatenate(
        [plus(*kept_y(gwo0, a1, xo), ywo), plus(*kept_y(gwi0, b1), ywi[:hid], xwi)], axis=0
    )
    f_u, k3, k1, gn2 = fence(f_u, k3, k1, gn2)
    kv_x, gn2 = fence(plus(gkv2, k3), gn2)
    xkv = over_x(kv_x)
    zf = stage_z(f_u)
    out = self_bwd(
        block_in, x1, gx2, gn2, gains, n1, [*s_0, *s_1], (fq0, fk0, fv0, fe0, fr0, fa0), (fq1, fk1, fv1, fe1, fr1, fa1)
    )
    gs0, gs1, gs2, gs3, gd, gg2, gg1, grad_in = out
    gs0, gs3, gd, gg1, xqo, xkv, c1, *zf = fence(gs0, gs3, gd, gg1, xqo, xkv, c1, *zf)
    s3 = core(gs3)
    qo_t, kv_t = (gqo0, c1, xqo), (gkv0, k1, xkv)
    c_y = plus(*[jnp.where(y_is0, b_, a_) for a_, b_ in zip(qo_t, kv_t)])
    f_w = plus(*zf)
    s3, c_y, f_w = fence(s3, c_y, f_w)
    s_x = plus(gs2, s3)
    s_x, c_y, f_w, gs1, gd, gg1 = fence(s_x, c_y, f_w, gs1, gd, gg1)
    xs = over_x(s_x)
    yc = over_y(c_y)
    bf = stage_z_back(f_w)
    s1 = core(gs1)
    flipped = jnp.asarray(np.ascontiguousarray(buckets[::-1]))
    grel = jnp.dot(gd, flipped, precision=lax.Precision.HIGHEST)
    grel = grel.reshape(tensor_size, heads * BUCKETS)
    slots = jnp.arange(tensor_size)[:, None] ^ t_index
    order = (slots == jnp.arange(tensor_size)[None, :]).astype(f32)
    grel = jnp.dot(order.T, grel, precision=lax.Precision.HIGHEST)
    grel = jnp.pad(grel.reshape(1, -1), ((0, 0), (0, d - grel.size)))
    small = jnp.concatenate([gg1, gg2, gg3, grel], axis=0)
    small_got = core(small)
    yc, small_got, s1, xs, *bf = fence(yc, small_got, s1, xs, *bf)
    ys = sent_y(gs0, s1, xs)
    zc = stage_z(plus(*[jnp.where(y_is0, a_, b_) for a_, b_ in zip(qo_t, kv_t)], yc))
    small = small + small_got
    small_got = over_x(small)
    f_v = ordered_z(bf)
    ys, small_got, f_v, *zc = fence(ys, small_got, f_v, *zc)
    zs = stage_z(plus(*kept_y(gs0, s1, xs), ys))
    small = small + small_got
    small_got = over_y(small)
    f_y, small_got = fence(f_v, small_got)
    f_f = over_y(f_y)
    c_w = plus(*zc)
    small_got, c_w, *zs = fence(small_got, c_w, *zs)
    bc = stage_z_back(c_w)
    bit = 2
    small = small + small_got
    small_got = swap(small, "dp", bit)
    bs = stage_z_back(plus(*zs))
    both = fence(small_got, *bs, *bc)
    small_got, bs, bc = both[0], both[1 : 1 + rest_size], both[1 + rest_size :]
    small = small + small_got
    while 2 * bit < dp_size:
        bit *= 2
        small = small + swap(small, "dp", bit)
    c_v = ordered_z(bc)
    c_f = over_y(c_v)
    s_v = ordered_z(bs)
    s_f = over_y(s_v)
    n_f = f_v.shape[0] // 2
    r_wo = ordered(f_v[:n_f], f_f[:n_f]).astype(f32)
    r_wi = ordered(f_v[n_f:], f_f[n_f:]).astype(f32)
    s_f, r_wo, r_wi = fence(s_f, r_wo, r_wi)
    r_s = ordered(s_v, s_f)
    g_s = [r_s[i * w : (i + 1) * w].astype(f32) for i in range(4)]
    c_f, *g_s = fence(c_f, *g_s)
    c_w = [jnp.where(y_is0, a_, b_) for a_, b_ in ((c_v, c_f), (c_f, c_v))]
    g_c = [v[i * w : (i + 1) * w].astype(f32) for v in c_w for i in range(2)]
    grad_rel = lax.dynamic_slice(small[3], (t_index * heads * BUCKETS,), (heads * BUCKETS,)).reshape(heads, BUCKETS).T

    return (
        block_out,
        grad_in,
        grad_enc,
        small[0],
        g_s[0].T,
        g_s[1].T,
        g_s[2].T,
        g_s[3],
        grad_rel,
        small[1],
        g_c[0].T,
        g_c[2].T,
        g_c[3].T,
        g_c[1],
        small[2],
        r_wi,
        r_wo,
    )


def solution(mesh):
    tensor_size = mesh.shape["tensor"]
    dp_size = mesh.shape["dp"]
    both = P(("dp", "tensor"), None)
    col = P(None, "tensor")
    row = P("tensor", None)
    placed = (both, both, P("dp"), P("dp"), P(), col, col, col, row, col, P(), col, col, col, row, P(), col, row, both)
    outs = (both, both, both, P(), col, col, col, row, col, P(), col, col, col, row, P(), col, row)
    return jax.shard_map(
        lambda *a: local_program(tensor_size, dp_size, *a),
        mesh=mesh,
        in_specs=placed,
        out_specs=outs,
        check_vma=False,
    )
```

```python
import math

import jax
import jax.numpy as jnp
import numpy as np
from jax import lax
from jax.experimental import pallas as pl
from jax.experimental.pallas import tpu as pltpu
from jax.sharding import PartitionSpec as P

BUCKETS = 32
MAX_DIST = 128
LEN = 256
ENC = 1024
DH = 64
KEYS = 256

norm_eps = 1e-06
masked_score = -1000000000.0
bf16 = jnp.bfloat16
f32 = jnp.float32
VMEM_CAP = 16 << 20
BIG_VMEM = 58 << 20


def bucket_of_distance():
    half_count = BUCKETS // 2
    growth_ratio = MAX_DIST / half_count
    limits = np.array(
        [int(math.ceil(half_count * growth_ratio ** (m / half_count))) for m in range(1, half_count)],
        dtype=np.int32,
    )
    distance = np.arange(LEN, dtype=np.int32)
    above = np.sum(distance[:, None] >= limits[None, :], axis=1)
    return np.where(distance < half_count, distance, half_count + above).astype(np.int32)


def nn(a, b):
    return lax.dot_general(a, b, (((1,), (0,)), ((), ())), preferred_element_type=f32)


def nt(a, b):
    return lax.dot_general(a, b, (((1,), (1,)), ((), ())), preferred_element_type=f32)


def tn(a, b):
    return lax.dot_general(a, b, (((0,), (0,)), ((), ())), preferred_element_type=f32)


def inv_rms(v):
    return lax.rsqrt(jnp.mean(v * v, axis=-1, keepdims=True) + norm_eps)


def normed(v, gain):
    return (v * inv_rms(v) * gain).astype(bf16)


def norm_back(v, gain, e):
    s = inv_rms(v)
    ge = gain * e
    dot = jnp.mean(ge * v, axis=-1, keepdims=True)
    grad_v = s * ge - v * (s * s * s * dot)
    grad_gain = jnp.sum(e * v * s, axis=0, keepdims=True)
    return grad_v, grad_gain


def lane_half(shape, h):
    lane = lax.broadcasted_iota(jnp.int32, shape, 1)
    return (lane < DH) if h == 0 else (lane >= DH)


def both_heads(rows):
    zero = jnp.zeros_like(rows)
    return jnp.concatenate([jnp.where(lane_half(rows.shape, h), rows, zero) for h in range(2)], axis=0)


def call(kernel, out_shape, args, *, grid=(), in_specs=None, out_specs=None, scratch=(), flops=0, nbytes=0, trans=0, name=None, vmem=VMEM_CAP):
    kw = {}
    if in_specs is not None:
        kw["in_specs"] = in_specs
    if out_specs is not None:
        kw["out_specs"] = out_specs
    return pl.pallas_call(
        kernel,
        out_shape=out_shape,
        grid=grid,
        scratch_shapes=scratch,
        compiler_params=pltpu.CompilerParams(vmem_limit_bytes=vmem),
        cost_estimate=pl.CostEstimate(flops=1, bytes_accessed=1, transcendentals=0),
        name=name,
        **kw,
    )(*args)


def whole(shape):
    return pl.BlockSpec(shape, lambda *_: (0,) * len(shape))


SMEM = pl.BlockSpec(memory_space=pltpu.SMEM)


def side_by_side(refs, i):
    w = refs[0].shape[0] // 4
    return jnp.concatenate([r[i * w : (i + 1) * w] for r in refs], axis=0)


def pair_rows(y_ref, refs, shared):
    def rows(i):
        if not shared:
            return side_by_side(refs, i)
        w = refs[0].shape[0] // 2
        first = y_ref[0] == i // 2
        part = slice((i % 2) * w, (i % 2 + 1) * w)
        return jnp.concatenate(
            [jnp.where(first, refs[0][part], refs[1][part]), jnp.where(first, refs[2][part], refs[3][part])], axis=0
        )

    return rows


def self_fwd_kernel(last, y_ref, len_ref, x_ref, g_ref, *rest):
    weights = rest[0:2]
    bias_ref = rest[2]
    rest = rest[3:]
    if last:
        xin_ref, q_ref, k_ref, vt_ref, e_ref, r_ref, at_ref, x1_ref, n1_ref, n2_ref, bs_ref = rest
    else:
        q_ref, k_ref, vt_ref, e_ref, r_ref, at_ref, x1_ref, bs_ref = rest
    nh = q_ref.shape[1] // DH
    nb = x_ref.shape[0] // LEN
    x = x_ref[...].astype(f32)
    n1 = normed(x, g_ref[0:1].astype(f32))
    if last:
        n1_ref[...] = n1

    q_ref[...] = nt(n1, side_by_side(weights, 0)).astype(bf16)
    k_ref[...] = nt(n1, side_by_side(weights, 1)).astype(bf16)
    vt_ref[...] = nt(side_by_side(weights, 2), n1).astype(bf16)
    key = lax.broadcasted_iota(jnp.int32, (LEN, 2 * LEN), 0)
    query = lax.broadcasted_iota(jnp.int32, (LEN, 2 * LEN), 1)
    query = jnp.where(query < LEN, query, query - LEN)
    for p in range(nh // 2):
        lanes = slice(p * 2 * DH, (p + 1) * 2 * DH)
        for h in range(2):
            row = jnp.broadcast_to(bias_ref[2 * p + h : 2 * p + h + 1, :], (LEN, LEN))
            bs_ref[:, h * LEN : (h + 1) * LEN] = pltpu.roll(row, 0, 1, stride=1, stride_axis=0)
        for b in range(nb):
            tok = slice(b * LEN, (b + 1) * LEN)
            allowed = (key <= query) & (key < len_ref[y_ref[1] + b])
            s = nt(k_ref[tok, lanes], both_heads(q_ref[tok, lanes])) + bs_ref[...]
            s = jnp.where(allowed, s, masked_score)
            e = jnp.exp(s - jnp.max(s, axis=0, keepdims=True))
            r = 1.0 / jnp.sum(e, axis=0, keepdims=True)
            e = e.astype(bf16)
            outs = []
            for h in range(2):
                head = 2 * p + h
                half = slice(h * LEN, (h + 1) * LEN)
                e_ref[b, head] = e[:, half]
                r_ref[b, head : head + 1, :] = r[:, half]
                outs.append(nn(vt_ref[head * DH : (head + 1) * DH, tok], e[:, half]) * r[:, half])
            at_ref[lanes, tok] = jnp.concatenate(outs, axis=0).astype(bf16)
    mixed = tn(at_ref[...], side_by_side(weights, 3))
    if last:
        x1 = xin_ref[...] + mixed
        n2_ref[...] = normed(x1, g_ref[1:2].astype(f32))
    else:
        x1 = x + mixed
    x1_ref[...] = x1


def self_fwd(last, y, lens, x, g, weights, bias, xin=None):
    t, d = x.shape
    w = weights[0].shape[0] // 4
    c = 2 * w
    nh = c // DH
    nb = t // LEN
    outs = [
        jax.ShapeDtypeStruct((t, c), bf16),
        jax.ShapeDtypeStruct((t, c), bf16),
        jax.ShapeDtypeStruct((c, t), bf16),
        jax.ShapeDtypeStruct((nb, nh, LEN, LEN), bf16),
        jax.ShapeDtypeStruct((nb, nh, LEN), f32),
        jax.ShapeDtypeStruct((c, t), bf16),
        jax.ShapeDtypeStruct((t, d), f32),
    ]
    args = [y, lens, x, g, *weights, bias]
    if last:
        args.append(xin)
        outs += [jax.ShapeDtypeStruct((t, d), bf16)] * 2
    flops = 2 * t * d * c * 4 + 2 * t * LEN * nh * 128 * 2
    return call(
        lambda *r: self_fwd_kernel(last, *r),
        tuple(outs),
        args,
        in_specs=[SMEM, SMEM] + [whole(a.shape) for a in args[2:]],
        out_specs=tuple(whole(o.shape) for o in outs),
        scratch=[pltpu.VMEM((LEN, 2 * LEN), f32)],
        flops=flops * 3,
        nbytes=12 * 1024 * 1024,
        trans=t * LEN * nh,
        name="self_fwd",
    )


def enc_kv_kernel(shared, y_ref, enc_ref, *rest):
    k_ref, v_ref = rest[-2:]
    enc = enc_ref[...]
    rows = pair_rows(y_ref, rest[:-2], shared)
    k_ref[...] = nt(enc, rows(0)).astype(bf16)
    v_ref[...] = nt(enc, rows(1)).astype(bf16)


def enc_kv(shared, y, enc, kv):
    t, d = enc.shape
    c = kv[0].shape[0] if shared else kv[0].shape[0] // 2
    rows = 512
    half = pl.BlockSpec((rows, c), lambda i: (i, 0))
    return call(
        lambda *r: enc_kv_kernel(shared, *r),
        (jax.ShapeDtypeStruct((t, c), bf16),) * 2,
        (y, enc, *kv),
        grid=(t // rows,),
        in_specs=[SMEM, pl.BlockSpec((rows, d), lambda i: (i, 0))] + [whole(a.shape) for a in kv],
        out_specs=(half, half),
        flops=2 * t * d * c * 2 * 2,
        nbytes=t * d * 2 + 4 * t * c * 2,
        name="enc_kv",
    )


def cross_fwd_kernel(last, pairs, y_ref, len_ref, n2_ref, g_ref, *rest):
    n_w = 4 if last else 2
    weights = pair_rows(y_ref, rest[:n_w], last)
    k_ref, v_ref, xin_ref = rest[n_w : n_w + 3]
    rest = rest[n_w + 3 :]
    if last:
        q_ref, r_ref, at_ref, x2_ref, n3_ref, s_ref, e_ref = rest
    else:
        q_ref, r_ref, at_ref, x2_ref, s_ref, e_ref = rest
    step = pl.program_id(0)
    b = step // pairs
    p = lax.rem(step, pairs)

    @pl.when(step == 0)
    def _():
        q_ref[...] = nt(n2_ref[...], weights(2)).astype(bf16)

    tok = pl.ds(pl.multiple_of(b * LEN, LEN), LEN)
    lanes = pl.ds(pl.multiple_of(p * 2 * DH, 2 * DH), 2 * DH)
    qp = q_ref[tok, lanes]
    count = len_ref[y_ref[1] + b]
    key = lax.broadcasted_iota(jnp.int32, (KEYS, 2 * LEN), 0)
    queries = both_heads(qp)
    top = None
    for c in range(ENC // KEYS):
        part = slice(c * KEYS, (c + 1) * KEYS)
        s = jnp.where(key < count - c * KEYS, nt(k_ref[part], queries), masked_score)
        s_ref[part] = s
        t = jnp.max(s.reshape(KEYS // 8, 8, 2 * LEN), axis=0)
        top = t if c == 0 else jnp.maximum(top, t)
    top = jnp.max(top, axis=0, keepdims=True)
    total = None
    for c in range(ENC // KEYS):
        part = slice(c * KEYS, (c + 1) * KEYS)
        e = jnp.exp(s_ref[part] - top)
        t = jnp.sum(e.reshape(KEYS // 8, 8, 2 * LEN), axis=0)
        total = t if c == 0 else total + t
        e_ref[part] = e.astype(bf16)
    r = 1.0 / jnp.sum(total, axis=0, keepdims=True)
    mixed = tn(v_ref[...], e_ref[...]) * r
    outs = []
    for h in range(2):
        half = slice(h * LEN, (h + 1) * LEN)
        r_ref[0, h : h + 1, :] = r[:, half]
        r_ref[0, 2 + h : 3 + h, :] = top[:, half]
        outs.append(mixed[h * DH : (h + 1) * DH, half])
    at_ref[lanes, tok] = jnp.concatenate(outs, axis=0).astype(bf16)

    @pl.when(step == pl.num_programs(0) - 1)
    def _():
        x2 = xin_ref[...] + tn(at_ref[...], weights(3))
        x2_ref[...] = x2
        if last:
            n3_ref[...] = normed(x2, g_ref[2:3].astype(f32))


def cross_fwd(last, y, lens, n2, g, qo, k, v, xin):
    t, d = n2.shape
    c = k.shape[1]
    nb = t // LEN
    pairs = c // (2 * DH)
    outs = [
        jax.ShapeDtypeStruct((t, c), bf16),
        jax.ShapeDtypeStruct((nb * pairs, 4, LEN), f32),
        jax.ShapeDtypeStruct((c, t), bf16),
        jax.ShapeDtypeStruct((t, d), f32),
    ]
    specs = [
        whole((t, c)),
        pl.BlockSpec((1, 4, LEN), lambda i: (i, 0, 0)),
        whole((c, t)),
        whole((t, d)),
    ]
    if last:
        outs.append(jax.ShapeDtypeStruct((t, d), bf16))
        specs.append(whole((t, d)))
    return call(
        lambda *r: cross_fwd_kernel(last, pairs, *r),
        tuple(outs),
        (y, lens, n2, g, *qo, k, v, xin),
        grid=(nb * pairs,),
        in_specs=[
            SMEM,
            SMEM,
            whole(n2.shape),
            whole(g.shape),
            *[whole(a.shape) for a in qo],
            pl.BlockSpec((ENC, 2 * DH), lambda i: (i // pairs, i % pairs)),
            pl.BlockSpec((ENC, 2 * DH), lambda i: (i // pairs, i % pairs)),
            whole(xin.shape),
        ],
        out_specs=tuple(specs),
        scratch=[pltpu.VMEM((ENC, 2 * LEN), f32), pltpu.VMEM((ENC, 2 * LEN), bf16)],
        flops=3 * (2 * t * d * c * 2 + 2 * t * ENC * c * 2 * 2),
        nbytes=14 * 1024 * 1024,
        trans=t * ENC * (c // DH),
        name="cross_fwd",
    )


ROOT = math.sqrt(2.0 / math.pi)
CUBE = 0.044715


def ff_kernel(last, y_ref, n3_ref, gf_ref, *rest):
    if last:
        ha_in, ha_out, ga_in, ga_out, hb_in, hb_out, gb_in, gb_out = rest[:8]
        rest = rest[8:]
        first = y_ref[0] == 0

        def weights(h_in, h_out, g_in, g_out):
            return (
                lambda: jnp.where(first, h_in[...], g_in[...]),
                lambda: jnp.where(first, g_out[...], h_out[...]),
            )

        shards = (weights(ha_in, ha_out, ga_in, ga_out), weights(hb_in, hb_out, gb_in, gb_out))
    else:
        wia_ref, woa_ref, wib_ref, wob_ref = rest[:4]
        rest = rest[4:]
        shards = ((lambda: wia_ref[...], lambda: woa_ref[...]), (lambda: wib_ref[...], lambda: wob_ref[...]))
    if last:
        yin_ref, gin_ref, x2_ref, g_ref = rest[:4]
        gwia, gwoa, gwib, gwob, out_ref, gx2_ref, go2_ref, gg_ref, y_acc, gn_ref, n3t_ref = rest[4:]
    else:
        gwia, gwoa, gwib, gwob, y_acc, gn_ref, n3t_ref = rest
    step = pl.program_id(0)

    @pl.when(step == 0)
    def _():
        n3t_ref[...] = n3_ref[...].T
        if last:
            y_acc[...] = yin_ref[...]
            gn_ref[...] = gin_ref[...]
        else:
            y_acc[...] = jnp.zeros_like(y_acc)
            gn_ref[...] = jnp.zeros_like(gn_ref)

    n3 = n3_ref[...]
    gf = gf_ref[...]
    kept = []
    for (get_wi, get_wo), gwi, gwo in zip(shards, (gwia, gwib), (gwoa, gwob)):
        wi, wo = get_wi(), get_wo()
        u = nn(n3, wi)
        dh = nt(gf, wo)
        u2 = u * u
        th = jnp.tanh(ROOT * u * (1.0 + CUBE * u2))
        half = 0.5 * (1.0 + th)
        r = (u * half).astype(bf16)
        slope = half + 0.5 * u * (1.0 - th * th) * (ROOT * (1.0 + (3.0 * CUBE) * u2))
        gu = (dh * slope).astype(bf16)
        kept.append((r, wo, gu, wi))
        gwo[...] = tn(r, gf).astype(bf16)
        gwi[...] = nn(n3t_ref[...], gu).astype(bf16)
    r, wo, gu, wi = [jnp.concatenate(v, axis=a) for v, a in zip(zip(*kept), (1, 0, 1, 1))]
    y_acc[...] += nn(r, wo)
    gn_ref[...] += nt(gu, wi)

    if last:

        @pl.when(step == pl.num_programs(0) - 1)
        def _():
            x2 = x2_ref[...]
            out_ref[...] = (x2 + y_acc[...]).astype(bf16)
            gx, gg = norm_back(x2, g_ref[2:3].astype(f32), gn_ref[...])
            gx2 = gf.astype(f32) + gx
            gx2_ref[...] = gx2
            go2_ref[...] = gx2.astype(bf16)
            gg_ref[...] = gg


def ff(last, y, n3, gf, weights, yin=None, gin=None, x2=None, g=None):
    t, d = n3.shape
    hid = weights[0].shape[1]
    blk = 256
    args = [y, n3, gf]
    col = pl.BlockSpec((d, blk), lambda i: (0, i))
    row = pl.BlockSpec((blk, d), lambda i: (i, 0))
    in_specs = [SMEM, whole((t, d)), whole((t, d))]
    if last:
        for v in weights:
            args += [v, v]
            in_specs += [col, row]
    else:
        args += weights
        in_specs += [col, row, col, row]
    outs = [jax.ShapeDtypeStruct((d, hid), bf16), jax.ShapeDtypeStruct((hid, d), bf16)] * 2
    specs = [col, row, col, row]
    acc = jax.ShapeDtypeStruct((t, d), f32)
    scratch = [pltpu.VMEM((d, t), bf16)]
    if last:
        args += [yin, gin, x2, g]
        in_specs += [whole((t, d))] * 3 + [whole(g.shape)]
        outs += [jax.ShapeDtypeStruct((t, d), bf16), acc, jax.ShapeDtypeStruct((t, d), bf16), jax.ShapeDtypeStruct((1, d), f32)]
        specs += [whole((t, d))] * 3 + [whole((1, d))]
        scratch = [pltpu.VMEM((t, d), f32)] * 2 + scratch
    else:
        outs += [acc, acc]
        specs += [whole((t, d))] * 2
    return call(
        lambda *r: ff_kernel(last, *r),
        tuple(outs),
        args,
        grid=(hid // blk,),
        in_specs=in_specs,
        out_specs=tuple(specs),
        scratch=scratch,
        flops=2 * 6 * 2 * t * d * hid * 2,
        nbytes=12 * 1024 * 1024,
        trans=2 * t * hid,
        vmem=20 << 20,
        name="ff",
    )


def cross_bwd_kernel(pairs, steps, y_ref, len_ref, go_ref, n2_ref, *rest):
    weights = (pair_rows(y_ref, rest[0:2], False), pair_rows(y_ref, rest[2:6], True))
    sides = (rest[6:11], rest[11:16])
    gk0, gv0, gk1, gv1, outs, gn_ref, gat_ref, gqt_ref, e_ref, gs_ref = *rest[16:20], rest[20:24], *rest[24:]
    w = outs[0].shape[0] // 2
    step = pl.program_id(0)
    key = lax.broadcasted_iota(jnp.int32, (KEYS, 2 * LEN), 0)

    def half(side, local, gk_ref, gv_ref):
        q_ref, k_ref, v_ref, r_ref, at_ref = sides[side]
        b = local // pairs
        p = lax.rem(local, pairs)

        @pl.when(local == 0)
        def _():
            gat_ref[...] = nt(weights[side](3), go_ref[...]).astype(bf16)

        tok = pl.ds(pl.multiple_of(b * LEN, LEN), LEN)
        lanes = pl.ds(pl.multiple_of(p * 2 * DH, 2 * DH), 2 * DH)
        qp = q_ref[tok, lanes]
        ga_t = gat_ref[lanes, tok]
        a_t = at_ref[lanes, tok]
        count = len_ref[y_ref[1] + b]
        grads, deltas = [], []
        for h in range(2):
            part = slice(h * DH, (h + 1) * DH)
            gah = ga_t[part].astype(f32) * r_ref[0, h : h + 1, :]
            deltas.append(jnp.sum(gah * a_t[part].astype(f32), axis=0, keepdims=True))
            gah = gah.astype(bf16)
            zero = jnp.zeros_like(gah)
            grads.append(jnp.concatenate([gah, zero] if h == 0 else [zero, gah], axis=0))
        grads = jnp.concatenate(grads, axis=1)
        delta = jnp.concatenate(deltas, axis=1)
        top = jnp.concatenate([r_ref[0, 2:3, :], r_ref[0, 3:4, :]], axis=1)
        queries = both_heads(qp)
        for c in range(ENC // KEYS):
            part = slice(c * KEYS, (c + 1) * KEYS)
            s = jnp.where(key < count - c * KEYS, nt(k_ref[part], queries), masked_score)
            e = jnp.exp(s - top)
            gs_ref[part] = (e * (nn(v_ref[part], grads) - delta)).astype(bf16)
            e_ref[part] = e.astype(bf16)
        gv_ref[...] = nt(e_ref[...], grads).astype(bf16)
        gk_ref[...] = nn(gs_ref[...], queries).astype(bf16)
        gq = tn(k_ref[...], gs_ref[...])
        gqt_ref[lanes, tok] = jnp.concatenate([gq[0:DH, 0:LEN], gq[DH:, LEN:]], axis=0).astype(bf16)

        @pl.when(local == steps - 1)
        def _():
            gqt = gqt_ref[...]
            gwq = nn(gqt, n2_ref[...]).astype(bf16)
            gwo = nn(at_ref[...], go_ref[...]).astype(bf16)
            for i in range(2):
                outs[2 * side + i][0:w] = gwq[i * w : (i + 1) * w]
                outs[2 * side + i][w:] = gwo[i * w : (i + 1) * w]
            gn = tn(gqt, weights[side](2))
            gn_ref[...] = gn if side == 1 else gn_ref[...] + gn

    @pl.when(step < steps)
    def _():
        half(1, step, gk1, gv1)

    @pl.when(step >= steps)
    def _():
        half(0, step - steps, gk0, gv0)


def cross_bwd(y, lens, go, n2, w0, w1, side0, side1):
    t, d = go.shape
    te, c = side0[1].shape
    nb = t // LEN
    pairs = c // (2 * DH)
    steps = nb * pairs

    def early(i):
        return jnp.minimum(i, steps - 1)

    def late(i):
        return jnp.maximum(i - steps, 0)

    def tokhead(when):
        return pl.BlockSpec((ENC, 2 * DH), lambda i: (when(i) // pairs, when(i) % pairs))

    def side_specs(when):
        return [whole((t, c)), tokhead(when), tokhead(when), pl.BlockSpec((1, 4, LEN), lambda i: (when(i), 0, 0)), whole((c, t))]

    grad = jax.ShapeDtypeStruct((te, c), bf16)
    out = jax.ShapeDtypeStruct((c, d), bf16)
    return call(
        lambda *r_: cross_bwd_kernel(pairs, steps, *r_),
        (grad,) * 4 + (out,) * 4 + (jax.ShapeDtypeStruct((t, d), f32),),
        (y, lens, go, n2, *w0, *w1, *side0, *side1),
        grid=(2 * steps,),
        in_specs=[SMEM, SMEM, whole((t, d)), whole((t, d))]
        + [whole(a.shape) for a in (*w0, *w1)]
        + side_specs(late)
        + side_specs(early),
        out_specs=(tokhead(late), tokhead(late), tokhead(early), tokhead(early)) + (whole((c, d)),) * 4 + (whole((t, d)),),
        scratch=[
            pltpu.VMEM((c, t), bf16),
            pltpu.VMEM((c, t), bf16),
            pltpu.VMEM((ENC, 2 * LEN), bf16),
            pltpu.VMEM((ENC, 2 * LEN), bf16),
        ],
        vmem=BIG_VMEM,
        name="cross_bwd",
    )


def enc_grad_kernel(y_ref, enc_ref, gk1_ref, gv1_ref, gk0_ref, gv0_ref, *rest):
    w0 = pair_rows(y_ref, rest[0:2], False)
    w1 = pair_rows(y_ref, rest[2:6], True)
    out_ref, outs, accs_ref = rest[6], rest[7:11], rest[11]
    w = outs[0].shape[0] // 2
    step = pl.program_id(0)
    enc = enc_ref[...]
    grads = [g[...] for g in (gk1_ref, gv1_ref, gk0_ref, gv0_ref)]
    rhs = jnp.concatenate([w1(0), w1(1), w0(0), w0(1)], axis=0)
    out_ref[...] = nn(jnp.concatenate(grads, axis=1), rhs)
    terms = [tn(g, enc) for g in grads]

    @pl.when(step == 0)
    def _():
        for i in range(4):
            accs_ref[i] = terms[i]

    @pl.when(step != 0)
    def _():
        for i in range(4):
            accs_ref[i] += terms[i]

    @pl.when(step == pl.num_programs(0) - 1)
    def _():
        for pair in range(2):
            for i in range(2):
                acc = accs_ref[2 * pair + i]
                outs[2 * pair][i * w : (i + 1) * w] = acc[0:w].astype(bf16)
                outs[2 * pair + 1][i * w : (i + 1) * w] = acc[w:].astype(bf16)


def enc_grad(y, enc, gk1, gv1, gk0, gv0, w0, w1):
    te, d = enc.shape
    c = gk1.shape[1]
    rows = 512
    half = pl.BlockSpec((rows, c), lambda i: (i, 0))
    block = pl.BlockSpec((rows, d), lambda i: (i, 0))
    out = jax.ShapeDtypeStruct((c, d), bf16)
    return call(
        enc_grad_kernel,
        (jax.ShapeDtypeStruct((te, d), f32),) + (out,) * 4,
        (y, enc, gk1, gv1, gk0, gv0, *w0, *w1),
        grid=(te // rows,),
        in_specs=[SMEM, block] + [half] * 4 + [whole(a.shape) for a in (*w0, *w1)],
        out_specs=(block,) + (whole((c, d)),) * 4,
        scratch=[pltpu.VMEM((4, c, d), f32)],
        vmem=BIG_VMEM,
        name="enc_grad",
    )


def self_bwd_kernel(x_ref, x1_ref, gx2_ref, gn2_ref, g_ref, n1_ref, *rest):
    weights = rest[0:4]
    sides = (rest[4:10], rest[10:16])
    outs = rest[16:20]
    gd_ref, gg2_ref, gg1_ref, gi_ref, gat_ref, gqt_ref, gk_ref, gv_ref, gx1_ref = rest[20:29]
    held, sems = rest[29:37], rest[37]
    arrivals = [
        pltpu.make_async_copy(src, dst, sems.at[i]) for i, (src, dst) in enumerate(zip((*weights[0:2], *sides[0]), held))
    ]
    for copy in arrivals:
        copy.start()
    weights = (*held[0:2], *weights[2:4])
    sides = (held[2:8], sides[1])
    w = outs[0].shape[0] // 4
    c = 2 * w
    nb = n1_ref.shape[0] // LEN
    gx, gg2 = norm_back(x1_ref[...], g_ref[1:2].astype(f32), gn2_ref[...])
    gx1 = gx2_ref[...] + gx
    gx1_ref[...] = gx1
    gg2_ref[...] = gg2
    go = gx1.astype(bf16)
    ri = lax.broadcasted_iota(jnp.int32, (LEN, LEN), 0)
    ci = lax.broadcasted_iota(jnp.int32, (LEN, LEN), 1)
    flip = jnp.where(ri + ci == LEN - 1, 1.0, 0.0).astype(bf16)
    n1 = n1_ref[...]
    gn = None
    for side in (1, 0):
        if side == 0:
            for copy in arrivals:
                copy.wait()
        shards = weights[2 * side : 2 * side + 2]
        q_ref, k_ref, vt_ref, e_ref, r_ref, at_ref = sides[side]
        gat_ref[...] = nt(side_by_side(shards, 3), go).astype(bf16)
        gwo = nn(at_ref[...], go).astype(bf16)
        for p in range(c // (2 * DH)):
            lanes = slice(p * 2 * DH, (p + 1) * 2 * DH)
            for h in range(2):
                head = side * (c // DH) + 2 * p + h
                gd_ref[head : head + 1, :] = jnp.zeros((1, LEN), f32)
            for b in range(nb):
                tok = slice(b * LEN, (b + 1) * LEN)
                grads, deltas = [], []
                for h in range(2):
                    rows = slice(lanes.start + h * DH, lanes.start + (h + 1) * DH)
                    gah = gat_ref[rows, tok].astype(f32) * r_ref[b, 2 * p + h : 2 * p + h + 1, :]
                    deltas.append(jnp.sum(gah * at_ref[rows, tok].astype(f32), axis=0, keepdims=True))
                    gah = gah.astype(bf16)
                    zero = jnp.zeros_like(gah)
                    grads.append(jnp.concatenate([gah, zero] if h == 0 else [zero, gah], axis=0))
                grads = jnp.concatenate(grads, axis=1)
                delta = jnp.concatenate(deltas, axis=1)
                e = jnp.concatenate([e_ref[b, 2 * p], e_ref[b, 2 * p + 1]], axis=1)
                gs = (e.astype(f32) * (tn(vt_ref[lanes, tok], grads) - delta)).astype(bf16)
                for h in range(2):
                    turned = pltpu.roll(nn(gs[:, h * LEN : (h + 1) * LEN], flip), 0, 1, stride=1, stride_axis=0)
                    head = side * (c // DH) + 2 * p + h
                    gd_ref[head : head + 1, :] += jnp.sum(turned, axis=0, keepdims=True)
                gv_ref[tok, lanes] = nt(e, grads).astype(bf16)
                gk_ref[tok, lanes] = nn(gs, both_heads(q_ref[tok, lanes])).astype(bf16)
                gq = tn(k_ref[tok, lanes], gs)
                gqt_ref[lanes, tok] = jnp.concatenate([gq[0:DH, 0:LEN], gq[DH:, LEN:]], axis=0).astype(bf16)
        gqt = gqt_ref[...]
        gk = gk_ref[...]
        gv = gv_ref[...]
        gwq = nn(gqt, n1).astype(bf16)
        gwk = tn(gk, n1).astype(bf16)
        gwv = tn(gv, n1).astype(bf16)
        for i, gw in enumerate((gwq, gwk, gwv, gwo)):
            for j in range(2):
                outs[2 * side + j][i * w : (i + 1) * w] = gw[j * w : (j + 1) * w]
        part = tn(gqt, side_by_side(shards, 0)) + nn(gk, side_by_side(shards, 1)) + nn(gv, side_by_side(shards, 2))
        gn = part if gn is None else gn + part
    gi, gg1 = norm_back(x_ref[...].astype(f32), g_ref[0:1].astype(f32), gn)
    gi_ref[...] = gx1_ref[...] + gi
    gg1_ref[...] = gg1


def self_bwd(x, x1, gx2, gn2, g, n1, weights, side0, side1):
    t, d = x1.shape
    c = weights[0].shape[0] // 2
    late = pl.BlockSpec(memory_space=pl.ANY)
    args = [x, x1, gx2, gn2, g, n1, *weights, *side0, *side1]
    outs = [jax.ShapeDtypeStruct((2 * c, d), bf16)] * 4 + [
        jax.ShapeDtypeStruct((2 * c // DH, LEN), f32),
        jax.ShapeDtypeStruct((1, d), f32),
        jax.ShapeDtypeStruct((1, d), f32),
        jax.ShapeDtypeStruct((t, d), f32),
    ]
    return call(
        self_bwd_kernel,
        tuple(outs),
        args,
        in_specs=[whole(a.shape) for a in args[:6]]
        + [late] * 2
        + [whole(a.shape) for a in weights[2:4]]
        + [late] * 6
        + [whole(a.shape) for a in side1],
        out_specs=tuple(whole(o.shape) for o in outs),
        scratch=[
            pltpu.VMEM((c, t), bf16),
            pltpu.VMEM((c, t), bf16),
            pltpu.VMEM((t, c), bf16),
            pltpu.VMEM((t, c), bf16),
            pltpu.VMEM((t, d), f32),
        ]
        + [pltpu.VMEM(a.shape, a.dtype) for a in (*weights[0:2], *side0)]
        + [pltpu.SemaphoreType.DMA((8,))],
        vmem=BIG_VMEM,
        name="self_bwd",
    )


def local_program(tensor_size, dp_size, *arrays):
    (block_in, enc_states, dec_len, enc_len, gain_self, self_query, self_key, self_value, self_out, rel_table,
     gain_cross, cross_query, cross_key, cross_value, cross_out, gain_ff, ff_in, ff_out, out_grad) = arrays
    t_index = lax.axis_index("tensor")
    d_index = lax.axis_index("dp")
    nb = block_in.shape[0] // LEN
    w, d = self_out.shape
    heads = w // DH

    def swap(v, axis, bit):
        n = tensor_size if axis == "tensor" else dp_size
        return lax.ppermute(v, axis, [(i, i ^ bit) for i in range(n)])

    def d_bit(bit):
        return (d_index // bit) % 2

    y = d_bit(1).astype(jnp.int32)
    y_is0 = y == 0
    place = jnp.stack([y, (t_index * nb).astype(jnp.int32)])

    def core(v):
        return swap(v, "tensor", 1)

    def over_x(v):
        return swap(v, "tensor", 2)

    def over_y(v):
        return swap(v, "dp", 1)

    def fence(*vals):
        return lax.optimization_barrier(vals)

    gains = jnp.stack([gain_self, gain_cross, gain_ff])

    buckets = np.eye(BUCKETS, dtype=np.float32)[bucket_of_distance()]
    rel_own = jnp.dot(rel_table.astype(f32).T, jnp.asarray(buckets.T), precision=lax.Precision.HIGHEST)
    rel_x = over_x(rel_own)
    own_s = jnp.concatenate([self_query.T, self_key.T, self_value.T, self_out], axis=0)
    x_s = over_x(own_s)
    s_0 = [own_s, core(own_s)]
    bias0 = jnp.concatenate([rel_own, core(rel_own)], axis=0)
    own_c = jnp.concatenate([cross_key.T, cross_value.T, cross_query.T, cross_out], axis=0)
    c_0 = [own_c, core(own_c)]
    out = self_fwd(False, place, dec_len, block_in, gains, s_0, bias0)
    *out, c_0[1] = fence(*out, c_0[1])
    fq0, fk0, fv0, fe0, fr0, fa0, xp = out
    k0, v0 = enc_kv(False, place, enc_states, c_0)
    k0, v0, xp, x_s, rel_x = fence(k0, v0, xp, x_s, rel_x)
    s_1 = [x_s, core(x_s)]
    bias1 = jnp.concatenate([rel_x, core(rel_x)], axis=0)
    half = own_c.shape[0] // 2
    send_c, x_s = fence(jnp.where(y_is0, own_c[:half], own_c[half:]), x_s)
    x_c = over_x(send_c)
    send_f, s_1[1], xp = fence(jnp.where(y_is0, ff_in, ff_out), s_1[1], xp)
    x_f = over_x(send_f)
    out = self_fwd(True, place, dec_len, block_in, gains, s_1, bias1, xp)
    *out, x_c = fence(*out, x_c)
    fq1, fk1, fv1, fe1, fr1, fa1, x1, n1, n2 = out
    y_c, c_c = over_y(x_c), core(x_c)
    cq0, cr0, ca0, x2p = cross_fwd(False, place, enc_len, n2, gains, c_0, k0, v0, x1)
    x2p, y_c, c_c = fence(x2p, y_c, c_c)
    c_1 = [x_c, y_c, c_c, core(y_c)]
    wi1, wo1 = core(ff_in), core(ff_out)
    k1, v1 = enc_kv(True, place, enc_states, c_1)
    k1, v1, x_f = fence(k1, v1, x_f)
    y_f, c_f = over_y(x_f), core(x_f)
    cq1, cr1, ca1, x2, n3 = cross_fwd(True, place, enc_len, n2, gains, c_1, k1, v1, x2p)
    n3, x2, wi1, wo1, c_f = fence(n3, x2, wi1, wo1, c_f)

    rest_size = dp_size // 2
    m = d_index // 2
    rest_groups = [[2 * i + j for i in range(rest_size)] for j in range(2)]

    def plus(*vals):
        total = vals[0].astype(f32)
        for v in vals[1:]:
            total = total + v.astype(f32)
        return total.astype(bf16)

    def pick(v, n, i):
        v = v.reshape((n, v.shape[0] // n) + v.shape[1:])
        return lax.dynamic_index_in_dim(v, i, 0, keepdims=False)

    def ordered(a, b):
        return jnp.where(y_is0, jnp.concatenate([a, b], axis=0), jnp.concatenate([b, a], axis=0))

    def sent_y(*vals):
        return over_y(plus(*[pick(v, 2, 1 - y) for v in vals]))

    def kept_y(*vals):
        return [pick(v, 2, y) for v in vals]

    z_bits = [1 << i for i in range(1, dp_size.bit_length() - 1)]

    def reversed_bits(i):
        return sum(((i >> a) & 1) << (len(z_bits) - 1 - a) for a in range(len(z_bits)))

    def stage_z_reversed(v):
        return [pick(v, rest_size, reversed_bits(m))] + [
            swap(pick(v, rest_size, reversed_bits(m ^ j)), "dp", 2 * j) for j in range(1, rest_size)
        ]

    def in_order(v, got, bit):
        low = d_bit(bit) == 0
        return jnp.where(low, jnp.concatenate([v, got], axis=0), jnp.concatenate([got, v], axis=0))

    def sum_ordered(parts):
        while len(parts) > 1:
            parts = [a + b for a, b in zip(parts[0::2], parts[1::2])]
        return parts[0]

    def stage_z(v):
        return [pick(v, rest_size, m)] + [swap(pick(v, rest_size, m ^ j), "dp", 2 * j) for j in range(1, rest_size)]

    def stage_z_back(v):
        return [v] + [swap(v, "dp", 2 * j) for j in range(1, rest_size)]

    def ordered_z(parts):
        bit = 1
        while len(parts) > 1:
            low = (m // bit) % 2 == 0
            parts = [
                jnp.where(low, jnp.concatenate([a, b], axis=0), jnp.concatenate([b, a], axis=0))
                for a, b in zip(parts[0::2], parts[1::2])
            ]
            bit *= 2
        return parts[0]

    gwi0, gwo0, gwi1, gwo1, yp, gp = ff(False, place, n3, out_grad, [ff_in, ff_out, wi1, wo1])
    yp, y_f = fence(yp, y_f)
    a1, b1 = core(gwo1), core(gwi1)
    f_1 = [x_f, y_f, c_f, core(y_f)]
    out = ff(True, place, n3, out_grad, f_1, yp, gp, x2, gains)
    *out, a1, b1 = fence(*out, a1, b1)
    gwi2, gwo2, gwi3, gwo3, block_out, gx2, go2, gg3 = out
    a3, b3 = core(gwo3), core(gwi3)
    a3, b3, go2 = fence(a3, b3, go2)
    wo_s = plus(gwo2, a3)
    wi_send = jnp.concatenate(
        [plus(pick(gwi0, 2, 1 - y), pick(b1, 2, 1 - y)), plus(pick(gwi2, 2, 1 - y), pick(b3, 2, 1 - y))], axis=0
    )
    wo_s, wi_send, go2 = fence(wo_s, wi_send, go2)
    xo = over_x(wo_s)
    ywi = over_y(wi_send)
    out = cross_bwd(place, enc_len, go2, n2, c_0, c_1, (cq0, k0, v0, cr0, ca0), (cq1, k1, v1, cr1, ca1))
    *out, xo, ywi = fence(*out, xo, ywi)
    gk0, gv0, gk1, gv1, gqo0, gqo1, gqo2, gqo3, gn2 = out
    c3 = core(gqo3)
    hid = gwi0.shape[0] // 2
    wi_x = plus(pick(gwi2, 2, y), pick(b3, 2, y), ywi[hid:])
    wo_y = plus(*[pick(v, 2, 1 - y) for v in (gwo0, a1, xo)])
    wi_x, wo_y, c3, gk0 = fence(wi_x, wo_y, c3, gk0)
    xwi, ywo = over_x(wi_x), over_y(wo_y)
    qo_x, gk0 = fence(plus(gqo2, c3), gk0)
    xqo = over_x(qo_x)
    grad_enc, gkv2, gkv3, gkv0, gkv1 = enc_grad(place, enc_states, gk1, gv1, gk0, gv0, c_0, c_1)
    gkv3, gn2, xwi, ywo = fence(gkv3, gn2, xwi, ywo)
    k3, k1, c1 = core(gkv3), core(gkv1), core(gqo1)
    f_u = jnp.concatenate(
        [plus(*kept_y(gwo0, a1, xo), ywo), plus(*kept_y(gwi0, b1), ywi[:hid], xwi)], axis=0
    )
    f_u, k3, k1, gn2 = fence(f_u, k3, k1, gn2)
    kv_x, gn2 = fence(plus(gkv2, k3), gn2)
    xkv = over_x(kv_x)
    zf = stage_z_reversed(f_u)
    out = self_bwd(
        block_in, x1, gx2, gn2, gains, n1, [*s_0, *s_1], (fq0, fk0, fv0, fe0, fr0, fa0), (fq1, fk1, fv1, fe1, fr1, fa1)
    )
    gs0, gs1, gs2, gs3, gd, gg2, gg1, grad_in = out
    gs0, gs3, gd, gg1, xqo, xkv, c1, *zf = fence(gs0, gs3, gd, gg1, xqo, xkv, c1, *zf)
    s3 = core(gs3)
    qo_t, kv_t = (gqo0, c1, xqo), (gkv0, k1, xkv)
    c_y = plus(*[jnp.where(y_is0, b_, a_) for a_, b_ in zip(qo_t, kv_t)])
    f_w = plus(*zf)
    s3, c_y, f_w = fence(s3, c_y, f_w)
    s_x = plus(gs2, s3)
    s_x, c_y, f_w, gs1, gd, gg1 = fence(s_x, c_y, f_w, gs1, gd, gg1)
    xs = over_x(s_x)
    yc = over_y(c_y)
    for bit in z_bits[:1:-1]:
        f_w = in_order(f_w, swap(f_w, "dp", bit), bit)
    f_got = swap(f_w, "dp", z_bits[1])
    s1 = core(gs1)
    flipped = jnp.asarray(np.ascontiguousarray(buckets[::-1]))
    grel = jnp.dot(gd, flipped, precision=lax.Precision.HIGHEST)
    grel = grel.reshape(tensor_size, heads * BUCKETS)
    slots = jnp.arange(tensor_size)[:, None] ^ t_index
    order = (slots == jnp.arange(tensor_size)[None, :]).astype(f32)
    grel = jnp.dot(order.T, grel, precision=lax.Precision.HIGHEST)
    grel = jnp.pad(grel.reshape(1, -1), ((0, 0), (0, d - grel.size)))
    small = jnp.concatenate([gg1, gg2, gg3, grel], axis=0)
    small_got = core(small)
    yc, small_got, s1, xs, f_got = fence(yc, small_got, s1, xs, f_got)
    ys = sent_y(gs0, s1, xs)
    zc = stage_z(plus(*[jnp.where(y_is0, a_, b_) for a_, b_ in zip(qo_t, kv_t)], yc))
    small = small + small_got
    small_got = over_x(small)
    f_w = in_order(f_w, f_got, z_bits[1])
    f_got = swap(f_w, "dp", 2)
    ys, small_got, *zc = fence(ys, small_got, *zc)
    zs = stage_z(plus(*kept_y(gs0, s1, xs), ys))
    small = small + small_got
    small_got = over_y(small)
    c_w = plus(*zc)
    small_got, c_w, f_got, *zs = fence(small_got, c_w, f_got, *zs)
    f_v = in_order(f_w, f_got, 2)
    f_f = over_y(f_v)
    bc = stage_z_back(c_w)
    bit = 2
    small = small + small_got
    small_got = swap(small, "dp", bit)
    bs = stage_z_back(plus(*zs))
    both = fence(small_got, *bs, *bc)
    small_got, bs, bc = both[0], both[1 : 1 + rest_size], both[1 + rest_size :]
    small = small + small_got
    while 2 * bit < dp_size:
        bit *= 2
        small = small + swap(small, "dp", bit)
    c_v = ordered_z(bc)
    c_f = over_y(c_v)
    s_v = ordered_z(bs)
    s_f = over_y(s_v)
    n_f = f_v.shape[0] // 2
    r_wo = ordered(f_v[:n_f], f_f[:n_f]).astype(f32)
    r_wi = ordered(f_v[n_f:], f_f[n_f:]).astype(f32)
    s_f, r_wo, r_wi = fence(s_f, r_wo, r_wi)
    r_s = ordered(s_v, s_f)
    g_s = [r_s[i * w : (i + 1) * w].astype(f32) for i in range(4)]
    c_f, *g_s = fence(c_f, *g_s)
    c_w = [jnp.where(y_is0, a_, b_) for a_, b_ in ((c_v, c_f), (c_f, c_v))]
    g_c = [v[i * w : (i + 1) * w].astype(f32) for v in c_w for i in range(2)]
    grad_rel = lax.dynamic_slice(small[3], (t_index * heads * BUCKETS,), (heads * BUCKETS,)).reshape(heads, BUCKETS).T

    return (
        block_out,
        grad_in,
        grad_enc,
        small[0],
        g_s[0].T,
        g_s[1].T,
        g_s[2].T,
        g_s[3],
        grad_rel,
        small[1],
        g_c[0].T,
        g_c[2].T,
        g_c[3].T,
        g_c[1],
        small[2],
        r_wi,
        r_wo,
    )


def solution(mesh):
    tensor_size = mesh.shape["tensor"]
    dp_size = mesh.shape["dp"]
    both = P(("dp", "tensor"), None)
    col = P(None, "tensor")
    row = P("tensor", None)
    placed = (both, both, P("dp"), P("dp"), P(), col, col, col, row, col, P(), col, col, col, row, P(), col, row, both)
    outs = (both, both, both, P(), col, col, col, row, col, P(), col, col, col, row, P(), col, row)
    return jax.shard_map(
        lambda *a: local_program(tensor_size, dp_size, *a),
        mesh=mesh,
        in_specs=placed,
        out_specs=outs,
        check_vma=False,
    )
```

```python
import math

import jax
import jax.numpy as jnp
import numpy as np
from jax import lax
from jax.experimental import pallas as pl
from jax.experimental.pallas import tpu as pltpu
from jax.sharding import PartitionSpec as P

BUCKETS = 32
MAX_DIST = 128
LEN = 256
ENC = 1024
DH = 64
KEYS = 256

norm_eps = 1e-06
masked_score = -1000000000.0
bf16 = jnp.bfloat16
f32 = jnp.float32
VMEM_CAP = 16 << 20
BIG_VMEM = 58 << 20


def bucket_of_distance():
    half_count = BUCKETS // 2
    growth_ratio = MAX_DIST / half_count
    limits = np.array(
        [int(math.ceil(half_count * growth_ratio ** (m / half_count))) for m in range(1, half_count)],
        dtype=np.int32,
    )
    distance = np.arange(LEN, dtype=np.int32)
    above = np.sum(distance[:, None] >= limits[None, :], axis=1)
    return np.where(distance < half_count, distance, half_count + above).astype(np.int32)


def nn(a, b):
    return lax.dot_general(a, b, (((1,), (0,)), ((), ())), preferred_element_type=f32)


def nt(a, b):
    return lax.dot_general(a, b, (((1,), (1,)), ((), ())), preferred_element_type=f32)


def tn(a, b):
    return lax.dot_general(a, b, (((0,), (0,)), ((), ())), preferred_element_type=f32)


def inv_rms(v):
    return lax.rsqrt(jnp.mean(v * v, axis=-1, keepdims=True) + norm_eps)


def normed(v, gain):
    return (v * inv_rms(v) * gain).astype(bf16)


def norm_back(v, gain, e):
    s = inv_rms(v)
    ge = gain * e
    dot = jnp.mean(ge * v, axis=-1, keepdims=True)
    grad_v = s * ge - v * (s * s * s * dot)
    grad_gain = jnp.sum(e * v * s, axis=0, keepdims=True)
    return grad_v, grad_gain


def lane_half(shape, h):
    lane = lax.broadcasted_iota(jnp.int32, shape, 1)
    return (lane < DH) if h == 0 else (lane >= DH)


def both_heads(rows):
    zero = jnp.zeros_like(rows)
    return jnp.concatenate([jnp.where(lane_half(rows.shape, h), rows, zero) for h in range(2)], axis=0)


def call(kernel, out_shape, args, *, grid=(), in_specs=None, out_specs=None, scratch=(), flops=0, nbytes=0, trans=0, name=None, vmem=VMEM_CAP):
    kw = {}
    if in_specs is not None:
        kw["in_specs"] = in_specs
    if out_specs is not None:
        kw["out_specs"] = out_specs
    return pl.pallas_call(
        kernel,
        out_shape=out_shape,
        grid=grid,
        scratch_shapes=scratch,
        compiler_params=pltpu.CompilerParams(vmem_limit_bytes=vmem),
        cost_estimate=pl.CostEstimate(flops=1, bytes_accessed=1, transcendentals=0),
        name=name,
        **kw,
    )(*args)


def whole(shape):
    return pl.BlockSpec(shape, lambda *_: (0,) * len(shape))


SMEM = pl.BlockSpec(memory_space=pltpu.SMEM)


def side_by_side(refs, i):
    w = refs[0].shape[0] // 4
    return jnp.concatenate([r[i * w : (i + 1) * w] for r in refs], axis=0)


def pair_rows(y_ref, refs, shared):
    def rows(i):
        if not shared:
            return side_by_side(refs, i)
        w = refs[0].shape[0] // 2
        first = y_ref[0] == i // 2
        part = slice((i % 2) * w, (i % 2 + 1) * w)
        return jnp.concatenate(
            [jnp.where(first, refs[0][part], refs[1][part]), jnp.where(first, refs[2][part], refs[3][part])], axis=0
        )

    return rows


def self_fwd_kernel(last, y_ref, len_ref, x_ref, g_ref, *rest):
    weights = rest[0:2]
    bias_ref = rest[2]
    rest = rest[3:]
    if last:
        xin_ref, q_ref, k_ref, vt_ref, e_ref, r_ref, at_ref, x1_ref, n1_ref, n2_ref, bs_ref = rest
    else:
        q_ref, k_ref, vt_ref, e_ref, r_ref, at_ref, x1_ref, bs_ref = rest
    nh = q_ref.shape[1] // DH
    nb = x_ref.shape[0] // LEN
    x = x_ref[...].astype(f32)
    n1 = normed(x, g_ref[0:1].astype(f32))
    if last:
        n1_ref[...] = n1

    q_ref[...] = nt(n1, side_by_side(weights, 0)).astype(bf16)
    k_ref[...] = nt(n1, side_by_side(weights, 1)).astype(bf16)
    vt_ref[...] = nt(side_by_side(weights, 2), n1).astype(bf16)
    key = lax.broadcasted_iota(jnp.int32, (LEN, 2 * LEN), 0)
    query = lax.broadcasted_iota(jnp.int32, (LEN, 2 * LEN), 1)
    query = jnp.where(query < LEN, query, query - LEN)
    for p in range(nh // 2):
        lanes = slice(p * 2 * DH, (p + 1) * 2 * DH)
        for h in range(2):
            row = jnp.broadcast_to(bias_ref[2 * p + h : 2 * p + h + 1, :], (LEN, LEN))
            bs_ref[:, h * LEN : (h + 1) * LEN] = pltpu.roll(row, 0, 1, stride=1, stride_axis=0)
        for b in range(nb):
            tok = slice(b * LEN, (b + 1) * LEN)
            allowed = (key <= query) & (key < len_ref[y_ref[1] + b])
            s = nt(k_ref[tok, lanes], both_heads(q_ref[tok, lanes])) + bs_ref[...]
            s = jnp.where(allowed, s, masked_score)
            e = jnp.exp(s - jnp.max(s, axis=0, keepdims=True))
            r = 1.0 / jnp.sum(e, axis=0, keepdims=True)
            e = e.astype(bf16)
            outs = []
            for h in range(2):
                head = 2 * p + h
                half = slice(h * LEN, (h + 1) * LEN)
                e_ref[b, head] = e[:, half]
                r_ref[b, head : head + 1, :] = r[:, half]
                outs.append(nn(vt_ref[head * DH : (head + 1) * DH, tok], e[:, half]) * r[:, half])
            at_ref[lanes, tok] = jnp.concatenate(outs, axis=0).astype(bf16)
    mixed = tn(at_ref[...], side_by_side(weights, 3))
    if last:
        x1 = xin_ref[...] + mixed
        n2_ref[...] = normed(x1, g_ref[1:2].astype(f32))
    else:
        x1 = x + mixed
    x1_ref[...] = x1


def self_fwd(last, y, lens, x, g, weights, bias, xin=None):
    t, d = x.shape
    w = weights[0].shape[0] // 4
    c = 2 * w
    nh = c // DH
    nb = t // LEN
    outs = [
        jax.ShapeDtypeStruct((t, c), bf16),
        jax.ShapeDtypeStruct((t, c), bf16),
        jax.ShapeDtypeStruct((c, t), bf16),
        jax.ShapeDtypeStruct((nb, nh, LEN, LEN), bf16),
        jax.ShapeDtypeStruct((nb, nh, LEN), f32),
        jax.ShapeDtypeStruct((c, t), bf16),
        jax.ShapeDtypeStruct((t, d), f32),
    ]
    args = [y, lens, x, g, *weights, bias]
    if last:
        args.append(xin)
        outs += [jax.ShapeDtypeStruct((t, d), bf16)] * 2
    flops = 2 * t * d * c * 4 + 2 * t * LEN * nh * 128 * 2
    return call(
        lambda *r: self_fwd_kernel(last, *r),
        tuple(outs),
        args,
        in_specs=[SMEM, SMEM] + [whole(a.shape) for a in args[2:]],
        out_specs=tuple(whole(o.shape) for o in outs),
        scratch=[pltpu.VMEM((LEN, 2 * LEN), f32)],
        flops=flops * 3,
        nbytes=12 * 1024 * 1024,
        trans=t * LEN * nh,
        name="self_fwd",
    )


def enc_kv_kernel(shared, y_ref, enc_ref, *rest):
    k_ref, v_ref = rest[-2:]
    enc = enc_ref[...]
    rows = pair_rows(y_ref, rest[:-2], shared)
    k_ref[...] = nt(enc, rows(0)).astype(bf16)
    v_ref[...] = nt(enc, rows(1)).astype(bf16)


def enc_kv(shared, y, enc, kv):
    t, d = enc.shape
    c = kv[0].shape[0] if shared else kv[0].shape[0] // 2
    rows = 512
    half = pl.BlockSpec((rows, c), lambda i: (i, 0))
    return call(
        lambda *r: enc_kv_kernel(shared, *r),
        (jax.ShapeDtypeStruct((t, c), bf16),) * 2,
        (y, enc, *kv),
        grid=(t // rows,),
        in_specs=[SMEM, pl.BlockSpec((rows, d), lambda i: (i, 0))] + [whole(a.shape) for a in kv],
        out_specs=(half, half),
        flops=2 * t * d * c * 2 * 2,
        nbytes=t * d * 2 + 4 * t * c * 2,
        name="enc_kv",
    )


def cross_fwd_kernel(last, pairs, y_ref, len_ref, n2_ref, g_ref, *rest):
    n_w = 4 if last else 2
    weights = pair_rows(y_ref, rest[:n_w], last)
    k_ref, v_ref, xin_ref = rest[n_w : n_w + 3]
    rest = rest[n_w + 3 :]
    if last:
        q_ref, r_ref, at_ref, x2_ref, n3_ref, s_ref, e_ref = rest
    else:
        q_ref, r_ref, at_ref, x2_ref, s_ref, e_ref = rest
    step = pl.program_id(0)
    b = step // pairs
    p = lax.rem(step, pairs)

    @pl.when(step == 0)
    def _():
        q_ref[...] = nt(n2_ref[...], weights(2)).astype(bf16)

    tok = pl.ds(pl.multiple_of(b * LEN, LEN), LEN)
    lanes = pl.ds(pl.multiple_of(p * 2 * DH, 2 * DH), 2 * DH)
    qp = q_ref[tok, lanes]
    count = len_ref[y_ref[1] + b]
    key = lax.broadcasted_iota(jnp.int32, (KEYS, 2 * LEN), 0)
    queries = both_heads(qp)
    top = None
    for c in range(ENC // KEYS):
        part = slice(c * KEYS, (c + 1) * KEYS)
        s = jnp.where(key < count - c * KEYS, nt(k_ref[part], queries), masked_score)
        s_ref[part] = s
        t = jnp.max(s.reshape(KEYS // 8, 8, 2 * LEN), axis=0)
        top = t if c == 0 else jnp.maximum(top, t)
    top = jnp.max(top, axis=0, keepdims=True)
    total = None
    for c in range(ENC // KEYS):
        part = slice(c * KEYS, (c + 1) * KEYS)
        e = jnp.exp(s_ref[part] - top)
        t = jnp.sum(e.reshape(KEYS // 8, 8, 2 * LEN), axis=0)
        total = t if c == 0 else total + t
        e_ref[part] = e.astype(bf16)
    r = 1.0 / jnp.sum(total, axis=0, keepdims=True)
    mixed = tn(v_ref[...], e_ref[...]) * r
    outs = []
    for h in range(2):
        half = slice(h * LEN, (h + 1) * LEN)
        r_ref[0, h : h + 1, :] = r[:, half]
        r_ref[0, 2 + h : 3 + h, :] = top[:, half]
        outs.append(mixed[h * DH : (h + 1) * DH, half])
    at_ref[lanes, tok] = jnp.concatenate(outs, axis=0).astype(bf16)

    @pl.when(step == pl.num_programs(0) - 1)
    def _():
        x2 = xin_ref[...] + tn(at_ref[...], weights(3))
        x2_ref[...] = x2
        if last:
            n3_ref[...] = normed(x2, g_ref[2:3].astype(f32))


def cross_fwd(last, y, lens, n2, g, qo, k, v, xin):
    t, d = n2.shape
    c = k.shape[1]
    nb = t // LEN
    pairs = c // (2 * DH)
    outs = [
        jax.ShapeDtypeStruct((t, c), bf16),
        jax.ShapeDtypeStruct((nb * pairs, 4, LEN), f32),
        jax.ShapeDtypeStruct((c, t), bf16),
        jax.ShapeDtypeStruct((t, d), f32),
    ]
    specs = [
        whole((t, c)),
        pl.BlockSpec((1, 4, LEN), lambda i: (i, 0, 0)),
        whole((c, t)),
        whole((t, d)),
    ]
    if last:
        outs.append(jax.ShapeDtypeStruct((t, d), bf16))
        specs.append(whole((t, d)))
    return call(
        lambda *r: cross_fwd_kernel(last, pairs, *r),
        tuple(outs),
        (y, lens, n2, g, *qo, k, v, xin),
        grid=(nb * pairs,),
        in_specs=[
            SMEM,
            SMEM,
            whole(n2.shape),
            whole(g.shape),
            *[whole(a.shape) for a in qo],
            pl.BlockSpec((ENC, 2 * DH), lambda i: (i // pairs, i % pairs)),
            pl.BlockSpec((ENC, 2 * DH), lambda i: (i // pairs, i % pairs)),
            whole(xin.shape),
        ],
        out_specs=tuple(specs),
        scratch=[pltpu.VMEM((ENC, 2 * LEN), f32), pltpu.VMEM((ENC, 2 * LEN), bf16)],
        flops=3 * (2 * t * d * c * 2 + 2 * t * ENC * c * 2 * 2),
        nbytes=14 * 1024 * 1024,
        trans=t * ENC * (c // DH),
        name="cross_fwd",
    )


ROOT = math.sqrt(2.0 / math.pi)
CUBE = 0.044715


def ff_kernel(last, y_ref, n3_ref, gf_ref, *rest):
    if last:
        ha_in, ha_out, ga_in, ga_out, hb_in, hb_out, gb_in, gb_out = rest[:8]
        rest = rest[8:]
        first = y_ref[0] == 0

        def weights(h_in, h_out, g_in, g_out):
            return (
                lambda: jnp.where(first, h_in[...], g_in[...]),
                lambda: jnp.where(first, g_out[...], h_out[...]),
            )

        shards = (weights(ha_in, ha_out, ga_in, ga_out), weights(hb_in, hb_out, gb_in, gb_out))
    else:
        wia_ref, woa_ref, wib_ref, wob_ref = rest[:4]
        rest = rest[4:]
        shards = ((lambda: wia_ref[...], lambda: woa_ref[...]), (lambda: wib_ref[...], lambda: wob_ref[...]))
    if last:
        yin_ref, gin_ref, x2_ref, g_ref = rest[:4]
        gwia, gwoa, gwib, gwob, out_ref, gx2_ref, go2_ref, gg_ref, y_acc, gn_ref, n3t_ref = rest[4:]
    else:
        gwia, gwoa, gwib, gwob, y_acc, gn_ref, n3t_ref = rest
    step = pl.program_id(0)

    @pl.when(step == 0)
    def _():
        n3t_ref[...] = n3_ref[...].T
        if last:
            y_acc[...] = yin_ref[...]
            gn_ref[...] = gin_ref[...]
        else:
            y_acc[...] = jnp.zeros_like(y_acc)
            gn_ref[...] = jnp.zeros_like(gn_ref)

    n3 = n3_ref[...]
    gf = gf_ref[...]
    kept = []
    for (get_wi, get_wo), gwi, gwo in zip(shards, (gwia, gwib), (gwoa, gwob)):
        wi, wo = get_wi(), get_wo()
        u = nn(n3, wi)
        dh = nt(gf, wo)
        u2 = u * u
        th = jnp.tanh(ROOT * u * (1.0 + CUBE * u2))
        half = 0.5 * (1.0 + th)
        r = (u * half).astype(bf16)
        slope = half + 0.5 * u * (1.0 - th * th) * (ROOT * (1.0 + (3.0 * CUBE) * u2))
        gu = (dh * slope).astype(bf16)
        kept.append((r, wo, gu, wi))
        gwo[...] = tn(r, gf).astype(bf16)
        gwi[...] = nn(n3t_ref[...], gu).astype(bf16)
    r, wo, gu, wi = [jnp.concatenate(v, axis=a) for v, a in zip(zip(*kept), (1, 0, 1, 1))]
    y_acc[...] += nn(r, wo)
    gn_ref[...] += nt(gu, wi)

    if last:

        @pl.when(step == pl.num_programs(0) - 1)
        def _():
            x2 = x2_ref[...]
            out_ref[...] = (x2 + y_acc[...]).astype(bf16)
            gx, gg = norm_back(x2, g_ref[2:3].astype(f32), gn_ref[...])
            gx2 = gf.astype(f32) + gx
            gx2_ref[...] = gx2
            go2_ref[...] = gx2.astype(bf16)
            gg_ref[...] = gg


def ff(last, y, n3, gf, weights, yin=None, gin=None, x2=None, g=None):
    t, d = n3.shape
    hid = weights[0].shape[1]
    blk = 256
    args = [y, n3, gf]
    col = pl.BlockSpec((d, blk), lambda i: (0, i))
    row = pl.BlockSpec((blk, d), lambda i: (i, 0))
    in_specs = [SMEM, whole((t, d)), whole((t, d))]
    if last:
        for v in weights:
            args += [v, v]
            in_specs += [col, row]
    else:
        args += weights
        in_specs += [col, row, col, row]
    outs = [jax.ShapeDtypeStruct((d, hid), bf16), jax.ShapeDtypeStruct((hid, d), bf16)] * 2
    specs = [col, row, col, row]
    acc = jax.ShapeDtypeStruct((t, d), f32)
    scratch = [pltpu.VMEM((d, t), bf16)]
    if last:
        args += [yin, gin, x2, g]
        in_specs += [whole((t, d))] * 3 + [whole(g.shape)]
        outs += [jax.ShapeDtypeStruct((t, d), bf16), acc, jax.ShapeDtypeStruct((t, d), bf16), jax.ShapeDtypeStruct((1, d), f32)]
        specs += [whole((t, d))] * 3 + [whole((1, d))]
        scratch = [pltpu.VMEM((t, d), f32)] * 2 + scratch
    else:
        outs += [acc, acc]
        specs += [whole((t, d))] * 2
    return call(
        lambda *r: ff_kernel(last, *r),
        tuple(outs),
        args,
        grid=(hid // blk,),
        in_specs=in_specs,
        out_specs=tuple(specs),
        scratch=scratch,
        flops=2 * 6 * 2 * t * d * hid * 2,
        nbytes=12 * 1024 * 1024,
        trans=2 * t * hid,
        vmem=20 << 20,
        name="ff",
    )


def cross_bwd_kernel(pairs, steps, y_ref, len_ref, go_ref, n2_ref, *rest):
    weights = (pair_rows(y_ref, rest[0:2], False), pair_rows(y_ref, rest[2:6], True))
    sides = (rest[6:11], rest[11:16])
    gk0, gv0, gk1, gv1, outs, gn_ref, gat_ref, gqt_ref, e_ref, gs_ref = *rest[16:20], rest[20:24], *rest[24:]
    w = outs[0].shape[0] // 2
    step = pl.program_id(0)
    key = lax.broadcasted_iota(jnp.int32, (KEYS, 2 * LEN), 0)

    def half(side, local, gk_ref, gv_ref):
        q_ref, k_ref, v_ref, r_ref, at_ref = sides[side]
        b = local // pairs
        p = lax.rem(local, pairs)

        @pl.when(local == 0)
        def _():
            gat_ref[...] = nt(weights[side](3), go_ref[...]).astype(bf16)

        tok = pl.ds(pl.multiple_of(b * LEN, LEN), LEN)
        lanes = pl.ds(pl.multiple_of(p * 2 * DH, 2 * DH), 2 * DH)
        qp = q_ref[tok, lanes]
        ga_t = gat_ref[lanes, tok]
        a_t = at_ref[lanes, tok]
        count = len_ref[y_ref[1] + b]
        grads, deltas = [], []
        for h in range(2):
            part = slice(h * DH, (h + 1) * DH)
            gah = ga_t[part].astype(f32) * r_ref[0, h : h + 1, :]
            deltas.append(jnp.sum(gah * a_t[part].astype(f32), axis=0, keepdims=True))
            gah = gah.astype(bf16)
            zero = jnp.zeros_like(gah)
            grads.append(jnp.concatenate([gah, zero] if h == 0 else [zero, gah], axis=0))
        grads = jnp.concatenate(grads, axis=1)
        delta = jnp.concatenate(deltas, axis=1)
        top = jnp.concatenate([r_ref[0, 2:3, :], r_ref[0, 3:4, :]], axis=1)
        queries = both_heads(qp)
        for c in range(ENC // KEYS):
            part = slice(c * KEYS, (c + 1) * KEYS)
            s = jnp.where(key < count - c * KEYS, nt(k_ref[part], queries), masked_score)
            e = jnp.exp(s - top)
            gs_ref[part] = (e * (nn(v_ref[part], grads) - delta)).astype(bf16)
            e_ref[part] = e.astype(bf16)
        gv_ref[...] = nt(e_ref[...], grads).astype(bf16)
        gk_ref[...] = nn(gs_ref[...], queries).astype(bf16)
        gq = tn(k_ref[...], gs_ref[...])
        gqt_ref[lanes, tok] = jnp.concatenate([gq[0:DH, 0:LEN], gq[DH:, LEN:]], axis=0).astype(bf16)

        @pl.when(local == steps - 1)
        def _():
            gqt = gqt_ref[...]
            gwq = nn(gqt, n2_ref[...]).astype(bf16)
            gwo = nn(at_ref[...], go_ref[...]).astype(bf16)
            for i in range(2):
                outs[2 * side + i][0:w] = gwq[i * w : (i + 1) * w]
                outs[2 * side + i][w:] = gwo[i * w : (i + 1) * w]
            gn = tn(gqt, weights[side](2))
            gn_ref[...] = gn if side == 1 else gn_ref[...] + gn

    @pl.when(step < steps)
    def _():
        half(1, step, gk1, gv1)

    @pl.when(step >= steps)
    def _():
        half(0, step - steps, gk0, gv0)


def cross_bwd(y, lens, go, n2, w0, w1, side0, side1):
    t, d = go.shape
    te, c = side0[1].shape
    nb = t // LEN
    pairs = c // (2 * DH)
    steps = nb * pairs

    def early(i):
        return jnp.minimum(i, steps - 1)

    def late(i):
        return jnp.maximum(i - steps, 0)

    def tokhead(when):
        return pl.BlockSpec((ENC, 2 * DH), lambda i: (when(i) // pairs, when(i) % pairs))

    def side_specs(when):
        return [whole((t, c)), tokhead(when), tokhead(when), pl.BlockSpec((1, 4, LEN), lambda i: (when(i), 0, 0)), whole((c, t))]

    grad = jax.ShapeDtypeStruct((te, c), bf16)
    out = jax.ShapeDtypeStruct((c, d), bf16)
    return call(
        lambda *r_: cross_bwd_kernel(pairs, steps, *r_),
        (grad,) * 4 + (out,) * 4 + (jax.ShapeDtypeStruct((t, d), f32),),
        (y, lens, go, n2, *w0, *w1, *side0, *side1),
        grid=(2 * steps,),
        in_specs=[SMEM, SMEM, whole((t, d)), whole((t, d))]
        + [whole(a.shape) for a in (*w0, *w1)]
        + side_specs(late)
        + side_specs(early),
        out_specs=(tokhead(late), tokhead(late), tokhead(early), tokhead(early)) + (whole((c, d)),) * 4 + (whole((t, d)),),
        scratch=[
            pltpu.VMEM((c, t), bf16),
            pltpu.VMEM((c, t), bf16),
            pltpu.VMEM((ENC, 2 * LEN), bf16),
            pltpu.VMEM((ENC, 2 * LEN), bf16),
        ],
        vmem=BIG_VMEM,
        name="cross_bwd",
    )


def enc_grad_kernel(y_ref, enc_ref, gk1_ref, gv1_ref, gk0_ref, gv0_ref, *rest):
    w0 = pair_rows(y_ref, rest[0:2], False)
    w1 = pair_rows(y_ref, rest[2:6], True)
    out_ref, outs, accs_ref = rest[6], rest[7:11], rest[11]
    w = outs[0].shape[0] // 2
    step = pl.program_id(0)
    enc = enc_ref[...]
    grads = [g[...] for g in (gk1_ref, gv1_ref, gk0_ref, gv0_ref)]
    rhs = jnp.concatenate([w1(0), w1(1), w0(0), w0(1)], axis=0)
    out_ref[...] = nn(jnp.concatenate(grads, axis=1), rhs)
    terms = [tn(g, enc) for g in grads]

    @pl.when(step == 0)
    def _():
        for i in range(4):
            accs_ref[i] = terms[i]

    @pl.when(step != 0)
    def _():
        for i in range(4):
            accs_ref[i] += terms[i]

    @pl.when(step == pl.num_programs(0) - 1)
    def _():
        for pair in range(2):
            for i in range(2):
                acc = accs_ref[2 * pair + i]
                outs[2 * pair][i * w : (i + 1) * w] = acc[0:w].astype(bf16)
                outs[2 * pair + 1][i * w : (i + 1) * w] = acc[w:].astype(bf16)


def enc_grad(y, enc, gk1, gv1, gk0, gv0, w0, w1):
    te, d = enc.shape
    c = gk1.shape[1]
    rows = 512
    half = pl.BlockSpec((rows, c), lambda i: (i, 0))
    block = pl.BlockSpec((rows, d), lambda i: (i, 0))
    out = jax.ShapeDtypeStruct((c, d), bf16)
    return call(
        enc_grad_kernel,
        (jax.ShapeDtypeStruct((te, d), f32),) + (out,) * 4,
        (y, enc, gk1, gv1, gk0, gv0, *w0, *w1),
        grid=(te // rows,),
        in_specs=[SMEM, block] + [half] * 4 + [whole(a.shape) for a in (*w0, *w1)],
        out_specs=(block,) + (whole((c, d)),) * 4,
        scratch=[pltpu.VMEM((4, c, d), f32)],
        vmem=BIG_VMEM,
        name="enc_grad",
    )


def self_bwd_kernel(x_ref, x1_ref, gx2_ref, gn2_ref, g_ref, n1_ref, *rest):
    weights = rest[0:4]
    sides = (rest[4:10], rest[10:16])
    outs = rest[16:20]
    gd_ref, gg2_ref, gg1_ref, gi_ref, gat_ref, gqt_ref, gk_ref, gv_ref, gx1_ref = rest[20:29]
    held, sems = rest[29:37], rest[37]
    arrivals = [
        pltpu.make_async_copy(src, dst, sems.at[i]) for i, (src, dst) in enumerate(zip((*weights[0:2], *sides[0]), held))
    ]
    for copy in arrivals:
        copy.start()
    weights = (*held[0:2], *weights[2:4])
    sides = (held[2:8], sides[1])
    w = outs[0].shape[0] // 4
    c = 2 * w
    nb = n1_ref.shape[0] // LEN
    gx, gg2 = norm_back(x1_ref[...], g_ref[1:2].astype(f32), gn2_ref[...])
    gx1 = gx2_ref[...] + gx
    gx1_ref[...] = gx1
    gg2_ref[...] = gg2
    go = gx1.astype(bf16)
    ri = lax.broadcasted_iota(jnp.int32, (LEN, LEN), 0)
    ci = lax.broadcasted_iota(jnp.int32, (LEN, LEN), 1)
    flip = jnp.where(ri + ci == LEN - 1, 1.0, 0.0).astype(bf16)
    n1 = n1_ref[...]
    gn = None
    for side in (1, 0):
        if side == 0:
            for copy in arrivals:
                copy.wait()
        shards = weights[2 * side : 2 * side + 2]
        q_ref, k_ref, vt_ref, e_ref, r_ref, at_ref = sides[side]
        gat_ref[...] = nt(side_by_side(shards, 3), go).astype(bf16)
        gwo = nn(at_ref[...], go).astype(bf16)
        for p in range(c // (2 * DH)):
            lanes = slice(p * 2 * DH, (p + 1) * 2 * DH)
            for h in range(2):
                head = side * (c // DH) + 2 * p + h
                gd_ref[head : head + 1, :] = jnp.zeros((1, LEN), f32)
            for b in range(nb):
                tok = slice(b * LEN, (b + 1) * LEN)
                grads, deltas = [], []
                for h in range(2):
                    rows = slice(lanes.start + h * DH, lanes.start + (h + 1) * DH)
                    gah = gat_ref[rows, tok].astype(f32) * r_ref[b, 2 * p + h : 2 * p + h + 1, :]
                    deltas.append(jnp.sum(gah * at_ref[rows, tok].astype(f32), axis=0, keepdims=True))
                    gah = gah.astype(bf16)
                    zero = jnp.zeros_like(gah)
                    grads.append(jnp.concatenate([gah, zero] if h == 0 else [zero, gah], axis=0))
                grads = jnp.concatenate(grads, axis=1)
                delta = jnp.concatenate(deltas, axis=1)
                e = jnp.concatenate([e_ref[b, 2 * p], e_ref[b, 2 * p + 1]], axis=1)
                gs = (e.astype(f32) * (tn(vt_ref[lanes, tok], grads) - delta)).astype(bf16)
                for h in range(2):
                    turned = pltpu.roll(nn(gs[:, h * LEN : (h + 1) * LEN], flip), 0, 1, stride=1, stride_axis=0)
                    head = side * (c // DH) + 2 * p + h
                    gd_ref[head : head + 1, :] += jnp.sum(turned, axis=0, keepdims=True)
                gv_ref[tok, lanes] = nt(e, grads).astype(bf16)
                gk_ref[tok, lanes] = nn(gs, both_heads(q_ref[tok, lanes])).astype(bf16)
                gq = tn(k_ref[tok, lanes], gs)
                gqt_ref[lanes, tok] = jnp.concatenate([gq[0:DH, 0:LEN], gq[DH:, LEN:]], axis=0).astype(bf16)
        gqt = gqt_ref[...]
        gk = gk_ref[...]
        gv = gv_ref[...]
        gwq = nn(gqt, n1).astype(bf16)
        gwk = tn(gk, n1).astype(bf16)
        gwv = tn(gv, n1).astype(bf16)
        for i, gw in enumerate((gwq, gwk, gwv, gwo)):
            for j in range(2):
                outs[2 * side + j][i * w : (i + 1) * w] = gw[j * w : (j + 1) * w]
        part = tn(gqt, side_by_side(shards, 0)) + nn(gk, side_by_side(shards, 1)) + nn(gv, side_by_side(shards, 2))
        gn = part if gn is None else gn + part
    gi, gg1 = norm_back(x_ref[...].astype(f32), g_ref[0:1].astype(f32), gn)
    gi_ref[...] = gx1_ref[...] + gi
    gg1_ref[...] = gg1


def self_bwd(x, x1, gx2, gn2, g, n1, weights, side0, side1):
    t, d = x1.shape
    c = weights[0].shape[0] // 2
    late = pl.BlockSpec(memory_space=pl.ANY)
    args = [x, x1, gx2, gn2, g, n1, *weights, *side0, *side1]
    outs = [jax.ShapeDtypeStruct((2 * c, d), bf16)] * 4 + [
        jax.ShapeDtypeStruct((2 * c // DH, LEN), f32),
        jax.ShapeDtypeStruct((1, d), f32),
        jax.ShapeDtypeStruct((1, d), f32),
        jax.ShapeDtypeStruct((t, d), f32),
    ]
    return call(
        self_bwd_kernel,
        tuple(outs),
        args,
        in_specs=[whole(a.shape) for a in args[:6]]
        + [late] * 2
        + [whole(a.shape) for a in weights[2:4]]
        + [late] * 6
        + [whole(a.shape) for a in side1],
        out_specs=tuple(whole(o.shape) for o in outs),
        scratch=[
            pltpu.VMEM((c, t), bf16),
            pltpu.VMEM((c, t), bf16),
            pltpu.VMEM((t, c), bf16),
            pltpu.VMEM((t, c), bf16),
            pltpu.VMEM((t, d), f32),
        ]
        + [pltpu.VMEM(a.shape, a.dtype) for a in (*weights[0:2], *side0)]
        + [pltpu.SemaphoreType.DMA((8,))],
        vmem=BIG_VMEM,
        name="self_bwd",
    )


def local_program(tensor_size, dp_size, *arrays):
    (block_in, enc_states, dec_len, enc_len, gain_self, self_query, self_key, self_value, self_out, rel_table,
     gain_cross, cross_query, cross_key, cross_value, cross_out, gain_ff, ff_in, ff_out, out_grad) = arrays
    t_index = lax.axis_index("tensor")
    d_index = lax.axis_index("dp")
    nb = block_in.shape[0] // LEN
    w, d = self_out.shape
    heads = w // DH

    def swap(v, axis, bit):
        n = tensor_size if axis == "tensor" else dp_size
        return lax.ppermute(v, axis, [(i, i ^ bit) for i in range(n)])

    def d_bit(bit):
        return (d_index // bit) % 2

    y = d_bit(1).astype(jnp.int32)
    y_is0 = y == 0
    place = jnp.stack([y, (t_index * nb).astype(jnp.int32)])

    def core(v):
        return swap(v, "tensor", 1)

    def over_x(v):
        return swap(v, "tensor", 2)

    def over_y(v):
        return swap(v, "dp", 1)

    def fence(*vals):
        return lax.optimization_barrier(vals)

    gains = jnp.stack([gain_self, gain_cross, gain_ff])

    buckets = np.eye(BUCKETS, dtype=np.float32)[bucket_of_distance()]
    rel_own = jnp.dot(rel_table.astype(f32).T, jnp.asarray(buckets.T), precision=lax.Precision.HIGHEST)
    rel_x = over_x(rel_own)
    own_s = jnp.concatenate([self_query.T, self_key.T, self_value.T, self_out], axis=0)
    x_s = over_x(own_s)
    s_0 = [own_s, core(own_s)]
    bias0 = jnp.concatenate([rel_own, core(rel_own)], axis=0)
    own_c = jnp.concatenate([cross_key.T, cross_value.T, cross_query.T, cross_out], axis=0)
    c_0 = [own_c, core(own_c)]
    out = self_fwd(False, place, dec_len, block_in, gains, s_0, bias0)
    *out, c_0[1] = fence(*out, c_0[1])
    fq0, fk0, fv0, fe0, fr0, fa0, xp = out
    k0, v0 = enc_kv(False, place, enc_states, c_0)
    k0, v0, xp, x_s, rel_x = fence(k0, v0, xp, x_s, rel_x)
    s_1 = [x_s, core(x_s)]
    bias1 = jnp.concatenate([rel_x, core(rel_x)], axis=0)
    half = own_c.shape[0] // 2
    send_c, x_s = fence(jnp.where(y_is0, own_c[:half], own_c[half:]), x_s)
    x_c = over_x(send_c)
    send_f, s_1[1], xp = fence(jnp.where(y_is0, ff_in, ff_out), s_1[1], xp)
    x_f = over_x(send_f)
    out = self_fwd(True, place, dec_len, block_in, gains, s_1, bias1, xp)
    *out, x_c = fence(*out, x_c)
    fq1, fk1, fv1, fe1, fr1, fa1, x1, n1, n2 = out
    y_c, c_c = over_y(x_c), core(x_c)
    cq0, cr0, ca0, x2p = cross_fwd(False, place, enc_len, n2, gains, c_0, k0, v0, x1)
    x2p, y_c, c_c = fence(x2p, y_c, c_c)
    c_1 = [x_c, y_c, c_c, core(y_c)]
    wi1, wo1 = core(ff_in), core(ff_out)
    k1, v1 = enc_kv(True, place, enc_states, c_1)
    k1, v1, x_f = fence(k1, v1, x_f)
    y_f, c_f = over_y(x_f), core(x_f)
    cq1, cr1, ca1, x2, n3 = cross_fwd(True, place, enc_len, n2, gains, c_1, k1, v1, x2p)
    n3, x2, wi1, wo1, c_f = fence(n3, x2, wi1, wo1, c_f)

    rest_size = dp_size // 2
    m = d_index // 2
    rest_groups = [[2 * i + j for i in range(rest_size)] for j in range(2)]

    def plus(*vals):
        total = vals[0].astype(f32)
        for v in vals[1:]:
            total = total + v.astype(f32)
        return total.astype(bf16)

    def pick(v, n, i):
        v = v.reshape((n, v.shape[0] // n) + v.shape[1:])
        return lax.dynamic_index_in_dim(v, i, 0, keepdims=False)

    def ordered(a, b):
        return jnp.where(y_is0, jnp.concatenate([a, b], axis=0), jnp.concatenate([b, a], axis=0))

    def sent_y(*vals):
        return over_y(plus(*[pick(v, 2, 1 - y) for v in vals]))

    def kept_y(*vals):
        return [pick(v, 2, y) for v in vals]

    z_bits = [1 << i for i in range(1, dp_size.bit_length() - 1)]

    def reversed_bits(i):
        return sum(((i >> a) & 1) << (len(z_bits) - 1 - a) for a in range(len(z_bits)))

    def stage_z_reversed(v):
        return [pick(v, rest_size, reversed_bits(m))] + [
            swap(pick(v, rest_size, reversed_bits(m ^ j)), "dp", 2 * j) for j in range(1, rest_size)
        ]

    def in_order(v, got, bit):
        low = d_bit(bit) == 0
        return jnp.where(low, jnp.concatenate([v, got], axis=0), jnp.concatenate([got, v], axis=0))

    def sum_ordered(parts):
        while len(parts) > 1:
            parts = [a + b for a, b in zip(parts[0::2], parts[1::2])]
        return parts[0]

    def stage_z(v):
        return [pick(v, rest_size, m)] + [swap(pick(v, rest_size, m ^ j), "dp", 2 * j) for j in range(1, rest_size)]

    def stage_z_back(v):
        return [v] + [swap(v, "dp", 2 * j) for j in range(1, rest_size)]

    def ordered_z(parts):
        bit = 1
        while len(parts) > 1:
            low = (m // bit) % 2 == 0
            parts = [
                jnp.where(low, jnp.concatenate([a, b], axis=0), jnp.concatenate([b, a], axis=0))
                for a, b in zip(parts[0::2], parts[1::2])
            ]
            bit *= 2
        return parts[0]

    gwi0, gwo0, gwi1, gwo1, yp, gp = ff(False, place, n3, out_grad, [ff_in, ff_out, wi1, wo1])
    yp, y_f = fence(yp, y_f)
    a1, b1 = core(gwo1), core(gwi1)
    f_1 = [x_f, y_f, c_f, core(y_f)]
    out = ff(True, place, n3, out_grad, f_1, yp, gp, x2, gains)
    *out, a1, b1 = fence(*out, a1, b1)
    gwi2, gwo2, gwi3, gwo3, block_out, gx2, go2, gg3 = out
    a3, b3 = core(gwo3), core(gwi3)
    a3, b3, go2 = fence(a3, b3, go2)
    wo_s = plus(gwo2, a3)
    wi_send = jnp.concatenate(
        [plus(pick(gwi0, 2, 1 - y), pick(b1, 2, 1 - y)), plus(pick(gwi2, 2, 1 - y), pick(b3, 2, 1 - y))], axis=0
    )
    wo_s, wi_send, go2 = fence(wo_s, wi_send, go2)
    xo = over_x(wo_s)
    ywi = over_y(wi_send)
    out = cross_bwd(place, enc_len, go2, n2, c_0, c_1, (cq0, k0, v0, cr0, ca0), (cq1, k1, v1, cr1, ca1))
    *out, xo, ywi = fence(*out, xo, ywi)
    gk0, gv0, gk1, gv1, gqo0, gqo1, gqo2, gqo3, gn2 = out
    c3 = core(gqo3)
    hid = gwi0.shape[0] // 2
    wi_x = plus(pick(gwi2, 2, y), pick(b3, 2, y), ywi[hid:])
    wo_y = plus(*[pick(v, 2, 1 - y) for v in (gwo0, a1, xo)])
    wi_x, wo_y, c3, gk0 = fence(wi_x, wo_y, c3, gk0)
    xwi, ywo = over_x(wi_x), over_y(wo_y)
    qo_x, gk0 = fence(plus(gqo2, c3), gk0)
    xqo = over_x(qo_x)
    grad_enc, gkv2, gkv3, gkv0, gkv1 = enc_grad(place, enc_states, gk1, gv1, gk0, gv0, c_0, c_1)
    gkv3, gn2, xwi, ywo = fence(gkv3, gn2, xwi, ywo)
    k3, k1, c1 = core(gkv3), core(gkv1), core(gqo1)
    f_u = jnp.concatenate(
        [plus(*kept_y(gwo0, a1, xo), ywo), plus(*kept_y(gwi0, b1), ywi[:hid], xwi)], axis=0
    )
    f_u, k3, k1, gn2 = fence(f_u, k3, k1, gn2)
    kv_x, gn2 = fence(plus(gkv2, k3), gn2)
    xkv = over_x(kv_x)
    zf = stage_z_reversed(f_u)
    out = self_bwd(
        block_in, x1, gx2, gn2, gains, n1, [*s_0, *s_1], (fq0, fk0, fv0, fe0, fr0, fa0), (fq1, fk1, fv1, fe1, fr1, fa1)
    )
    gs0, gs1, gs2, gs3, gd, gg2, gg1, grad_in = out
    gs0, gs3, gd, gg1, xqo, xkv, c1, *zf = fence(gs0, gs3, gd, gg1, xqo, xkv, c1, *zf)
    s3 = core(gs3)
    qo_t, kv_t = (gqo0, c1, xqo), (gkv0, k1, xkv)
    c_y = plus(*[jnp.where(y_is0, b_, a_) for a_, b_ in zip(qo_t, kv_t)])
    f_w = plus(*zf)
    s3, c_y, f_w = fence(s3, c_y, f_w)
    s_x = plus(gs2, s3)
    s_x, c_y, f_w, gs1, gd, gg1 = fence(s_x, c_y, f_w, gs1, gd, gg1)
    xs = over_x(s_x)
    yc = over_y(c_y)
    for bit in z_bits[:1:-1]:
        f_w = in_order(f_w, swap(f_w, "dp", bit), bit)
    f_got = swap(f_w, "dp", z_bits[1])
    s1 = core(gs1)
    flipped = jnp.asarray(np.ascontiguousarray(buckets[::-1]))
    grel = jnp.dot(gd, flipped, precision=lax.Precision.HIGHEST)
    grel = grel.reshape(tensor_size, heads * BUCKETS)
    slots = jnp.arange(tensor_size)[:, None] ^ t_index
    order = (slots == jnp.arange(tensor_size)[None, :]).astype(f32)
    grel = jnp.dot(order.T, grel, precision=lax.Precision.HIGHEST)
    grel = jnp.pad(grel.reshape(1, -1), ((0, 0), (0, d - grel.size)))
    small = jnp.concatenate([gg1, gg2, gg3, grel], axis=0)
    small_got = core(small)
    yc, small_got, s1, xs, f_got = fence(yc, small_got, s1, xs, f_got)
    ys = sent_y(gs0, s1, xs)
    zc = stage_z_reversed(plus(*[jnp.where(y_is0, a_, b_) for a_, b_ in zip(qo_t, kv_t)], yc))
    small = small + small_got
    small_got = over_x(small)
    f_w = in_order(f_w, f_got, z_bits[1])
    f_got = swap(f_w, "dp", 2)
    ys, small_got, *zc = fence(ys, small_got, *zc)
    zs = stage_z(plus(*kept_y(gs0, s1, xs), ys))
    small = small + small_got
    small_got = over_y(small)
    c_w = plus(*zc)
    for bit in z_bits[:1:-1]:
        c_w = in_order(c_w, swap(c_w, "dp", bit), bit)
    c_got = swap(c_w, "dp", z_bits[1])
    small_got, c_got, f_got, *zs = fence(small_got, c_got, f_got, *zs)
    f_v = in_order(f_w, f_got, 2)
    f_f = over_y(f_v)
    c_w = in_order(c_w, c_got, z_bits[1])
    c_got = swap(c_w, "dp", 2)
    bit = 2
    small = small + small_got
    small_got = swap(small, "dp", bit)
    bs = stage_z_back(plus(*zs))
    small_got, c_got, *bs = fence(small_got, c_got, *bs)
    small = small + small_got
    while 2 * bit < dp_size:
        bit *= 2
        small = small + swap(small, "dp", bit)
    c_v = in_order(c_w, c_got, 2)
    c_f = over_y(c_v)
    s_v = ordered_z(bs)
    s_f = over_y(s_v)
    n_f = f_v.shape[0] // 2
    r_wo = ordered(f_v[:n_f], f_f[:n_f]).astype(f32)
    r_wi = ordered(f_v[n_f:], f_f[n_f:]).astype(f32)
    s_f, r_wo, r_wi = fence(s_f, r_wo, r_wi)
    r_s = ordered(s_v, s_f)
    g_s = [r_s[i * w : (i + 1) * w].astype(f32) for i in range(4)]
    c_f, *g_s = fence(c_f, *g_s)
    c_both = [jnp.where(y_is0, a_, b_) for a_, b_ in ((c_v, c_f), (c_f, c_v))]
    g_c = [v[i * w : (i + 1) * w].astype(f32) for v in c_both for i in range(2)]
    grad_rel = lax.dynamic_slice(small[3], (t_index * heads * BUCKETS,), (heads * BUCKETS,)).reshape(heads, BUCKETS).T

    return (
        block_out,
        grad_in,
        grad_enc,
        small[0],
        g_s[0].T,
        g_s[1].T,
        g_s[2].T,
        g_s[3],
        grad_rel,
        small[1],
        g_c[0].T,
        g_c[2].T,
        g_c[3].T,
        g_c[1],
        small[2],
        r_wi,
        r_wo,
    )


def solution(mesh):
    tensor_size = mesh.shape["tensor"]
    dp_size = mesh.shape["dp"]
    both = P(("dp", "tensor"), None)
    col = P(None, "tensor")
    row = P("tensor", None)
    placed = (both, both, P("dp"), P("dp"), P(), col, col, col, row, col, P(), col, col, col, row, P(), col, row, both)
    outs = (both, both, both, P(), col, col, col, row, col, P(), col, col, col, row, P(), col, row)
    return jax.shard_map(
        lambda *a: local_program(tensor_size, dp_size, *a),
        mesh=mesh,
        in_specs=placed,
        out_specs=outs,
        check_vma=False,
    )
```

```python
import math

import jax
import jax.numpy as jnp
import numpy as np
from jax import lax
from jax.experimental import pallas as pl
from jax.experimental.pallas import tpu as pltpu
from jax.sharding import PartitionSpec as P

BUCKETS = 32
MAX_DIST = 128
LEN = 256
ENC = 1024
DH = 64
KEYS = 128

norm_eps = 1e-06
masked_score = -1000000000.0
bf16 = jnp.bfloat16
f32 = jnp.float32
VMEM_CAP = 16 << 20
BIG_VMEM = 58 << 20


def bucket_of_distance():
    half_count = BUCKETS // 2
    growth_ratio = MAX_DIST / half_count
    limits = np.array(
        [int(math.ceil(half_count * growth_ratio ** (m / half_count))) for m in range(1, half_count)],
        dtype=np.int32,
    )
    distance = np.arange(LEN, dtype=np.int32)
    above = np.sum(distance[:, None] >= limits[None, :], axis=1)
    return np.where(distance < half_count, distance, half_count + above).astype(np.int32)


def nn(a, b):
    return lax.dot_general(a, b, (((1,), (0,)), ((), ())), preferred_element_type=f32)


def nt(a, b):
    return lax.dot_general(a, b, (((1,), (1,)), ((), ())), preferred_element_type=f32)


def tn(a, b):
    return lax.dot_general(a, b, (((0,), (0,)), ((), ())), preferred_element_type=f32)


def inv_rms(v):
    return lax.rsqrt(jnp.mean(v * v, axis=-1, keepdims=True) + norm_eps)


def normed(v, gain):
    return (v * inv_rms(v) * gain).astype(bf16)


def norm_back(v, gain, e):
    s = inv_rms(v)
    ge = gain * e
    dot = jnp.mean(ge * v, axis=-1, keepdims=True)
    grad_v = s * ge - v * (s * s * s * dot)
    grad_gain = jnp.sum(e * v * s, axis=0, keepdims=True)
    return grad_v, grad_gain


def lane_half(shape, h):
    lane = lax.broadcasted_iota(jnp.int32, shape, 1)
    return (lane < DH) if h == 0 else (lane >= DH)


def both_heads(rows):
    zero = jnp.zeros_like(rows)
    return jnp.concatenate([jnp.where(lane_half(rows.shape, h), rows, zero) for h in range(2)], axis=0)


def call(kernel, out_shape, args, *, grid=(), in_specs=None, out_specs=None, scratch=(), flops=0, nbytes=0, trans=0, name=None, vmem=VMEM_CAP):
    kw = {}
    if in_specs is not None:
        kw["in_specs"] = in_specs
    if out_specs is not None:
        kw["out_specs"] = out_specs
    return pl.pallas_call(
        kernel,
        out_shape=out_shape,
        grid=grid,
        scratch_shapes=scratch,
        compiler_params=pltpu.CompilerParams(vmem_limit_bytes=vmem),
        cost_estimate=pl.CostEstimate(flops=1, bytes_accessed=1, transcendentals=0),
        name=name,
        **kw,
    )(*args)


def whole(shape):
    return pl.BlockSpec(shape, lambda *_: (0,) * len(shape))


SMEM = pl.BlockSpec(memory_space=pltpu.SMEM)


def side_by_side(refs, i):
    w = refs[0].shape[0] // 4
    return jnp.concatenate([r[i * w : (i + 1) * w] for r in refs], axis=0)


def pair_rows(y_ref, refs, shared):
    def rows(i):
        if not shared:
            return side_by_side(refs, i)
        w = refs[0].shape[0] // 2
        first = y_ref[0] == i // 2
        part = slice((i % 2) * w, (i % 2 + 1) * w)
        return jnp.concatenate(
            [jnp.where(first, refs[0][part], refs[1][part]), jnp.where(first, refs[2][part], refs[3][part])], axis=0
        )

    return rows


def self_fwd_kernel(last, y_ref, len_ref, x_ref, g_ref, *rest):
    weights = rest[0:2]
    bias_ref = rest[2]
    rest = rest[3:]
    if last:
        xin_ref, q_ref, k_ref, vt_ref, e_ref, r_ref, at_ref, x1_ref, n1_ref, n2_ref, bs_ref = rest
    else:
        q_ref, k_ref, vt_ref, e_ref, r_ref, at_ref, x1_ref, bs_ref = rest
    nh = q_ref.shape[1] // DH
    nb = x_ref.shape[0] // LEN
    x = x_ref[...].astype(f32)
    n1 = normed(x, g_ref[0:1].astype(f32))
    if last:
        n1_ref[...] = n1

    q_ref[...] = nt(n1, side_by_side(weights, 0)).astype(bf16)
    k_ref[...] = nt(n1, side_by_side(weights, 1)).astype(bf16)
    vt_ref[...] = nt(side_by_side(weights, 2), n1).astype(bf16)
    key = lax.broadcasted_iota(jnp.int32, (LEN, 2 * LEN), 0)
    query = lax.broadcasted_iota(jnp.int32, (LEN, 2 * LEN), 1)
    query = jnp.where(query < LEN, query, query - LEN)
    for p in range(nh // 2):
        lanes = slice(p * 2 * DH, (p + 1) * 2 * DH)
        for h in range(2):
            row = jnp.broadcast_to(bias_ref[2 * p + h : 2 * p + h + 1, :], (LEN, LEN))
            bs_ref[:, h * LEN : (h + 1) * LEN] = pltpu.roll(row, 0, 1, stride=1, stride_axis=0)
        for b in range(nb):
            tok = slice(b * LEN, (b + 1) * LEN)
            allowed = (key <= query) & (key < len_ref[y_ref[1] + b])
            s = nt(k_ref[tok, lanes], both_heads(q_ref[tok, lanes])) + bs_ref[...]
            s = jnp.where(allowed, s, masked_score)
            e = jnp.exp(s - jnp.max(s, axis=0, keepdims=True))
            r = 1.0 / jnp.sum(e, axis=0, keepdims=True)
            e = e.astype(bf16)
            outs = []
            for h in range(2):
                head = 2 * p + h
                half = slice(h * LEN, (h + 1) * LEN)
                e_ref[b, head] = e[:, half]
                r_ref[b, head : head + 1, :] = r[:, half]
                outs.append(nn(vt_ref[head * DH : (head + 1) * DH, tok], e[:, half]) * r[:, half])
            at_ref[lanes, tok] = jnp.concatenate(outs, axis=0).astype(bf16)
    mixed = tn(at_ref[...], side_by_side(weights, 3))
    if last:
        x1 = xin_ref[...] + mixed
        n2_ref[...] = normed(x1, g_ref[1:2].astype(f32))
    else:
        x1 = x + mixed
    x1_ref[...] = x1


def self_fwd(last, y, lens, x, g, weights, bias, xin=None):
    t, d = x.shape
    w = weights[0].shape[0] // 4
    c = 2 * w
    nh = c // DH
    nb = t // LEN
    outs = [
        jax.ShapeDtypeStruct((t, c), bf16),
        jax.ShapeDtypeStruct((t, c), bf16),
        jax.ShapeDtypeStruct((c, t), bf16),
        jax.ShapeDtypeStruct((nb, nh, LEN, LEN), bf16),
        jax.ShapeDtypeStruct((nb, nh, LEN), f32),
        jax.ShapeDtypeStruct((c, t), bf16),
        jax.ShapeDtypeStruct((t, d), f32),
    ]
    args = [y, lens, x, g, *weights, bias]
    if last:
        args.append(xin)
        outs += [jax.ShapeDtypeStruct((t, d), bf16)] * 2
    flops = 2 * t * d * c * 4 + 2 * t * LEN * nh * 128 * 2
    return call(
        lambda *r: self_fwd_kernel(last, *r),
        tuple(outs),
        args,
        in_specs=[SMEM, SMEM] + [whole(a.shape) for a in args[2:]],
        out_specs=tuple(whole(o.shape) for o in outs),
        scratch=[pltpu.VMEM((LEN, 2 * LEN), f32)],
        flops=flops * 3,
        nbytes=12 * 1024 * 1024,
        trans=t * LEN * nh,
        name="self_fwd",
    )


def enc_kv_kernel(shared, y_ref, enc_ref, *rest):
    k_ref, v_ref = rest[-2:]
    enc = enc_ref[...]
    rows = pair_rows(y_ref, rest[:-2], shared)
    k_ref[...] = nt(enc, rows(0)).astype(bf16)
    v_ref[...] = nt(enc, rows(1)).astype(bf16)


def enc_kv(shared, y, enc, kv):
    t, d = enc.shape
    c = kv[0].shape[0] if shared else kv[0].shape[0] // 2
    rows = 512
    half = pl.BlockSpec((rows, c), lambda i: (i, 0))
    return call(
        lambda *r: enc_kv_kernel(shared, *r),
        (jax.ShapeDtypeStruct((t, c), bf16),) * 2,
        (y, enc, *kv),
        grid=(t // rows,),
        in_specs=[SMEM, pl.BlockSpec((rows, d), lambda i: (i, 0))] + [whole(a.shape) for a in kv],
        out_specs=(half, half),
        flops=2 * t * d * c * 2 * 2,
        nbytes=t * d * 2 + 4 * t * c * 2,
        name="enc_kv",
    )


def cross_fwd_kernel(last, pairs, y_ref, len_ref, n2_ref, g_ref, *rest):
    n_w = 4 if last else 2
    weights = pair_rows(y_ref, rest[:n_w], last)
    k_ref, v_ref, xin_ref = rest[n_w : n_w + 3]
    rest = rest[n_w + 3 :]
    if last:
        q_ref, r_ref, at_ref, x2_ref, n3_ref, s_ref, e_ref = rest
    else:
        q_ref, r_ref, at_ref, x2_ref, s_ref, e_ref = rest
    step = pl.program_id(0)
    b = step // pairs
    p = lax.rem(step, pairs)

    @pl.when(step == 0)
    def _():
        q_ref[...] = nt(n2_ref[...], weights(2)).astype(bf16)

    tok = pl.ds(pl.multiple_of(b * LEN, LEN), LEN)
    lanes = pl.ds(pl.multiple_of(p * 2 * DH, 2 * DH), 2 * DH)
    qp = q_ref[tok, lanes]
    count = len_ref[y_ref[1] + b]
    key = lax.broadcasted_iota(jnp.int32, (KEYS, 2 * LEN), 0)
    queries = both_heads(qp)
    top = None
    for c in range(ENC // KEYS):
        part = slice(c * KEYS, (c + 1) * KEYS)
        s = jnp.where(key < count - c * KEYS, nt(k_ref[part], queries), masked_score)
        s_ref[part] = s
        t = jnp.max(s.reshape(KEYS // 8, 8, 2 * LEN), axis=0)
        top = t if c == 0 else jnp.maximum(top, t)
    top = jnp.max(top, axis=0, keepdims=True)
    total = None
    for c in range(ENC // KEYS):
        part = slice(c * KEYS, (c + 1) * KEYS)
        e = jnp.exp(s_ref[part] - top)
        t = jnp.sum(e.reshape(KEYS // 8, 8, 2 * LEN), axis=0)
        total = t if c == 0 else total + t
        e_ref[part] = e.astype(bf16)
    r = 1.0 / jnp.sum(total, axis=0, keepdims=True)
    mixed = tn(v_ref[...], e_ref[...]) * r
    outs = []
    for h in range(2):
        half = slice(h * LEN, (h + 1) * LEN)
        r_ref[0, h : h + 1, :] = r[:, half]
        r_ref[0, 2 + h : 3 + h, :] = top[:, half]
        outs.append(mixed[h * DH : (h + 1) * DH, half])
    at_ref[lanes, tok] = jnp.concatenate(outs, axis=0).astype(bf16)

    @pl.when(step == pl.num_programs(0) - 1)
    def _():
        x2 = xin_ref[...] + tn(at_ref[...], weights(3))
        x2_ref[...] = x2
        if last:
            n3_ref[...] = normed(x2, g_ref[2:3].astype(f32))


def cross_fwd(last, y, lens, n2, g, qo, k, v, xin):
    t, d = n2.shape
    c = k.shape[1]
    nb = t // LEN
    pairs = c // (2 * DH)
    outs = [
        jax.ShapeDtypeStruct((t, c), bf16),
        jax.ShapeDtypeStruct((nb * pairs, 4, LEN), f32),
        jax.ShapeDtypeStruct((c, t), bf16),
        jax.ShapeDtypeStruct((t, d), f32),
    ]
    specs = [
        whole((t, c)),
        pl.BlockSpec((1, 4, LEN), lambda i: (i, 0, 0)),
        whole((c, t)),
        whole((t, d)),
    ]
    if last:
        outs.append(jax.ShapeDtypeStruct((t, d), bf16))
        specs.append(whole((t, d)))
    return call(
        lambda *r: cross_fwd_kernel(last, pairs, *r),
        tuple(outs),
        (y, lens, n2, g, *qo, k, v, xin),
        grid=(nb * pairs,),
        in_specs=[
            SMEM,
            SMEM,
            whole(n2.shape),
            whole(g.shape),
            *[whole(a.shape) for a in qo],
            pl.BlockSpec((ENC, 2 * DH), lambda i: (i // pairs, i % pairs)),
            pl.BlockSpec((ENC, 2 * DH), lambda i: (i // pairs, i % pairs)),
            whole(xin.shape),
        ],
        out_specs=tuple(specs),
        scratch=[pltpu.VMEM((ENC, 2 * LEN), f32), pltpu.VMEM((ENC, 2 * LEN), bf16)],
        flops=3 * (2 * t * d * c * 2 + 2 * t * ENC * c * 2 * 2),
        nbytes=14 * 1024 * 1024,
        trans=t * ENC * (c // DH),
        name="cross_fwd",
    )


ROOT = math.sqrt(2.0 / math.pi)
CUBE = 0.044715


def ff_kernel(last, y_ref, n3_ref, gf_ref, *rest):
    if last:
        ha_in, ha_out, ga_in, ga_out, hb_in, hb_out, gb_in, gb_out = rest[:8]
        rest = rest[8:]
        first = y_ref[0] == 0

        def weights(h_in, h_out, g_in, g_out):
            return (
                lambda: jnp.where(first, h_in[...], g_in[...]),
                lambda: jnp.where(first, g_out[...], h_out[...]),
            )

        shards = (weights(ha_in, ha_out, ga_in, ga_out), weights(hb_in, hb_out, gb_in, gb_out))
    else:
        wia_ref, woa_ref, wib_ref, wob_ref = rest[:4]
        rest = rest[4:]
        shards = ((lambda: wia_ref[...], lambda: woa_ref[...]), (lambda: wib_ref[...], lambda: wob_ref[...]))
    if last:
        yin_ref, gin_ref, x2_ref, g_ref = rest[:4]
        gwia, gwoa, gwib, gwob, out_ref, gx2_ref, go2_ref, gg_ref, y_acc, gn_ref, n3t_ref = rest[4:]
    else:
        gwia, gwoa, gwib, gwob, y_acc, gn_ref, n3t_ref = rest
    step = pl.program_id(0)

    @pl.when(step == 0)
    def _():
        n3t_ref[...] = n3_ref[...].T
        if last:
            y_acc[...] = yin_ref[...]
            gn_ref[...] = gin_ref[...]
        else:
            y_acc[...] = jnp.zeros_like(y_acc)
            gn_ref[...] = jnp.zeros_like(gn_ref)

    n3 = n3_ref[...]
    gf = gf_ref[...]
    kept = []
    for (get_wi, get_wo), gwi, gwo in zip(shards, (gwia, gwib), (gwoa, gwob)):
        wi, wo = get_wi(), get_wo()
        u = nn(n3, wi)
        dh = nt(gf, wo)
        u2 = u * u
        th = jnp.tanh(ROOT * u * (1.0 + CUBE * u2))
        half = 0.5 * (1.0 + th)
        r = (u * half).astype(bf16)
        slope = half + 0.5 * u * (1.0 - th * th) * (ROOT * (1.0 + (3.0 * CUBE) * u2))
        gu = (dh * slope).astype(bf16)
        kept.append((r, wo, gu, wi))
        gwo[...] = tn(r, gf).astype(bf16)
        gwi[...] = nn(n3t_ref[...], gu).astype(bf16)
    r, wo, gu, wi = [jnp.concatenate(v, axis=a) for v, a in zip(zip(*kept), (1, 0, 1, 1))]
    y_acc[...] += nn(r, wo)
    gn_ref[...] += nt(gu, wi)

    if last:

        @pl.when(step == pl.num_programs(0) - 1)
        def _():
            x2 = x2_ref[...]
            out_ref[...] = (x2 + y_acc[...]).astype(bf16)
            gx, gg = norm_back(x2, g_ref[2:3].astype(f32), gn_ref[...])
            gx2 = gf.astype(f32) + gx
            gx2_ref[...] = gx2
            go2_ref[...] = gx2.astype(bf16)
            gg_ref[...] = gg


def ff(last, y, n3, gf, weights, yin=None, gin=None, x2=None, g=None):
    t, d = n3.shape
    hid = weights[0].shape[1]
    blk = 256
    args = [y, n3, gf]
    col = pl.BlockSpec((d, blk), lambda i: (0, i))
    row = pl.BlockSpec((blk, d), lambda i: (i, 0))
    in_specs = [SMEM, whole((t, d)), whole((t, d))]
    if last:
        for v in weights:
            args += [v, v]
            in_specs += [col, row]
    else:
        args += weights
        in_specs += [col, row, col, row]
    outs = [jax.ShapeDtypeStruct((d, hid), bf16), jax.ShapeDtypeStruct((hid, d), bf16)] * 2
    specs = [col, row, col, row]
    acc = jax.ShapeDtypeStruct((t, d), f32)
    scratch = [pltpu.VMEM((d, t), bf16)]
    if last:
        args += [yin, gin, x2, g]
        in_specs += [whole((t, d))] * 3 + [whole(g.shape)]
        outs += [jax.ShapeDtypeStruct((t, d), bf16), acc, jax.ShapeDtypeStruct((t, d), bf16), jax.ShapeDtypeStruct((1, d), f32)]
        specs += [whole((t, d))] * 3 + [whole((1, d))]
        scratch = [pltpu.VMEM((t, d), f32)] * 2 + scratch
    else:
        outs += [acc, acc]
        specs += [whole((t, d))] * 2
    return call(
        lambda *r: ff_kernel(last, *r),
        tuple(outs),
        args,
        grid=(hid // blk,),
        in_specs=in_specs,
        out_specs=tuple(specs),
        scratch=scratch,
        flops=2 * 6 * 2 * t * d * hid * 2,
        nbytes=12 * 1024 * 1024,
        trans=2 * t * hid,
        vmem=20 << 20,
        name="ff",
    )


def cross_bwd_kernel(pairs, steps, y_ref, len_ref, go_ref, n2_ref, *rest):
    weights = (pair_rows(y_ref, rest[0:2], False), pair_rows(y_ref, rest[2:6], True))
    sides = (rest[6:11], rest[11:16])
    gk0, gv0, gk1, gv1, outs, gn_ref, gat_ref, gqt_ref, e_ref, gs_ref = *rest[16:20], rest[20:24], *rest[24:]
    w = outs[0].shape[0] // 2
    step = pl.program_id(0)
    key = lax.broadcasted_iota(jnp.int32, (KEYS, 2 * LEN), 0)

    def half(side, local, gk_ref, gv_ref):
        q_ref, k_ref, v_ref, r_ref, at_ref = sides[side]
        b = local // pairs
        p = lax.rem(local, pairs)

        @pl.when(local == 0)
        def _():
            gat_ref[...] = nt(weights[side](3), go_ref[...]).astype(bf16)

        tok = pl.ds(pl.multiple_of(b * LEN, LEN), LEN)
        lanes = pl.ds(pl.multiple_of(p * 2 * DH, 2 * DH), 2 * DH)
        qp = q_ref[tok, lanes]
        ga_t = gat_ref[lanes, tok]
        a_t = at_ref[lanes, tok]
        count = len_ref[y_ref[1] + b]
        grads, deltas = [], []
        for h in range(2):
            part = slice(h * DH, (h + 1) * DH)
            gah = ga_t[part].astype(f32) * r_ref[0, h : h + 1, :]
            deltas.append(jnp.sum(gah * a_t[part].astype(f32), axis=0, keepdims=True))
            gah = gah.astype(bf16)
            zero = jnp.zeros_like(gah)
            grads.append(jnp.concatenate([gah, zero] if h == 0 else [zero, gah], axis=0))
        grads = jnp.concatenate(grads, axis=1)
        delta = jnp.concatenate(deltas, axis=1)
        top = jnp.concatenate([r_ref[0, 2:3, :], r_ref[0, 3:4, :]], axis=1)
        queries = both_heads(qp)
        for c in range(ENC // KEYS):
            part = slice(c * KEYS, (c + 1) * KEYS)
            s = jnp.where(key < count - c * KEYS, nt(k_ref[part], queries), masked_score)
            e = jnp.exp(s - top)
            gs_ref[part] = (e * (nn(v_ref[part], grads) - delta)).astype(bf16)
            e_ref[part] = e.astype(bf16)
        gv_ref[...] = nt(e_ref[...], grads).astype(bf16)
        gk_ref[...] = nn(gs_ref[...], queries).astype(bf16)
        gq = tn(k_ref[...], gs_ref[...])
        gqt_ref[lanes, tok] = jnp.concatenate([gq[0:DH, 0:LEN], gq[DH:, LEN:]], axis=0).astype(bf16)

        @pl.when(local == steps - 1)
        def _():
            gqt = gqt_ref[...]
            gwq = nn(gqt, n2_ref[...]).astype(bf16)
            gwo = nn(at_ref[...], go_ref[...]).astype(bf16)
            for i in range(2):
                outs[2 * side + i][0:w] = gwq[i * w : (i + 1) * w]
                outs[2 * side + i][w:] = gwo[i * w : (i + 1) * w]
            gn = tn(gqt, weights[side](2))
            gn_ref[...] = gn if side == 1 else gn_ref[...] + gn

    @pl.when(step < steps)
    def _():
        half(1, step, gk1, gv1)

    @pl.when(step >= steps)
    def _():
        half(0, step - steps, gk0, gv0)


def cross_bwd(y, lens, go, n2, w0, w1, side0, side1):
    t, d = go.shape
    te, c = side0[1].shape
    nb = t // LEN
    pairs = c // (2 * DH)
    steps = nb * pairs

    def early(i):
        return jnp.minimum(i, steps - 1)

    def late(i):
        return jnp.maximum(i - steps, 0)

    def tokhead(when):
        return pl.BlockSpec((ENC, 2 * DH), lambda i: (when(i) // pairs, when(i) % pairs))

    def side_specs(when):
        return [whole((t, c)), tokhead(when), tokhead(when), pl.BlockSpec((1, 4, LEN), lambda i: (when(i), 0, 0)), whole((c, t))]

    grad = jax.ShapeDtypeStruct((te, c), bf16)
    out = jax.ShapeDtypeStruct((c, d), bf16)
    return call(
        lambda *r_: cross_bwd_kernel(pairs, steps, *r_),
        (grad,) * 4 + (out,) * 4 + (jax.ShapeDtypeStruct((t, d), f32),),
        (y, lens, go, n2, *w0, *w1, *side0, *side1),
        grid=(2 * steps,),
        in_specs=[SMEM, SMEM, whole((t, d)), whole((t, d))]
        + [whole(a.shape) for a in (*w0, *w1)]
        + side_specs(late)
        + side_specs(early),
        out_specs=(tokhead(late), tokhead(late), tokhead(early), tokhead(early)) + (whole((c, d)),) * 4 + (whole((t, d)),),
        scratch=[
            pltpu.VMEM((c, t), bf16),
            pltpu.VMEM((c, t), bf16),
            pltpu.VMEM((ENC, 2 * LEN), bf16),
            pltpu.VMEM((ENC, 2 * LEN), bf16),
        ],
        vmem=BIG_VMEM,
        name="cross_bwd",
    )


def enc_grad_kernel(y_ref, enc_ref, gk1_ref, gv1_ref, gk0_ref, gv0_ref, *rest):
    w0 = pair_rows(y_ref, rest[0:2], False)
    w1 = pair_rows(y_ref, rest[2:6], True)
    out_ref, outs, accs_ref = rest[6], rest[7:11], rest[11]
    w = outs[0].shape[0] // 2
    step = pl.program_id(0)
    enc = enc_ref[...]
    grads = [g[...] for g in (gk1_ref, gv1_ref, gk0_ref, gv0_ref)]
    rhs = jnp.concatenate([w1(0), w1(1), w0(0), w0(1)], axis=0)
    out_ref[...] = nn(jnp.concatenate(grads, axis=1), rhs)
    terms = [tn(g, enc) for g in grads]

    @pl.when(step == 0)
    def _():
        for i in range(4):
            accs_ref[i] = terms[i]

    @pl.when(step != 0)
    def _():
        for i in range(4):
            accs_ref[i] += terms[i]

    @pl.when(step == pl.num_programs(0) - 1)
    def _():
        for pair in range(2):
            for i in range(2):
                acc = accs_ref[2 * pair + i]
                outs[2 * pair][i * w : (i + 1) * w] = acc[0:w].astype(bf16)
                outs[2 * pair + 1][i * w : (i + 1) * w] = acc[w:].astype(bf16)


def enc_grad(y, enc, gk1, gv1, gk0, gv0, w0, w1):
    te, d = enc.shape
    c = gk1.shape[1]
    rows = 512
    half = pl.BlockSpec((rows, c), lambda i: (i, 0))
    block = pl.BlockSpec((rows, d), lambda i: (i, 0))
    out = jax.ShapeDtypeStruct((c, d), bf16)
    return call(
        enc_grad_kernel,
        (jax.ShapeDtypeStruct((te, d), f32),) + (out,) * 4,
        (y, enc, gk1, gv1, gk0, gv0, *w0, *w1),
        grid=(te // rows,),
        in_specs=[SMEM, block] + [half] * 4 + [whole(a.shape) for a in (*w0, *w1)],
        out_specs=(block,) + (whole((c, d)),) * 4,
        scratch=[pltpu.VMEM((4, c, d), f32)],
        vmem=BIG_VMEM,
        name="enc_grad",
    )


def self_bwd_kernel(x_ref, x1_ref, gx2_ref, gn2_ref, g_ref, n1_ref, *rest):
    weights = rest[0:4]
    sides = (rest[4:10], rest[10:16])
    outs = rest[16:20]
    gd_ref, gg2_ref, gg1_ref, gi_ref, gat_ref, gqt_ref, gk_ref, gv_ref, gx1_ref = rest[20:29]
    held, sems = rest[29:37], rest[37]
    arrivals = [
        pltpu.make_async_copy(src, dst, sems.at[i]) for i, (src, dst) in enumerate(zip((*weights[0:2], *sides[0]), held))
    ]
    for copy in arrivals:
        copy.start()
    weights = (*held[0:2], *weights[2:4])
    sides = (held[2:8], sides[1])
    w = outs[0].shape[0] // 4
    c = 2 * w
    nb = n1_ref.shape[0] // LEN
    gx, gg2 = norm_back(x1_ref[...], g_ref[1:2].astype(f32), gn2_ref[...])
    gx1 = gx2_ref[...] + gx
    gx1_ref[...] = gx1
    gg2_ref[...] = gg2
    go = gx1.astype(bf16)
    ri = lax.broadcasted_iota(jnp.int32, (LEN, LEN), 0)
    ci = lax.broadcasted_iota(jnp.int32, (LEN, LEN), 1)
    flip = jnp.where(ri + ci == LEN - 1, 1.0, 0.0).astype(bf16)
    n1 = n1_ref[...]
    gn = None
    for side in (1, 0):
        if side == 0:
            for copy in arrivals:
                copy.wait()
        shards = weights[2 * side : 2 * side + 2]
        q_ref, k_ref, vt_ref, e_ref, r_ref, at_ref = sides[side]
        gat_ref[...] = nt(side_by_side(shards, 3), go).astype(bf16)
        gwo = nn(at_ref[...], go).astype(bf16)
        for p in range(c // (2 * DH)):
            lanes = slice(p * 2 * DH, (p + 1) * 2 * DH)
            for h in range(2):
                head = side * (c // DH) + 2 * p + h
                gd_ref[head : head + 1, :] = jnp.zeros((1, LEN), f32)
            for b in range(nb):
                tok = slice(b * LEN, (b + 1) * LEN)
                grads, deltas = [], []
                for h in range(2):
                    rows = slice(lanes.start + h * DH, lanes.start + (h + 1) * DH)
                    gah = gat_ref[rows, tok].astype(f32) * r_ref[b, 2 * p + h : 2 * p + h + 1, :]
                    deltas.append(jnp.sum(gah * at_ref[rows, tok].astype(f32), axis=0, keepdims=True))
                    gah = gah.astype(bf16)
                    zero = jnp.zeros_like(gah)
                    grads.append(jnp.concatenate([gah, zero] if h == 0 else [zero, gah], axis=0))
                grads = jnp.concatenate(grads, axis=1)
                delta = jnp.concatenate(deltas, axis=1)
                e = jnp.concatenate([e_ref[b, 2 * p], e_ref[b, 2 * p + 1]], axis=1)
                gs = (e.astype(f32) * (tn(vt_ref[lanes, tok], grads) - delta)).astype(bf16)
                for h in range(2):
                    turned = pltpu.roll(nn(gs[:, h * LEN : (h + 1) * LEN], flip), 0, 1, stride=1, stride_axis=0)
                    head = side * (c // DH) + 2 * p + h
                    gd_ref[head : head + 1, :] += jnp.sum(turned, axis=0, keepdims=True)
                gv_ref[tok, lanes] = nt(e, grads).astype(bf16)
                gk_ref[tok, lanes] = nn(gs, both_heads(q_ref[tok, lanes])).astype(bf16)
                gq = tn(k_ref[tok, lanes], gs)
                gqt_ref[lanes, tok] = jnp.concatenate([gq[0:DH, 0:LEN], gq[DH:, LEN:]], axis=0).astype(bf16)
        gqt = gqt_ref[...]
        gk = gk_ref[...]
        gv = gv_ref[...]
        gwq = nn(gqt, n1).astype(bf16)
        gwk = tn(gk, n1).astype(bf16)
        gwv = tn(gv, n1).astype(bf16)
        for i, gw in enumerate((gwq, gwk, gwv, gwo)):
            for j in range(2):
                outs[2 * side + j][i * w : (i + 1) * w] = gw[j * w : (j + 1) * w]
        part = tn(gqt, side_by_side(shards, 0)) + nn(gk, side_by_side(shards, 1)) + nn(gv, side_by_side(shards, 2))
        gn = part if gn is None else gn + part
    gi, gg1 = norm_back(x_ref[...].astype(f32), g_ref[0:1].astype(f32), gn)
    gi_ref[...] = gx1_ref[...] + gi
    gg1_ref[...] = gg1


def self_bwd(x, x1, gx2, gn2, g, n1, weights, side0, side1):
    t, d = x1.shape
    c = weights[0].shape[0] // 2
    late = pl.BlockSpec(memory_space=pl.ANY)
    args = [x, x1, gx2, gn2, g, n1, *weights, *side0, *side1]
    outs = [jax.ShapeDtypeStruct((2 * c, d), bf16)] * 4 + [
        jax.ShapeDtypeStruct((2 * c // DH, LEN), f32),
        jax.ShapeDtypeStruct((1, d), f32),
        jax.ShapeDtypeStruct((1, d), f32),
        jax.ShapeDtypeStruct((t, d), f32),
    ]
    return call(
        self_bwd_kernel,
        tuple(outs),
        args,
        in_specs=[whole(a.shape) for a in args[:6]]
        + [late] * 2
        + [whole(a.shape) for a in weights[2:4]]
        + [late] * 6
        + [whole(a.shape) for a in side1],
        out_specs=tuple(whole(o.shape) for o in outs),
        scratch=[
            pltpu.VMEM((c, t), bf16),
            pltpu.VMEM((c, t), bf16),
            pltpu.VMEM((t, c), bf16),
            pltpu.VMEM((t, c), bf16),
            pltpu.VMEM((t, d), f32),
        ]
        + [pltpu.VMEM(a.shape, a.dtype) for a in (*weights[0:2], *side0)]
        + [pltpu.SemaphoreType.DMA((8,))],
        vmem=BIG_VMEM,
        name="self_bwd",
    )


def local_program(tensor_size, dp_size, *arrays):
    (block_in, enc_states, dec_len, enc_len, gain_self, self_query, self_key, self_value, self_out, rel_table,
     gain_cross, cross_query, cross_key, cross_value, cross_out, gain_ff, ff_in, ff_out, out_grad) = arrays
    t_index = lax.axis_index("tensor")
    d_index = lax.axis_index("dp")
    nb = block_in.shape[0] // LEN
    w, d = self_out.shape
    heads = w // DH

    def swap(v, axis, bit):
        n = tensor_size if axis == "tensor" else dp_size
        return lax.ppermute(v, axis, [(i, i ^ bit) for i in range(n)])

    def d_bit(bit):
        return (d_index // bit) % 2

    y = d_bit(1).astype(jnp.int32)
    y_is0 = y == 0
    place = jnp.stack([y, (t_index * nb).astype(jnp.int32)])

    def core(v):
        return swap(v, "tensor", 1)

    def over_x(v):
        return swap(v, "tensor", 2)

    def over_y(v):
        return swap(v, "dp", 1)

    def fence(*vals):
        return lax.optimization_barrier(vals)

    gains = jnp.stack([gain_self, gain_cross, gain_ff])

    buckets = np.eye(BUCKETS, dtype=np.float32)[bucket_of_distance()]
    rel_own = jnp.dot(rel_table.astype(f32).T, jnp.asarray(buckets.T), precision=lax.Precision.HIGHEST)
    rel_x = over_x(rel_own)
    own_s = jnp.concatenate([self_query.T, self_key.T, self_value.T, self_out], axis=0)
    x_s = over_x(own_s)
    s_0 = [own_s, core(own_s)]
    bias0 = jnp.concatenate([rel_own, core(rel_own)], axis=0)
    own_c = jnp.concatenate([cross_key.T, cross_value.T, cross_query.T, cross_out], axis=0)
    c_0 = [own_c, core(own_c)]
    out = self_fwd(False, place, dec_len, block_in, gains, s_0, bias0)
    *out, c_0[1] = fence(*out, c_0[1])
    fq0, fk0, fv0, fe0, fr0, fa0, xp = out
    k0, v0 = enc_kv(False, place, enc_states, c_0)
    k0, v0, xp, x_s, rel_x = fence(k0, v0, xp, x_s, rel_x)
    s_1 = [x_s, core(x_s)]
    bias1 = jnp.concatenate([rel_x, core(rel_x)], axis=0)
    half = own_c.shape[0] // 2
    send_c, x_s = fence(jnp.where(y_is0, own_c[:half], own_c[half:]), x_s)
    x_c = over_x(send_c)
    send_f, s_1[1], xp = fence(jnp.where(y_is0, ff_in, ff_out), s_1[1], xp)
    x_f = over_x(send_f)
    out = self_fwd(True, place, dec_len, block_in, gains, s_1, bias1, xp)
    *out, x_c = fence(*out, x_c)
    fq1, fk1, fv1, fe1, fr1, fa1, x1, n1, n2 = out
    y_c, c_c = over_y(x_c), core(x_c)
    cq0, cr0, ca0, x2p = cross_fwd(False, place, enc_len, n2, gains, c_0, k0, v0, x1)
    x2p, y_c, c_c = fence(x2p, y_c, c_c)
    c_1 = [x_c, y_c, c_c, core(y_c)]
    wi1, wo1 = core(ff_in), core(ff_out)
    k1, v1 = enc_kv(True, place, enc_states, c_1)
    k1, v1, x_f = fence(k1, v1, x_f)
    y_f, c_f = over_y(x_f), core(x_f)
    cq1, cr1, ca1, x2, n3 = cross_fwd(True, place, enc_len, n2, gains, c_1, k1, v1, x2p)
    n3, x2, wi1, wo1, c_f = fence(n3, x2, wi1, wo1, c_f)

    rest_size = dp_size // 2
    m = d_index // 2
    rest_groups = [[2 * i + j for i in range(rest_size)] for j in range(2)]

    def plus(*vals):
        total = vals[0].astype(f32)
        for v in vals[1:]:
            total = total + v.astype(f32)
        return total.astype(bf16)

    def pick(v, n, i):
        v = v.reshape((n, v.shape[0] // n) + v.shape[1:])
        return lax.dynamic_index_in_dim(v, i, 0, keepdims=False)

    def ordered(a, b):
        return jnp.where(y_is0, jnp.concatenate([a, b], axis=0), jnp.concatenate([b, a], axis=0))

    def sent_y(*vals):
        return over_y(plus(*[pick(v, 2, 1 - y) for v in vals]))

    def kept_y(*vals):
        return [pick(v, 2, y) for v in vals]

    z_bits = [1 << i for i in range(1, dp_size.bit_length() - 1)]

    def reversed_bits(i):
        return sum(((i >> a) & 1) << (len(z_bits) - 1 - a) for a in range(len(z_bits)))

    def stage_z_reversed(v):
        return [pick(v, rest_size, reversed_bits(m))] + [
            swap(pick(v, rest_size, reversed_bits(m ^ j)), "dp", 2 * j) for j in range(1, rest_size)
        ]

    def in_order(v, got, bit):
        low = d_bit(bit) == 0
        return jnp.where(low, jnp.concatenate([v, got], axis=0), jnp.concatenate([got, v], axis=0))

    def sum_ordered(parts):
        while len(parts) > 1:
            parts = [a + b for a, b in zip(parts[0::2], parts[1::2])]
        return parts[0]

    def stage_z(v):
        return [pick(v, rest_size, m)] + [swap(pick(v, rest_size, m ^ j), "dp", 2 * j) for j in range(1, rest_size)]

    def stage_z_back(v):
        return [v] + [swap(v, "dp", 2 * j) for j in range(1, rest_size)]

    def ordered_z(parts):
        bit = 1
        while len(parts) > 1:
            low = (m // bit) % 2 == 0
            parts = [
                jnp.where(low, jnp.concatenate([a, b], axis=0), jnp.concatenate([b, a], axis=0))
                for a, b in zip(parts[0::2], parts[1::2])
            ]
            bit *= 2
        return parts[0]

    gwi0, gwo0, gwi1, gwo1, yp, gp = ff(False, place, n3, out_grad, [ff_in, ff_out, wi1, wo1])
    yp, y_f = fence(yp, y_f)
    a1, b1 = core(gwo1), core(gwi1)
    f_1 = [x_f, y_f, c_f, core(y_f)]
    out = ff(True, place, n3, out_grad, f_1, yp, gp, x2, gains)
    *out, a1, b1 = fence(*out, a1, b1)
    gwi2, gwo2, gwi3, gwo3, block_out, gx2, go2, gg3 = out
    a3, b3 = core(gwo3), core(gwi3)
    a3, b3, go2 = fence(a3, b3, go2)
    wo_s = plus(gwo2, a3)
    wi_send = jnp.concatenate(
        [plus(pick(gwi0, 2, 1 - y), pick(b1, 2, 1 - y)), plus(pick(gwi2, 2, 1 - y), pick(b3, 2, 1 - y))], axis=0
    )
    wo_s, wi_send, go2 = fence(wo_s, wi_send, go2)
    xo = over_x(wo_s)
    ywi = over_y(wi_send)
    out = cross_bwd(place, enc_len, go2, n2, c_0, c_1, (cq0, k0, v0, cr0, ca0), (cq1, k1, v1, cr1, ca1))
    *out, xo, ywi = fence(*out, xo, ywi)
    gk0, gv0, gk1, gv1, gqo0, gqo1, gqo2, gqo3, gn2 = out
    c3 = core(gqo3)
    hid = gwi0.shape[0] // 2
    wi_x = plus(pick(gwi2, 2, y), pick(b3, 2, y), ywi[hid:])
    wo_y = plus(*[pick(v, 2, 1 - y) for v in (gwo0, a1, xo)])
    wi_x, wo_y, c3, gk0 = fence(wi_x, wo_y, c3, gk0)
    xwi, ywo = over_x(wi_x), over_y(wo_y)
    qo_x, gk0 = fence(plus(gqo2, c3), gk0)
    xqo = over_x(qo_x)
    grad_enc, gkv2, gkv3, gkv0, gkv1 = enc_grad(place, enc_states, gk1, gv1, gk0, gv0, c_0, c_1)
    gkv3, gn2, xwi, ywo = fence(gkv3, gn2, xwi, ywo)
    k3, k1, c1 = core(gkv3), core(gkv1), core(gqo1)
    f_u = jnp.concatenate(
        [plus(*kept_y(gwo0, a1, xo), ywo), plus(*kept_y(gwi0, b1), ywi[:hid], xwi)], axis=0
    )
    f_u, k3, k1, gn2 = fence(f_u, k3, k1, gn2)
    kv_x, gn2 = fence(plus(gkv2, k3), gn2)
    xkv = over_x(kv_x)
    zf = stage_z_reversed(f_u)
    out = self_bwd(
        block_in, x1, gx2, gn2, gains, n1, [*s_0, *s_1], (fq0, fk0, fv0, fe0, fr0, fa0), (fq1, fk1, fv1, fe1, fr1, fa1)
    )
    gs0, gs1, gs2, gs3, gd, gg2, gg1, grad_in = out
    gs0, gs3, gd, gg1, xqo, xkv, c1, *zf = fence(gs0, gs3, gd, gg1, xqo, xkv, c1, *zf)
    s3 = core(gs3)
    qo_t, kv_t = (gqo0, c1, xqo), (gkv0, k1, xkv)
    c_y = plus(*[jnp.where(y_is0, b_, a_) for a_, b_ in zip(qo_t, kv_t)])
    f_w = plus(*zf)
    s3, c_y, f_w = fence(s3, c_y, f_w)
    s_x = plus(gs2, s3)
    s_x, c_y, f_w, gs1, gd, gg1 = fence(s_x, c_y, f_w, gs1, gd, gg1)
    xs = over_x(s_x)
    yc = over_y(c_y)
    for bit in z_bits[:1:-1]:
        f_w = in_order(f_w, swap(f_w, "dp", bit), bit)
    f_got = swap(f_w, "dp", z_bits[1])
    s1 = core(gs1)
    flipped = jnp.asarray(np.ascontiguousarray(buckets[::-1]))
    grel = jnp.dot(gd, flipped, precision=lax.Precision.HIGHEST)
    grel = grel.reshape(tensor_size, heads * BUCKETS)
    slots = jnp.arange(tensor_size)[:, None] ^ t_index
    order = (slots == jnp.arange(tensor_size)[None, :]).astype(f32)
    grel = jnp.dot(order.T, grel, precision=lax.Precision.HIGHEST)
    grel = jnp.pad(grel.reshape(1, -1), ((0, 0), (0, d - grel.size)))
    small = jnp.concatenate([gg1, gg2, gg3, grel], axis=0)
    small_got = core(small)
    yc, small_got, s1, xs, f_got = fence(yc, small_got, s1, xs, f_got)
    ys = sent_y(gs0, s1, xs)
    zc = stage_z(plus(*[jnp.where(y_is0, a_, b_) for a_, b_ in zip(qo_t, kv_t)], yc))
    small = small + small_got
    small_got = over_x(small)
    f_w = in_order(f_w, f_got, z_bits[1])
    f_got = swap(f_w, "dp", 2)
    ys, small_got, *zc = fence(ys, small_got, *zc)
    zs = stage_z(plus(*kept_y(gs0, s1, xs), ys))
    small = small + small_got
    small_got = over_y(small)
    c_w = plus(*zc)
    small_got, c_w, f_got, *zs = fence(small_got, c_w, f_got, *zs)
    f_v = in_order(f_w, f_got, 2)
    f_f = over_y(f_v)
    bc = stage_z_back(c_w)
    bit = 2
    small = small + small_got
    small_got = swap(small, "dp", bit)
    bs = stage_z_back(plus(*zs))
    both = fence(small_got, *bs, *bc)
    small_got, bs, bc = both[0], both[1 : 1 + rest_size], both[1 + rest_size :]
    small = small + small_got
    while 2 * bit < dp_size:
        bit *= 2
        small = small + swap(small, "dp", bit)
    c_v = ordered_z(bc)
    c_f = over_y(c_v)
    s_v = ordered_z(bs)
    s_f = over_y(s_v)
    n_f = f_v.shape[0] // 2
    r_wo = ordered(f_v[:n_f], f_f[:n_f]).astype(f32)
    r_wi = ordered(f_v[n_f:], f_f[n_f:]).astype(f32)
    s_f, r_wo, r_wi = fence(s_f, r_wo, r_wi)
    r_s = ordered(s_v, s_f)
    g_s = [r_s[i * w : (i + 1) * w].astype(f32) for i in range(4)]
    c_f, *g_s = fence(c_f, *g_s)
    c_w = [jnp.where(y_is0, a_, b_) for a_, b_ in ((c_v, c_f), (c_f, c_v))]
    g_c = [v[i * w : (i + 1) * w].astype(f32) for v in c_w for i in range(2)]
    grad_rel = lax.dynamic_slice(small[3], (t_index * heads * BUCKETS,), (heads * BUCKETS,)).reshape(heads, BUCKETS).T

    return (
        block_out,
        grad_in,
        grad_enc,
        small[0],
        g_s[0].T,
        g_s[1].T,
        g_s[2].T,
        g_s[3],
        grad_rel,
        small[1],
        g_c[0].T,
        g_c[2].T,
        g_c[3].T,
        g_c[1],
        small[2],
        r_wi,
        r_wo,
    )


def solution(mesh):
    tensor_size = mesh.shape["tensor"]
    dp_size = mesh.shape["dp"]
    both = P(("dp", "tensor"), None)
    col = P(None, "tensor")
    row = P("tensor", None)
    placed = (both, both, P("dp"), P("dp"), P(), col, col, col, row, col, P(), col, col, col, row, P(), col, row, both)
    outs = (both, both, both, P(), col, col, col, row, col, P(), col, col, col, row, P(), col, row)
    return jax.shard_map(
        lambda *a: local_program(tensor_size, dp_size, *a),
        mesh=mesh,
        in_specs=placed,
        out_specs=outs,
        check_vma=False,
    )
```
